32 devices in a mesh: seq: 8 (over z, y), head: 4 (over x, core).
Axes of the slice: x: 2, y: 2, z: 4, core: 2. Of those that a mesh axis runs over, the one named last changes fastest.
Arguments:
- queries: bfloat16 [8192, 2048], P('seq', 'head'), may hold values from -100 to 100
- values: bfloat16 [8192, 2048], P('seq', 'head'), may hold values from -6 to 6
- codes: int32 [8192, 16], P('seq', 'head'), may hold values from 0 to 511
- codebook: bfloat16 [16, 512, 128], P('head'), may hold values from -4 to 4
- out_weight: bfloat16 [2048, 2048], P('head'), may hold values from -0.125 to 0.125
- grad_out: bfloat16 [8192, 2048], P('seq', 'head'), may hold values from -6 to 6
Outputs:
- grad_queries: bfloat16 [8192, 2048], P('seq', 'head')
- grad_values: bfloat16 [8192, 2048], P('seq', 'head')
- grad_codebook: float32 [16, 512, 128], P('head')
The draws below stay inside these ranges and needn't reach their ends.
All inputs are finite; a program needn't handle non-finite values.
Results may differ from the reference program's by a relative error of at most 0.012.
The reference program's roundings to bfloat16 on the way count: a program that leaves them out, or rounds other values in their place, can miss the bound.
Values may be sent and summed in bfloat16 or wider, within the bound.
A program may use at most 192 MiB of HBM per device.

```python
import math
import jax
import jax.numpy as jnp
import numpy as np
from jax import lax

D = 2048
HEADS = 16
E = 128
S = 512
BLOCK = 512
TOKENS = 8192


def codeword_table(key):
    codewords = jnp.clip(jax.random.normal(jax.random.fold_in(key, 11), (HEADS, S, E), jnp.float32), -4.0, 4.0)
    return codewords


def draw_codebook(key, part):
    return codeword_table(key).astype(jnp.bfloat16)


def draw_queries(key, part):
    queries = jnp.clip(jax.random.normal(jax.random.fold_in(key, 21), (TOKENS, HEADS * E), jnp.float32), -6.0, 6.0)
    return queries.astype(jnp.bfloat16)


def set_ends(values, key, low, high):
    shape = values.shape
    index_at = [jax.random.randint(jax.random.fold_in(key, axis), (), 0, shape[axis]) for axis in range(len(shape))]
    values = values.at[tuple(index_at)].set(low)
    longest = shape.index(max(shape))
    index_at[longest] = (index_at[longest] + 1) % shape[longest]
    return values.at[tuple(index_at)].set(high)


def shard_levels(rng, extent, cuts, least, high):
    level = 1.0
    for axis_at, parts in cuts:
        steps = jax.random.uniform(jax.random.fold_in(jax.random.fold_in(rng, 6), axis_at), (parts,), jnp.float32, least / len(cuts), high / len(cuts))
        level = level * jnp.repeat(jnp.exp(steps), extent[axis_at] // parts).reshape((-1,) + (1,) * (len(extent) - 1 - axis_at))
    return level


def cumulative_ranks(number_of, lean):
    weights = [(1 << 20) // math.isqrt(rank ** lean) + 1 for rank in range(1, number_of + 1)]
    scale = 1 + sum(weights) // (1 << 30)
    return np.cumsum(np.array([max(1, weight // scale) for weight in weights]))


def skewed_ids(key, shape, amount, skew):
    grid = cumulative_ranks(amount, skew)
    ticket = jax.random.randint(jax.random.fold_in(key, 1), shape, 0, int(grid[amount - 1]))
    rank = jnp.searchsorted(jnp.asarray(grid, jnp.int32), ticket, side="right")
    return jax.random.permutation(jax.random.fold_in(key, 2), amount)[rank].astype(jnp.int32)


def scatter_about(key, extent, deviation, most, cuts=(), held_as=jnp.bfloat16):
    result = jax.random.normal(key, extent, jnp.float32) * deviation
    if len(cuts) > 0:
        result = shard_levels(key, extent, cuts, -0.22, 0.18) * result
    return jnp.clip(result, min=-most, max=most).astype(held_as)


def setup_inputs(seed: int = 0) -> dict:
    splits = jax.random.split(jax.random.key(seed), 7)
    queries = draw_queries(jax.random.fold_in(splits[6], 71), 0)
    values = scatter_about(splits[1], (TOKENS, HEADS * E), 1.0, 6.0, ((0, 8), (1, 4)))
    codes = set_ends(skewed_ids(splits[2], (TOKENS, HEADS), S, 2), jax.random.fold_in(splits[2], 3), 0, S - 1).astype(jnp.int32)
    codebook = draw_codebook(jax.random.fold_in(splits[6], 71), 0)
    out_weight = scatter_about(splits[4], (HEADS * E, D), D ** -0.5, 0.125, ((0, 4),))
    grad_out = scatter_about(splits[5], (TOKENS, D), 1.0, 6.0, ((0, 8), (1, 4)))
    return dict(queries=queries, values=values, codes=codes, codebook=codebook, out_weight=out_weight, grad_out=grad_out)


def lowered(array):
    return lax.optimization_barrier(array.astype(jnp.bfloat16)).astype(jnp.float32)


def product(form, left, right):
    return jnp.einsum(form, left.astype(jnp.float32), right.astype(jnp.float32))


def block_terms(query, value, block_codes, dout, codebook, prefix_values, prefix_counts):
    block_rows, heads_all, head_width = query.shape
    entries = codebook.shape[1]
    scale = head_width ** -0.5
    onehot = (block_codes[:, :, None] == jnp.arange(entries, dtype=jnp.int32)[None, None, :]).astype(jnp.float32)
    keys = lowered(product("ths,hse->the", onehot, codebook))
    scores = product("the,uhe->htu", query, keys) * scale
    positions = jnp.arange(block_rows, dtype=jnp.int32)
    causal = positions[:, None] >= positions[None, :]
    cache_scores = product("the,hce->htc", query, codebook) * scale
    counts_row = prefix_counts[:, None, :]
    present = counts_row > 0.0
    highest = jnp.maximum(jnp.max(jnp.where(causal, scores, -jnp.inf), axis=-1, keepdims=True),
                          jnp.max(jnp.where(present, cache_scores, -jnp.inf), axis=-1, keepdims=True))
    local_exp = jnp.where(causal, jnp.exp(jnp.where(causal, scores - highest, 0.0)), 0.0)
    cache_exp = jnp.where(present, jnp.exp(jnp.where(present, cache_scores - highest, 0.0)), 0.0)
    total = jnp.sum(local_exp, axis=-1, keepdims=True) + jnp.sum(cache_exp * counts_row, axis=-1, keepdims=True)
    local_prob = local_exp / total
    cache_prob = cache_exp / total
    local_low = lowered(local_prob)
    cache_low = lowered(cache_prob)
    cache_values = lowered(prefix_values)
    attended = product("htu,uhe->hte", local_low, value) + product("htc,hce->hte", cache_low, cache_values)
    delta = jnp.sum(jnp.transpose(dout.astype(jnp.float32), (1, 0, 2)) * attended, axis=-1)[..., None]
    local_grad = product("the,uhe->htu", dout, value)
    local_score_grad = lowered(local_prob * (local_grad - delta) * scale)
    cache_grad = product("the,hce->htc", dout, cache_values)
    cache_score_grad = lowered(cache_prob * (cache_grad - delta * counts_row) * scale)
    grad_query = (product("htu,uhe->the", local_score_grad, keys)
                  + product("htc,hce->the", cache_score_grad, codebook)).astype(jnp.bfloat16)
    key_grad = lowered(product("htu,the->uhe", local_score_grad, query))
    grad_code = product("ths,the->hse", onehot, key_grad) + product("htc,the->hce", cache_score_grad, query)
    value_part = product("htc,the->hce", cache_low, dout)
    local_values = product("htu,the->uhe", local_low, dout)
    own_values = product("ths,the->hse", onehot, value)
    own_counts = jnp.sum(onehot, axis=0)
    return grad_query, local_values, grad_code, value_part, own_values, own_counts


def reference(queries, values, codes, codebook, out_weight, grad_out):
    heads_all, entries, head_width = codebook.shape
    grad_heads = jnp.dot(grad_out, out_weight.T, preferred_element_type=jnp.float32).astype(jnp.bfloat16)
    nblocks = queries.shape[0] // BLOCK

    def stacked(array):
        return array.reshape(nblocks, BLOCK, heads_all, head_width)

    items = (stacked(queries), stacked(values), codes.reshape(nblocks, BLOCK, heads_all), stacked(grad_heads))

    def forward(carry, item):
        prefix_values, prefix_counts, code_sum = carry
        query, value, block_codes, dout = item
        grad_query, local_values, grad_code, value_part, own_values, own_counts = block_terms(
            query, value, block_codes, dout, codebook, prefix_values, prefix_counts)
        return (prefix_values + own_values, prefix_counts + own_counts, code_sum + grad_code), (grad_query, local_values, value_part)

    start_values = jnp.zeros((heads_all, entries, head_width), jnp.float32)
    start_counts = jnp.zeros((heads_all, entries), jnp.float32)
    (ignored_values, ignored_counts, grad_codebook), (grad_query, local_values, value_parts) = lax.scan(
        forward, (start_values, start_counts, start_values), items)

    def backward(later, item):
        block_codes, local_part, value_part = item
        onehot = (block_codes[:, :, None] == jnp.arange(entries, dtype=jnp.int32)[None, None, :]).astype(jnp.float32)
        lookup = jnp.einsum("ths,hse->the", onehot, lowered(later))
        return later + value_part, (local_part + lookup).astype(jnp.bfloat16)

    ignored_later, grad_value = lax.scan(backward, start_values,
                                         (codes.reshape(nblocks, BLOCK, heads_all), local_values, value_parts), reverse=True)
    return (grad_query.reshape(-1, heads_all * head_width), grad_value.reshape(-1, heads_all * head_width), grad_codebook)
```

```python
import functools

import jax
import jax.numpy as jnp
from jax import lax
from jax.experimental import pallas as pl
from jax.experimental.pallas import tpu as pltpu
from jax.sharding import PartitionSpec as P

BLOCK = 512
TILE = 256
CHUNK = 128
NEG = -1e30
LOG2E = 1.4426950408889634
F32 = jnp.float32
BF16 = jnp.bfloat16
MESH = pl.DeviceIdType.MESH


def nn(a, b):
    return lax.dot_general(a, b, (((1,), (0,)), ((), ())), preferred_element_type=F32)


def nt(a, b):
    return lax.dot_general(a, b, (((1,), (1,)), ((), ())), preferred_element_type=F32)


def kernel(
    n_seq, n_head,
    q_in, v_in, codes_in, cb_in, w_in, go_in,
    gq_ref, gv_ref, gc_ref,
    q_ref, v_ref, codes_ref, cb_ref, w_ref, gath, dout,
    hot_t, hot, keys, keys_t, book_t, own, cnt_block, cnt_pre, cnt_full, cval,
    lprob, cprob, key_acc, local_part, vpart, code_acc, later_ref,
    cn_own, cny_in, cnz_out, cnz_in,
    py_out, py_in, pz_out, pz_in, pa_out, pa_in,
    ly_out, ly_in, lz_out, lz_in, la_out, la_in,
    cy_out, cy_in, cz_out, cz_in, c_fin,
    load_s, go_s, ag_s, ag_r, cny_s, cny_r, cnz_s, cnz_r,
    py_s, py_r, pz_s, pz_r, pa_s, pa_r,
    ly_s, ly_r, lz_s, lz_r, la_s, la_r,
    cy_s, cy_r, ca_s, ca_r, cz_s, cz_r, cf_s, cf_r,
):
    rows_all = q_ref.shape[0]
    heads, entries, width = cb_ref.shape
    nb = rows_all // BLOCK
    parts = BLOCK // TILE
    chunks = rows_all // CHUNK
    per_tile = TILE // CHUNK
    outer = n_seq // 2
    half = entries // 2
    piece = half // outer
    scale = width ** (-0.5)
    me = lax.axis_index("seq")
    mine = lax.axis_index("head")
    at = me // 2
    side = me % 2
    partner = me + 1 - 2 * side
    is_hi = side.astype(F32)
    is_lo = 1.0 - is_hi
    own_half = pl.ds(pl.multiple_of(side * half, half), half)
    other_half = pl.ds(pl.multiple_of((1 - side) * half, half), half)
    has_down = at > 0
    has_up = at < outer - 1
    bits = []
    bit = n_head // 2
    while bit >= 1:
        bits.append(bit)
        bit //= 2

    def flip(index, mask):
        for b in bits:
            if mask & b:
                index = index + b - 2 * b * ((index // b) % 2)
        return index

    def go_load(chunk):
        span = pl.ds(chunk * CHUNK, CHUNK)
        return pltpu.make_async_copy(go_in.at[span], gath.at[mine, span], go_s.at[chunk])

    loads = [
        pltpu.make_async_copy(src, dst, load_s.at[k])
        for k, (src, dst) in enumerate(
            ((codes_in, codes_ref), (cb_in, cb_ref), (v_in, v_ref), (q_in, q_ref), (w_in, w_ref)))
    ]
    loads[0].start()
    for chunk in range(chunks):
        go_load(chunk).start()
    for copy in loads[1:]:
        copy.start()

    barrier = pltpu.get_barrier_semaphore()
    pl.semaphore_signal(barrier, inc=1, device_id={"seq": partner}, device_id_type=MESH)
    for b in bits:
        pl.semaphore_signal(barrier, inc=1, device_id={"head": flip(mine, b)}, device_id_type=MESH)

    def greet(k, carry):
        pl.semaphore_signal(barrier, inc=1, device_id={"seq": (me + 2 * k) % n_seq}, device_id_type=MESH)
        return carry

    lax.fori_loop(1, outer, greet, 0)
    pl.semaphore_wait(barrier, outer + len(bits))

    def gather_copy(src_mask, to, chunk):
        block = flip(mine, src_mask)
        span = pl.ds(chunk * CHUNK, CHUNK)
        slot = src_mask ^ to
        return pltpu.make_async_remote_copy(
            src_ref=gath.at[block, span], dst_ref=gath.at[block, span],
            send_sem=ag_s.at[slot, chunk], recv_sem=ag_r.at[slot, chunk],
            device_id={"head": flip(mine, to)}, device_id_type=MESH)

    plan = []
    known = [0]
    for b in bits:
        plan += [(m, b) for m in known]
        known += [m ^ b for m in known]
    by_slot = {m ^ b: (m, b) for m, b in plan}
    for chunk in range(chunks):
        go_load(chunk).wait()
        for m, b in plan:
            if m == 0 and b == bits[0]:
                gather_copy(m, b, chunk).start()
    for m, b in plan:
        if m == 0 and b != bits[0]:
            for chunk in range(chunks):
                gather_copy(m, b, chunk).start()
    taken = set()

    def arrive(slot, chunk):
        if (slot, chunk) not in taken:
            taken.add((slot, chunk))
            m, b = by_slot[slot]
            gather_copy(m, b, chunk).wait_recv()

    def relay(chunk):
        for m, b in plan:
            if m != 0:
                arrive(m, chunk)
                gather_copy(m, b, chunk).start()

    def seq_copy(src, dst, send, recv, to):
        return pltpu.make_async_remote_copy(
            src_ref=src, dst_ref=dst, send_sem=send, recv_sem=recv,
            device_id={"seq": to}, device_id_type=MESH)

    count_pair = seq_copy(cn_own, cny_in, cny_s.at[0], cny_r.at[0], partner)

    def count_chain(to):
        return seq_copy(cnz_out, cnz_in, cnz_s.at[0], cnz_r.at[0], to)

    loads[0].wait()
    row_at = lax.broadcasted_iota(jnp.int32, (entries, BLOCK), 0)
    lane_at = lax.broadcasted_iota(jnp.int32, (BLOCK, entries), 1)

    def count(h, carry):
        total = jnp.zeros((1, entries), F32)
        for b in range(nb):
            code_row = codes_ref[pl.ds(h, 1), pl.ds(b * BLOCK, BLOCK)]
            code_full = jnp.transpose(jnp.broadcast_to(code_row, (width, BLOCK)))
            code_cols = jnp.concatenate([code_full] * (entries // width), axis=1)
            one_f = (lane_at == code_cols).astype(F32)
            hot[h, b] = one_f.astype(BF16)
            counts = jnp.sum(one_f, axis=0, keepdims=True)
            cnt_block[h, b] = counts
            total += counts
        cn_own[h] = total
        return carry

    lax.fori_loop(0, heads, count, 0)
    count_pair.start()

    def share_counts():
        count_pair.wait_recv()

        @pl.when(jnp.logical_not(has_down))
        def _():
            cnz_in[...] = jnp.zeros(cnz_in.shape, F32)

        @pl.when(has_down)
        def _():
            count_chain(me - 2).wait_recv()

        cnz_out[...] = cnz_in[...] + cn_own[...] + cny_in[...]

        @pl.when(has_up)
        def _():
            count_chain(me + 2).start()

        def per_head(h, carry):
            row = cnz_in[h] + cny_in[h] * is_hi
            for b in range(nb):
                cnt_pre[h, b] = row
                row = row + cnt_block[h, b]
            return carry

        lax.fori_loop(0, heads, per_head, 0)

    def prefix_pair(h):
        return seq_copy(py_out.at[h], py_in.at[h], py_s.at[h], py_r.at[h], partner)

    def prefix_hop(h, to):
        return seq_copy(pz_out.at[h], pz_in.at[h], pz_s.at[h], pz_r.at[h], to)

    def prefix_back(h):
        return seq_copy(pa_out.at[h], pa_in.at[h], pa_s.at[h], pa_r.at[h], partner)

    loads[1].wait()
    loads[2].wait()

    def sums(h, carry):
        head_lanes = pl.ds(pl.multiple_of(h * width, width), width)
        book = cb_ref[h]
        book_t[h] = jnp.transpose(book.astype(F32)).astype(BF16)
        for b in range(nb):
            rows = pl.ds(b * BLOCK, BLOCK)
            code_row = codes_ref[pl.ds(h, 1), rows]
            one_t = (row_at == code_row).astype(F32).astype(BF16)
            hot_t[h, b] = one_t
            key = nn(hot[h, b], book)
            keys[h, b] = key.astype(BF16)
            keys_t[h, b] = jnp.transpose(key).astype(BF16)
            own[h, b] = nn(one_t, v_ref[rows, head_lanes])
        total = own[h, 0, other_half]
        for b in range(1, nb):
            total += own[h, b, other_half]
        py_out[h] = total.astype(BF16)
        prefix_pair(h).start()

        @pl.when(h == jnp.minimum(at, heads - 1))
        def _():
            share_counts()

        return carry

    lax.fori_loop(0, heads, sums, 0)

    def prefix_chain(h):
        prefix_pair(h).wait_recv()

        @pl.when(jnp.logical_not(has_down))
        def _():
            pz_in[h] = jnp.zeros(pz_in.shape[1:], BF16)

        @pl.when(has_down)
        def _():
            prefix_hop(h, me - 2).wait_recv()

        below = pz_in[h].astype(F32)
        pair = py_in[h].astype(F32)
        total = own[h, 0, own_half]
        for b in range(1, nb):
            total += own[h, b, own_half]
        pz_out[h] = (below + total + pair).astype(BF16)

        @pl.when(has_up)
        def _():
            prefix_hop(h, me + 2).start()

        pa_out[h] = (below + total * is_lo).astype(BF16)
        prefix_back(h).start()
        prefix = below + pair * is_hi
        for b in range(nb):
            cval[h, b, own_half] = prefix.astype(BF16)
            prefix = prefix + own[h, b, own_half]

    def prefix_gather(h):
        prefix_back(h).wait_recv()
        prefix = pa_in[h].astype(F32)
        for b in range(nb):
            cval[h, b, other_half] = prefix.astype(BF16)
            prefix = prefix + own[h, b, other_half]

    def softmax(h, b):
        head_lanes = pl.ds(pl.multiple_of(h * width, width), width)
        book = cb_ref[h]
        count_full = jnp.transpose(jnp.broadcast_to(cnt_pre[h, b], (width, entries)))
        cnt_full[h, b] = count_full
        bias_full = jnp.where(count_full > 0.0, 0.0, NEG)
        counts = jnp.concatenate([count_full] * (TILE // width), axis=1)
        bias = jnp.concatenate([bias_full] * (TILE // width), axis=1)
        for p in range(parts):
            seen = (p + 1) * TILE
            query = q_ref[pl.ds(pl.multiple_of(b * BLOCK + p * TILE, TILE), TILE), head_lanes]
            at_u = lax.broadcasted_iota(jnp.int32, (seen, TILE), 0)
            at_t = lax.broadcasted_iota(jnp.int32, (seen, TILE), 1) + p * TILE
            scores = jnp.where(at_u <= at_t, nt(keys[h, b, 0:seen], query) * (scale * LOG2E), NEG)
            cache_scores = nt(book, query) * (scale * LOG2E) + bias
            highest = jnp.maximum(
                jnp.max(scores, axis=0, keepdims=True), jnp.max(cache_scores, axis=0, keepdims=True))
            local_exp = jnp.exp2(scores - highest)
            cache_exp = jnp.exp2(cache_scores - highest)
            total = jnp.sum(local_exp, axis=0, keepdims=True) + jnp.sum(cache_exp * counts, axis=0, keepdims=True)
            inverse = 1.0 / total
            lprob[h, b, seen * p // 2:seen * p // 2 + seen] = local_exp * inverse
            cprob[h, b, p] = cache_exp * inverse

    loads[3].wait()
    units = heads * nb
    early = list(range(chunks // 2))
    relay(early[0])
    relay_at = {}
    for j in early[1:]:
        relay_at.setdefault(max(0, units * j // len(early) - 1), []).append(j)

    def unit(u, carry):
        h, b = u // nb, u % nb
        softmax(h, b)

        @pl.when(u < heads)
        def _():
            prefix_chain(u)

        if units >= 2 * heads:
            @pl.when((u >= heads) & (u < 2 * heads))
            def _():
                prefix_gather(u - heads)

        for step, which in relay_at.items():
            @pl.when(u == step)
            def _(which=which):
                for chunk in which:
                    relay(chunk)

        return carry

    lax.fori_loop(0, units, unit, 0)
    if units < 2 * heads:
        for h in range(heads):
            prefix_gather(h)
    loads[4].wait()

    depth = go_in.shape[1]

    def project(start):
        rows = pl.ds(start, TILE)
        total = nt(gath[0, rows], w_ref[:, 0:depth])
        for k in range(1, n_head):
            total += nt(gath[k, rows], w_ref[:, k * depth:(k + 1) * depth])
        dout[rows] = total.astype(BF16)

    def value_pass(h, b, p):
        head_lanes = pl.ds(pl.multiple_of(h * width, width), width)
        grad = dout[pl.ds(b * BLOCK + p * TILE, TILE), head_lanes]
        value = nn(cprob[h, b, p].astype(BF16), grad)
        if p == 0:
            vpart[h, b] = value
        else:
            vpart[h, b] += value

    def grad_pass(h, b, p):
        head_lanes = pl.ds(pl.multiple_of(h * width, width), width)
        rows = pl.ds(b * BLOCK + p * TILE, TILE)
        seen = (p + 1) * TILE
        query = q_ref[rows, head_lanes]
        grad = dout[rows, head_lanes]
        counts = jnp.concatenate([cnt_full[h, b]] * (TILE // width), axis=1)
        local_grad = nt(v_ref[pl.ds(b * BLOCK, seen), head_lanes], grad)
        cache_grad = nt(cval[h, b], grad)
        local_prob = lprob[h, b, seen * p // 2:seen * p // 2 + seen]
        cache_prob = cprob[h, b, p]
        local_low = local_prob.astype(BF16)
        cache_low = cache_prob.astype(BF16)
        delta = (jnp.sum(local_low.astype(F32) * local_grad, axis=0, keepdims=True)
                 + jnp.sum(cache_low.astype(F32) * cache_grad, axis=0, keepdims=True))
        local_score_grad = (local_prob * (local_grad - delta) * scale).astype(BF16)
        cache_score_grad = (cache_prob * (cache_grad - delta * counts) * scale).astype(BF16)
        gq_t = nn(keys_t[h, b, :, 0:seen], local_score_grad) + nn(book_t[h], cache_score_grad)
        gq_ref[rows, head_lanes] = jnp.transpose(gq_t).astype(BF16)
        code = nn(cache_score_grad, query)
        key_grad = nn(local_score_grad, query)
        local = nn(local_low, grad)
        last = p * TILE
        if p > 0:
            key_acc[h, 0:last] += key_grad[0:last]
            local_part[h, b, 0:last] += local[0:last]
        key_acc[h, last:seen] = key_grad[last:seen]
        local_part[h, b, last:seen] = local[last:seen]
        if p == parts - 1:
            code += nn(hot_t[h, b], key_acc[h].astype(BF16))
        if b == 0 and p == 0:
            code_acc[h] = code
        else:
            code_acc[h] += code

    def later_pair(h):
        return seq_copy(ly_out.at[h], ly_in.at[h], ly_s.at[h], ly_r.at[h], partner)

    def later_hop(h, to):
        return seq_copy(lz_out.at[h], lz_in.at[h], lz_s.at[h], lz_r.at[h], to)

    def later_back(h):
        return seq_copy(la_out.at[h], la_in.at[h], la_s.at[h], la_r.at[h], partner)

    def part_total(h, span):
        total = vpart[h, 0, span]
        for b in range(1, nb):
            total += vpart[h, b, span]
        return total

    def send_later(h):
        ly_out[h] = part_total(h, other_half).astype(BF16)
        later_pair(h).start()

    def later_chain(h):
        later_pair(h).wait_recv()

        @pl.when(jnp.logical_not(has_up))
        def _():
            lz_in[h] = jnp.zeros(lz_in.shape[1:], BF16)

        @pl.when(has_up)
        def _():
            later_hop(h, me + 2).wait_recv()

        above = lz_in[h].astype(F32)
        pair = ly_in[h].astype(F32)
        total = part_total(h, own_half)
        lz_out[h] = (above + total + pair).astype(BF16)

        @pl.when(has_down)
        def _():
            later_hop(h, me - 2).start()

        la_out[h] = (above + total * is_hi).astype(BF16)
        later_back(h).start()
        later_ref[h, own_half] = above + pair * is_lo

    def later_gather(h):
        later_back(h).wait_recv()
        later_ref[h, other_half] = la_in[h].astype(F32)
        head_lanes = pl.ds(pl.multiple_of(h * width, width), width)
        later = later_ref[h]
        for b in reversed(range(nb)):
            rows = pl.ds(b * BLOCK, BLOCK)
            lookup = nn(hot[h, b], later.astype(BF16))
            gv_ref[rows, head_lanes] = (local_part[h, b] + lookup).astype(BF16)
            later = later + vpart[h, b]

    def code_pair(h):
        return seq_copy(cy_out.at[h], cy_in.at[h], cy_s.at[h], cy_r.at[h], partner)

    def code_out(h, to, source):
        return seq_copy(
            cz_out.at[h, to], cz_in.at[h, source], cz_s.at[h, to], cz_r.at[h, source], 2 * to + side)

    def code_back(h, to, source):
        return seq_copy(
            c_fin.at[h, side, source], c_fin.at[h, side, source], cf_s.at[h, to], cf_r.at[h, source], 2 * to + side)

    def code_half(h, which):
        return seq_copy(c_fin.at[h, which], c_fin.at[h, which], ca_s.at[h], ca_r.at[h], partner)

    def over_chain(action):
        def body(k, carry):
            action((at + k) % outer)
            return carry

        lax.fori_loop(1, outer, body, 0)

    def send_code(h):
        cy_out[h] = code_acc[h, other_half].astype(BF16)
        code_pair(h).start()

    def reduce_code(h):
        code_pair(h).wait_recv()
        total = code_acc[h, own_half] + cy_in[h].astype(F32)
        cz_out[h] = total.astype(BF16).reshape(outer, piece, width)
        over_chain(lambda to: code_out(h, to, at).start())
        cz_in[h, at] = cz_out[h, at]

    def spread_code(h):
        over_chain(lambda source: code_out(h, source, source).wait_recv())
        total = cz_in[h, 0].astype(F32)
        for k in range(1, outer):
            total += cz_in[h, k].astype(F32)
        c_fin[h, side, at] = total.astype(BF16)
        over_chain(lambda to: code_back(h, to, at).start())

    def pair_code(h):
        over_chain(lambda source: code_back(h, source, source).wait_recv())
        code_half(h, side).start()
        gc_ref[h, own_half] = c_fin[h, side].astype(F32).reshape(half, width)

    def last_code(h):
        code_half(h, 1 - side).wait_recv()
        gc_ref[h, other_half] = c_fin[h, 1 - side].astype(F32).reshape(half, width)

    tiles = nb * parts
    slots = max(1, (tiles - 1) * heads)
    late = list(range(chunks // 2, chunks))
    late_at = {}
    for j, chunk in enumerate(late):
        late_at.setdefault(min(slots - 1, slots * j // len(late) + 1), []).append(chunk)

    for g in range(tiles):
        b, p = g // parts, g % parts
        final = g == tiles - 1
        if final:
            for chunk in late:
                for m, _ in plan:
                    if m != 0 and (m, chunk) not in taken:
                        relay(chunk)
        for chunk in range(g * per_tile, (g + 1) * per_tile):
            for slot in by_slot:
                arrive(slot, chunk)
        project(g * TILE)

        def values(h, carry, b=b, p=p, final=final):
            value_pass(h, b, p)
            if final:
                send_later(h)
            return carry

        lax.fori_loop(0, heads, values, 0)

        def grads(h, carry, g=g, b=b, p=p, final=final):
            grad_pass(h, b, p)
            for slot, which in late_at.items():
                if slot // heads == g:
                    @pl.when(h == slot % heads)
                    def _(which=which):
                        for chunk in which:
                            relay(chunk)
            if final:
                send_code(h)

                @pl.when(jnp.logical_not(has_up) & (h >= 1))
                def _():
                    later_chain(h - 1)

            return carry

        lax.fori_loop(0, heads, grads, 0)

    behind = outer - 1 - at
    soon = behind * 2 < outer
    last_ones = behind * 4 >= 3 * outer

    def reduce_step(h, carry):
        @pl.when(soon & (has_up | (h == heads - 1)))
        def _():
            later_chain(h)

        reduce_code(h)

        @pl.when(jnp.logical_not(soon | last_ones))
        def _():
            later_chain(h)

        return carry

    lax.fori_loop(0, heads, reduce_step, 0)

    def spread_step(h, carry):
        spread_code(h)

        @pl.when(last_ones)
        def _():
            later_chain(h)

        return carry

    lax.fori_loop(0, heads, spread_step, 0)

    def pair_step(h, carry):
        pair_code(h)
        later_gather(h)
        return carry

    lax.fori_loop(0, heads, pair_step, 0)

    def last_step(h, carry):
        last_code(h)
        return carry

    lax.fori_loop(0, heads, last_step, 0)

    def drain(h, carry):
        prefix_pair(h).wait_send()
        prefix_back(h).wait_send()
        later_pair(h).wait_send()
        later_back(h).wait_send()

        @pl.when(has_up)
        def _():
            prefix_hop(h, me + 2).wait_send()

        @pl.when(has_down)
        def _():
            later_hop(h, me - 2).wait_send()

        code_pair(h).wait_send()
        code_half(h, side).wait_send()
        over_chain(lambda to: code_out(h, to, at).wait_send())
        over_chain(lambda to: code_back(h, to, at).wait_send())
        return carry

    lax.fori_loop(0, heads, drain, 0)
    count_pair.wait_send()

    @pl.when(has_up)
    def _():
        count_chain(me + 2).wait_send()

    for m, b in plan:
        for chunk in range(chunks):
            gather_copy(m, b, chunk).wait_send()


def per_device(queries, values, codes, codebook, out_weight, grad_out):
    n_seq, n_head = lax.axis_size("seq"), lax.axis_size("head")
    row_count = queries.shape[0]
    heads, entries, width = codebook.shape
    nb = row_count // BLOCK
    parts = BLOCK // TILE
    chunks = row_count // CHUNK
    half = entries // 2
    hbm = pl.BlockSpec(memory_space=pltpu.HBM)
    vmem = pl.BlockSpec(memory_space=pltpu.VMEM)
    dma = pltpu.SemaphoreType.DMA
    halves = pltpu.VMEM((heads, half, width), BF16)
    pieces = pltpu.VMEM((heads, n_seq // 2, entries // n_seq, width), BF16)
    counts = pltpu.VMEM((heads, 1, entries), F32)
    return pl.pallas_call(
        functools.partial(kernel, n_seq, n_head),
        out_shape=(
            jax.ShapeDtypeStruct(queries.shape, BF16),
            jax.ShapeDtypeStruct(queries.shape, BF16),
            jax.ShapeDtypeStruct(codebook.shape, F32),
        ),
        in_specs=[hbm] * 6,
        out_specs=(vmem,) * 3,
        scratch_shapes=[
            pltpu.VMEM(queries.shape, BF16),
            pltpu.VMEM(queries.shape, BF16),
            pltpu.VMEM((heads, row_count), jnp.int32),
            pltpu.VMEM(codebook.shape, BF16),
            pltpu.VMEM(out_weight.shape, BF16),
            pltpu.VMEM((n_head,) + grad_out.shape, BF16),
            pltpu.VMEM(queries.shape, BF16),
            pltpu.VMEM((heads, nb, entries, BLOCK), BF16),
            pltpu.VMEM((heads, nb, BLOCK, entries), BF16),
            pltpu.VMEM((heads, nb, BLOCK, width), BF16),
            pltpu.VMEM((heads, nb, width, BLOCK), BF16),
            pltpu.VMEM((heads, width, entries), BF16),
            pltpu.VMEM((heads, nb, entries, width), F32),
            pltpu.VMEM((heads, nb, 1, entries), F32),
            pltpu.VMEM((heads, nb, 1, entries), F32),
            pltpu.VMEM((heads, nb, entries, width), F32),
            pltpu.VMEM((heads, nb, entries, width), BF16),
            pltpu.VMEM((heads, nb, (parts + 1) * BLOCK // 2, TILE), F32),
            pltpu.VMEM((heads, nb, parts, entries, TILE), F32),
            pltpu.VMEM((heads, BLOCK, width), F32),
            pltpu.VMEM((heads, nb, BLOCK, width), F32),
            pltpu.VMEM((heads, nb, entries, width), F32),
            pltpu.VMEM((heads, entries, width), F32),
            pltpu.VMEM((heads, entries, width), F32),
            counts, counts, counts, counts,
            halves, halves, halves, halves, halves, halves,
            halves, halves, halves, halves, halves, halves,
            halves, halves, pieces, pieces,
            pltpu.VMEM((heads, 2, n_seq // 2, entries // n_seq, width), BF16),
            dma((5,)), dma((chunks,)),
            dma((n_head, chunks)), dma((n_head, chunks)),
            dma((1,)), dma((1,)), dma((1,)), dma((1,)),
        ] + [dma((heads,))] * 16 + [dma((heads, n_seq // 2))] * 4,
        compiler_params=pltpu.CompilerParams(
            collective_id=0, has_side_effects=True, vmem_limit_bytes=57 * 1024 * 1024),
    )(queries, values, codes.T, codebook, out_weight, grad_out)


def solution(mesh):
    return jax.shard_map(
        per_device,
        mesh=mesh,
        in_specs=(
            P("seq", "head"),
            P("seq", "head"),
            P("seq", "head"),
            P("head", None, None),
            P("head", None),
            P("seq", "head"),
        ),
        out_specs=(P("seq", "head"), P("seq", "head"), P("head", None, None)),
        check_vma=False,
    )
```

```python
import functools

import jax
import jax.numpy as jnp
from jax import lax
from jax.experimental import pallas as pl
from jax.experimental.pallas import tpu as pltpu
from jax.sharding import PartitionSpec as P

BLOCK = 512
TILE = 256
CHUNK = 128
NEG = -1e30
LOG2E = 1.4426950408889634
F32 = jnp.float32
BF16 = jnp.bfloat16
MESH = pl.DeviceIdType.MESH


def nn(a, b):
    return lax.dot_general(a, b, (((1,), (0,)), ((), ())), preferred_element_type=F32)


def nt(a, b):
    return lax.dot_general(a, b, (((1,), (1,)), ((), ())), preferred_element_type=F32)


def kernel(
    n_seq, n_head,
    q_in, v_in, codes_in, cb_in, w_in, go_in,
    gq_ref, gv_ref, gc_ref,
    q_ref, v_ref, codes_ref, cb_ref, w_ref, gath, dout,
    hot_t, hot, keys, keys_t, book_t, own, cnt_block, cnt_pre, cnt_full, cval,
    local_low, cache_low, local_part, vpart, code_acc, later_ref,
    cn_own, cn_in,
    py_out, py_in, pz_out, pz_in, pa_out, pa_in,
    ly_out, ly_in, lz_out, lz_in, la_out, la_in,
    cy_out, cy_in, cz_out, cz_in, c_fin,
    load_s, go_s, ag_s, ag_r, cn_s, cn_r,
    py_s, py_r, pz_s, pz_r, pa_s, pa_r,
    ly_s, ly_r, lz_s, lz_r, la_s, la_r,
    cy_s, cy_r, ca_s, ca_r, cz_s, cz_r, cf_s, cf_r,
):
    rows_all = q_ref.shape[0]
    heads, entries, width = cb_ref.shape
    nb = rows_all // BLOCK
    parts = BLOCK // TILE
    chunks = rows_all // CHUNK
    per_tile = TILE // CHUNK
    outer = n_seq // 2
    half = entries // 2
    piece = half // outer
    scale = width ** (-0.5)
    me = lax.axis_index("seq")
    mine = lax.axis_index("head")
    at = me // 2
    side = me % 2
    partner = me + 1 - 2 * side
    is_hi = side.astype(F32)
    is_lo = 1.0 - is_hi
    own_half = pl.ds(pl.multiple_of(side * half, half), half)
    other_half = pl.ds(pl.multiple_of((1 - side) * half, half), half)
    has_down = at > 0
    has_up = at < outer - 1
    bits = []
    bit = n_head // 2
    while bit >= 1:
        bits.append(bit)
        bit //= 2

    def flip(index, mask):
        for b in bits:
            if mask & b:
                index = index + b - 2 * b * ((index // b) % 2)
        return index

    def go_load(chunk):
        span = pl.ds(chunk * CHUNK, CHUNK)
        return pltpu.make_async_copy(go_in.at[span], gath.at[mine, span], go_s.at[chunk])

    loads = [
        pltpu.make_async_copy(src, dst, load_s.at[k])
        for k, (src, dst) in enumerate(
            ((codes_in, codes_ref), (cb_in, cb_ref), (v_in, v_ref), (q_in, q_ref), (w_in, w_ref)))
    ]
    loads[0].start()
    for chunk in range(chunks):
        go_load(chunk).start()
    for copy in loads[1:]:
        copy.start()

    barrier = pltpu.get_barrier_semaphore()
    def greet(k, carry):
        pl.semaphore_signal(barrier, inc=1, device_id={"seq": (me + k) % n_seq}, device_id_type=MESH)
        return carry

    lax.fori_loop(1, n_seq, greet, 0)
    for b in bits:
        pl.semaphore_signal(barrier, inc=1, device_id={"head": flip(mine, b)}, device_id_type=MESH)

    loads[0].wait()
    row_at = lax.broadcasted_iota(jnp.int32, (entries, BLOCK), 0)
    lane_at = lax.broadcasted_iota(jnp.int32, (BLOCK, entries), 1)

    def count(h, carry):
        total = jnp.zeros((1, entries), F32)
        for b in range(nb):
            code_row = codes_ref[pl.ds(h, 1), pl.ds(b * BLOCK, BLOCK)]
            code_full = jnp.transpose(jnp.broadcast_to(code_row, (width, BLOCK)))
            code_cols = jnp.concatenate([code_full] * (entries // width), axis=1)
            one_f = (lane_at == code_cols).astype(F32)
            hot[h, b] = one_f.astype(BF16)
            counts = jnp.sum(one_f, axis=0, keepdims=True)
            cnt_block[h, b] = counts
            total += counts
        cn_own[h] = total
        return carry

    lax.fori_loop(0, heads, count, 0)
    pl.semaphore_wait(barrier, n_seq - 1 + len(bits))

    def gather_copy(src_mask, to, chunk):
        block = flip(mine, src_mask)
        span = pl.ds(chunk * CHUNK, CHUNK)
        slot = src_mask ^ to
        return pltpu.make_async_remote_copy(
            src_ref=gath.at[block, span], dst_ref=gath.at[block, span],
            send_sem=ag_s.at[slot, chunk], recv_sem=ag_r.at[slot, chunk],
            device_id={"head": flip(mine, to)}, device_id_type=MESH)

    plan = []
    known = [0]
    for b in bits:
        plan += [(m, b) for m in known]
        known += [m ^ b for m in known]
    by_slot = {m ^ b: (m, b) for m, b in plan}
    for chunk in range(chunks):
        go_load(chunk).wait()
        for m, b in plan:
            if m == 0 and b == bits[0]:
                gather_copy(m, b, chunk).start()
    for m, b in plan:
        if m == 0 and b != bits[0]:
            for chunk in range(chunks):
                gather_copy(m, b, chunk).start()
    taken = set()

    def arrive(slot, chunk):
        if (slot, chunk) not in taken:
            taken.add((slot, chunk))
            m, b = by_slot[slot]
            gather_copy(m, b, chunk).wait_recv()

    def relay(chunk):
        for m, b in plan:
            if m != 0:
                arrive(m, chunk)
                gather_copy(m, b, chunk).start()

    def seq_copy(src, dst, send, recv, to):
        return pltpu.make_async_remote_copy(
            src_ref=src, dst_ref=dst, send_sem=send, recv_sem=recv,
            device_id={"seq": to}, device_id_type=MESH)

    def count_copy(to, source):
        return seq_copy(cn_own, cn_in.at[source], cn_s.at[to], cn_r.at[source], to)

    def send_counts(to, carry):
        count_copy(to, me).start()
        return carry

    lax.fori_loop(me + 1, n_seq, send_counts, 0)

    def take_counts():
        def wait(source, carry):
            count_copy(source, source).wait_recv()
            return carry

        lax.fori_loop(0, me, wait, 0)
        before = lax.fori_loop(0, me, lambda j, total: total + cn_in[j], jnp.zeros(cn_own.shape, F32))
        row = before
        for b in range(nb):
            cnt_pre[:, b] = row
            row = row + cnt_block[:, b]

    def prefix_pair(h):
        return seq_copy(py_out.at[h], py_in.at[h], py_s.at[h], py_r.at[h], partner)

    def prefix_hop(h, to):
        return seq_copy(pz_out.at[h], pz_in.at[h], pz_s.at[h], pz_r.at[h], to)

    def prefix_back(h):
        return seq_copy(pa_out.at[h], pa_in.at[h], pa_s.at[h], pa_r.at[h], partner)

    loads[1].wait()
    loads[2].wait()

    def sums(h, carry):
        head_lanes = pl.ds(pl.multiple_of(h * width, width), width)
        for b in range(nb):
            rows = pl.ds(b * BLOCK, BLOCK)
            one_t = (row_at == codes_ref[pl.ds(h, 1), rows]).astype(F32).astype(BF16)
            hot_t[h, b] = one_t
            own[h, b] = nn(one_t, v_ref[rows, head_lanes])
        total = own[h, 0, other_half]
        for b in range(1, nb):
            total += own[h, b, other_half]
        py_out[h] = total.astype(BF16)
        prefix_pair(h).start()
        return carry

    lax.fori_loop(0, heads, sums, 0)

    def make_keys(h, carry):
        book = cb_ref[h]
        book_t[h] = jnp.transpose(book.astype(F32)).astype(BF16)
        for b in range(nb):
            key = nn(hot[h, b], book)
            keys[h, b] = key.astype(BF16)
            keys_t[h, b] = jnp.transpose(key).astype(BF16)
        return carry

    lax.fori_loop(0, heads, make_keys, 0)

    def prefix_chain(h):
        prefix_pair(h).wait_recv()

        @pl.when(jnp.logical_not(has_down))
        def _():
            pz_in[h] = jnp.zeros(pz_in.shape[1:], BF16)

        @pl.when(has_down)
        def _():
            prefix_hop(h, me - 2).wait_recv()

        below = pz_in[h].astype(F32)
        pair = py_in[h].astype(F32)
        total = own[h, 0, own_half]
        for b in range(1, nb):
            total += own[h, b, own_half]
        pz_out[h] = (below + total + pair).astype(BF16)

        @pl.when(has_up)
        def _():
            prefix_hop(h, me + 2).start()

        pa_out[h] = (below + total * is_lo).astype(BF16)
        prefix_back(h).start()
        prefix = below + pair * is_hi
        for b in range(nb):
            cval[h, b, own_half] = prefix.astype(BF16)
            prefix = prefix + own[h, b, own_half]

    def prefix_gather(h):
        prefix_back(h).wait_recv()
        prefix = pa_in[h].astype(F32)
        for b in range(nb):
            cval[h, b, other_half] = prefix.astype(BF16)
            prefix = prefix + own[h, b, other_half]

    def softmax(h, b):
        head_lanes = pl.ds(pl.multiple_of(h * width, width), width)
        book = cb_ref[h]
        count_full = jnp.transpose(jnp.broadcast_to(cnt_pre[h, b], (width, entries)))
        cnt_full[h, b] = count_full
        bias_full = jnp.where(count_full > 0.0, 0.0, NEG)
        counts = jnp.concatenate([count_full] * (TILE // width), axis=1)
        bias = jnp.concatenate([bias_full] * (TILE // width), axis=1)
        for p in range(parts):
            seen = (p + 1) * TILE
            query = q_ref[pl.ds(pl.multiple_of(b * BLOCK + p * TILE, TILE), TILE), head_lanes]
            at_u = lax.broadcasted_iota(jnp.int32, (seen, TILE), 0)
            at_t = lax.broadcasted_iota(jnp.int32, (seen, TILE), 1) + p * TILE
            scores = jnp.where(at_u <= at_t, nt(keys[h, b, 0:seen], query) * (scale * LOG2E), NEG)
            cache_scores = nt(book, query) * (scale * LOG2E) + bias
            highest = jnp.maximum(
                jnp.max(scores, axis=0, keepdims=True), jnp.max(cache_scores, axis=0, keepdims=True))
            local_exp = jnp.exp2(scores - highest)
            cache_exp = jnp.exp2(cache_scores - highest)
            total = jnp.sum(local_exp, axis=0, keepdims=True) + jnp.sum(cache_exp * counts, axis=0, keepdims=True)
            inverse = 1.0 / total
            lanes = slice(p * TILE, seen)
            local_low[h, b, 0:seen, lanes] = (local_exp * inverse).astype(BF16)
            if seen < BLOCK:
                local_low[h, b, seen:BLOCK, lanes] = jnp.zeros((BLOCK - seen, TILE), BF16)
            cache_low[h, b, :, lanes] = (cache_exp * inverse).astype(BF16)

    pairs = heads // 2
    rounds = heads * nb // 2
    turn = 2 * at

    def chain_at(slot):
        j = slot - turn

        @pl.when((j >= 0) & (j < pairs))
        def _():
            prefix_chain(2 * j)
            prefix_chain(2 * j + 1)

    relay_at = {}
    for chunk in range(chunks):
        where = ("pre", "pre", 1, rounds - 1, "mid", rounds, rounds + 2, rounds + heads - 1)[8 * chunk // chunks]
        relay_at.setdefault(where, []).append(chunk)

    def relays(first, last, now):
        for slot, which in relay_at.items():
            if not isinstance(slot, str) and first <= slot < last:
                @pl.when(now == slot - first)
                def _(which=which):
                    for chunk in which:
                        relay(chunk)

    def relay_named(name):
        for chunk in relay_at.get(name, []):
            relay(chunk)

    chain_at(0)
    take_counts()
    chain_at(1)
    relay_named("pre")
    loads[3].wait()

    def unit(k, carry):
        softmax(2 * k // nb, 2 * k % nb)
        softmax((2 * k + 1) // nb, (2 * k + 1) % nb)
        chain_at(k + 2)
        relays(0, rounds, k)
        return carry

    lax.fori_loop(0, rounds, unit, 0)
    loads[4].wait()

    depth = go_in.shape[1]

    def project(start):
        rows = pl.ds(start, TILE)
        total = nt(gath[0, rows], w_ref[:, 0:depth])
        for k in range(1, n_head):
            total += nt(gath[k, rows], w_ref[:, k * depth:(k + 1) * depth])
        dout[rows] = total.astype(BF16)

    def value_pass(h, b):
        head_lanes = pl.ds(pl.multiple_of(h * width, width), width)
        vpart[h, b] = nn(cache_low[h, b], dout[pl.ds(b * BLOCK, BLOCK), head_lanes])

    def grad_pass(h, b):
        head_lanes = pl.ds(pl.multiple_of(h * width, width), width)
        rows = pl.ds(b * BLOCK, BLOCK)
        query = q_ref[rows, head_lanes]
        grad = dout[rows, head_lanes]
        counts = jnp.concatenate([cnt_full[h, b]] * (BLOCK // width), axis=1)
        local_grad = nt(v_ref[rows, head_lanes], grad)
        cache_grad = nt(cval[h, b], grad)
        local_prob = local_low[h, b].astype(F32)
        cache_prob = cache_low[h, b].astype(F32)
        delta = (jnp.sum(local_prob * local_grad, axis=0, keepdims=True)
                 + jnp.sum(cache_prob * cache_grad, axis=0, keepdims=True))
        local_score_grad = (local_prob * (local_grad - delta) * scale).astype(BF16)
        cache_score_grad = (cache_prob * (cache_grad - delta * counts) * scale).astype(BF16)
        gq_t = nn(keys_t[h, b], local_score_grad) + nn(book_t[h], cache_score_grad)
        gq_ref[rows, head_lanes] = jnp.transpose(gq_t).astype(BF16)
        key_grad = nn(local_score_grad, query).astype(BF16)
        code = nn(hot_t[h, b], key_grad) + nn(cache_score_grad, query)
        local_part[h, b] = nn(local_low[h, b], grad)
        if b == 0:
            code_acc[h] = code
        else:
            code_acc[h] += code

    def later_pair(h):
        return seq_copy(ly_out.at[h], ly_in.at[h], ly_s.at[h], ly_r.at[h], partner)

    def later_hop(h, to):
        return seq_copy(lz_out.at[h], lz_in.at[h], lz_s.at[h], lz_r.at[h], to)

    def later_back(h):
        return seq_copy(la_out.at[h], la_in.at[h], la_s.at[h], la_r.at[h], partner)

    def part_total(h, span):
        total = vpart[h, 0, span]
        for b in range(1, nb):
            total += vpart[h, b, span]
        return total

    def send_later(h):
        ly_out[h] = part_total(h, other_half).astype(BF16)
        later_pair(h).start()

    def later_chain(h):
        later_pair(h).wait_recv()

        @pl.when(jnp.logical_not(has_up))
        def _():
            lz_in[h] = jnp.zeros(lz_in.shape[1:], BF16)

        @pl.when(has_up)
        def _():
            later_hop(h, me + 2).wait_recv()

        above = lz_in[h].astype(F32)
        pair = ly_in[h].astype(F32)
        total = part_total(h, own_half)
        lz_out[h] = (above + total + pair).astype(BF16)

        @pl.when(has_down)
        def _():
            later_hop(h, me - 2).start()

        la_out[h] = (above + total * is_hi).astype(BF16)
        later_back(h).start()
        later_ref[h, own_half] = above + pair * is_lo

    def later_gather(h):
        later_back(h).wait_recv()
        later_ref[h, other_half] = la_in[h].astype(F32)
        head_lanes = pl.ds(pl.multiple_of(h * width, width), width)
        later = later_ref[h]
        for b in reversed(range(nb)):
            rows = pl.ds(b * BLOCK, BLOCK)
            lookup = nn(hot[h, b], later.astype(BF16))
            gv_ref[rows, head_lanes] = (local_part[h, b] + lookup).astype(BF16)
            later = later + vpart[h, b]

    def code_pair(h):
        return seq_copy(cy_out.at[h], cy_in.at[h], cy_s.at[h], cy_r.at[h], partner)

    def code_out(h, to, source):
        return seq_copy(
            cz_out.at[h, to], cz_in.at[h, source], cz_s.at[h, to], cz_r.at[h, source], 2 * to + side)

    def code_back(h, to, source):
        return seq_copy(
            c_fin.at[h, side, source], c_fin.at[h, side, source], cf_s.at[h, to], cf_r.at[h, source], 2 * to + side)

    def code_half(h, which):
        return seq_copy(c_fin.at[h, which], c_fin.at[h, which], ca_s.at[h], ca_r.at[h], partner)

    def over_chain(action):
        def body(k, carry):
            action((at + k) % outer)
            return carry

        lax.fori_loop(1, outer, body, 0)

    def send_code(h):
        cy_out[h] = code_acc[h, other_half].astype(BF16)
        code_pair(h).start()

    def reduce_code(h):
        code_pair(h).wait_recv()
        total = code_acc[h, own_half] + cy_in[h].astype(F32)
        cz_out[h] = total.astype(BF16).reshape(outer, piece, width)
        over_chain(lambda to: code_out(h, to, at).start())
        cz_in[h, at] = cz_out[h, at]

    def spread_code(h):
        over_chain(lambda source: code_out(h, source, source).wait_recv())
        total = cz_in[h, 0].astype(F32)
        for k in range(1, outer):
            total += cz_in[h, k].astype(F32)
        c_fin[h, side, at] = total.astype(BF16)
        over_chain(lambda to: code_back(h, to, at).start())

    def pair_code(h):
        over_chain(lambda source: code_back(h, source, source).wait_recv())
        code_half(h, side).start()
        gc_ref[h, own_half] = c_fin[h, side].astype(F32).reshape(half, width)

    def last_code(h):
        code_half(h, 1 - side).wait_recv()
        gc_ref[h, other_half] = c_fin[h, 1 - side].astype(F32).reshape(half, width)

    for b in range(nb):
        final = b == nb - 1
        for part in range(parts):
            start = b * BLOCK + part * TILE
            for chunk in range(start // CHUNK, (start + TILE) // CHUNK):
                for slot in by_slot:
                    arrive(slot, chunk)
            project(start)
        if b == 0:
            relay_named("mid")

            def rest(j, carry):
                @pl.when(turn + j >= rounds + 2)
                def _():
                    prefix_chain(2 * j)
                    prefix_chain(2 * j + 1)

                return carry

            lax.fori_loop(0, pairs, rest, 0)

        def values(h, carry, b=b, final=final):
            value_pass(h, b)
            if final:
                send_later(h)
            return carry

        lax.fori_loop(0, heads, values, 0)

        def grads(h, carry, b=b, final=final):
            if b == 0:
                prefix_gather(h)
            grad_pass(h, b)
            if b == 0:
                relays(rounds, rounds + heads, h)
            if final:
                send_code(h)

                @pl.when(jnp.logical_not(has_up) & (h >= 1))
                def _():
                    later_chain(h - 1)

            return carry

        lax.fori_loop(0, heads, grads, 0)

    behind = outer - 1 - at
    soon = behind * 2 < outer
    last_ones = behind * 4 >= 3 * outer

    @pl.when(behind == 0)
    def _():
        later_chain(heads - 1)

    def chain_step(h, carry):
        @pl.when(soon & (behind > 0))
        def _():
            later_chain(h)

        return carry

    lax.fori_loop(0, heads, chain_step, 0)

    def reduce_step(h, carry):
        reduce_code(h)

        @pl.when(jnp.logical_not(soon | last_ones))
        def _():
            later_chain(h)

        return carry

    lax.fori_loop(0, heads, reduce_step, 0)

    def spread_step(h, carry):
        @pl.when(last_ones)
        def _():
            later_chain(h)

        spread_code(h)
        return carry

    lax.fori_loop(0, heads, spread_step, 0)

    def pair_step(h, carry):
        pair_code(h)
        later_gather(h)
        return carry

    lax.fori_loop(0, heads, pair_step, 0)

    def last_step(h, carry):
        last_code(h)
        return carry

    lax.fori_loop(0, heads, last_step, 0)

    def drain(h, carry):
        prefix_pair(h).wait_send()
        prefix_back(h).wait_send()
        later_pair(h).wait_send()
        later_back(h).wait_send()

        @pl.when(has_up)
        def _():
            prefix_hop(h, me + 2).wait_send()

        @pl.when(has_down)
        def _():
            later_hop(h, me - 2).wait_send()

        code_pair(h).wait_send()
        code_half(h, side).wait_send()
        over_chain(lambda to: code_out(h, to, at).wait_send())
        over_chain(lambda to: code_back(h, to, at).wait_send())
        return carry

    lax.fori_loop(0, heads, drain, 0)

    def drain_counts(to, carry):
        count_copy(to, me).wait_send()
        return carry

    lax.fori_loop(me + 1, n_seq, drain_counts, 0)
    for m, b in plan:
        for chunk in range(chunks):
            gather_copy(m, b, chunk).wait_send()


def write_out(*refs):
    sems = refs[-1]
    copies = [pltpu.make_async_copy(refs[k], refs[k + 3], sems.at[k]) for k in range(3)]
    for copy in copies:
        copy.start()
    for copy in copies:
        copy.wait()


def per_device(queries, values, codes, codebook, out_weight, grad_out):
    n_seq, n_head = lax.axis_size("seq"), lax.axis_size("head")
    row_count = queries.shape[0]
    heads, entries, width = codebook.shape
    nb = row_count // BLOCK
    parts = BLOCK // TILE
    chunks = row_count // CHUNK
    half = entries // 2
    hbm = pl.BlockSpec(memory_space=pltpu.HBM)
    vmem = pl.BlockSpec(memory_space=pltpu.VMEM)
    dma = pltpu.SemaphoreType.DMA
    halves = pltpu.VMEM((heads, half, width), BF16)
    pieces = pltpu.VMEM((heads, n_seq // 2, entries // n_seq, width), BF16)
    counts = pltpu.VMEM((heads, 1, entries), F32)
    results = pl.pallas_call(
        functools.partial(kernel, n_seq, n_head),
        out_shape=(
            jax.ShapeDtypeStruct(queries.shape, BF16),
            jax.ShapeDtypeStruct(queries.shape, BF16),
            jax.ShapeDtypeStruct(codebook.shape, F32),
        ),
        in_specs=[hbm] * 6,
        out_specs=(vmem,) * 3,
        scratch_shapes=[
            pltpu.VMEM(queries.shape, BF16),
            pltpu.VMEM(queries.shape, BF16),
            pltpu.VMEM((heads, row_count), jnp.int32),
            pltpu.VMEM(codebook.shape, BF16),
            pltpu.VMEM(out_weight.shape, BF16),
            pltpu.VMEM((n_head,) + grad_out.shape, BF16),
            pltpu.VMEM(queries.shape, BF16),
            pltpu.VMEM((heads, nb, entries, BLOCK), BF16),
            pltpu.VMEM((heads, nb, BLOCK, entries), BF16),
            pltpu.VMEM((heads, nb, BLOCK, width), BF16),
            pltpu.VMEM((heads, nb, width, BLOCK), BF16),
            pltpu.VMEM((heads, width, entries), BF16),
            pltpu.VMEM((heads, nb, entries, width), F32),
            pltpu.VMEM((heads, nb, 1, entries), F32),
            pltpu.VMEM((heads, nb, 1, entries), F32),
            pltpu.VMEM((heads, nb, entries, width), F32),
            pltpu.VMEM((heads, nb, entries, width), BF16),
            pltpu.VMEM((heads, nb, BLOCK, BLOCK), BF16),
            pltpu.VMEM((heads, nb, entries, BLOCK), BF16),
            pltpu.VMEM((heads, nb, BLOCK, width), F32),
            pltpu.VMEM((heads, nb, entries, width), F32),
            pltpu.VMEM((heads, entries, width), F32),
            pltpu.VMEM((heads, entries, width), F32),
            counts, pltpu.VMEM((n_seq, heads, 1, entries), F32),
            halves, halves, halves, halves, halves, halves,
            halves, halves, halves, halves, halves, halves,
            halves, halves, pieces, pieces,
            pltpu.VMEM((heads, 2, n_seq // 2, entries // n_seq, width), BF16),
            dma((5,)), dma((chunks,)),
            dma((n_head, chunks)), dma((n_head, chunks)),
            dma((n_seq,)), dma((n_seq,)),
        ] + [dma((heads,))] * 16 + [dma((heads, n_seq // 2))] * 4,
        compiler_params=pltpu.CompilerParams(
            collective_id=0, has_side_effects=True, vmem_limit_bytes=50 * 1024 * 1024),
    )(*(pltpu.with_memory_space_constraint(x, pltpu.HBM) for x in (queries, values, codes.T, codebook, out_weight, grad_out)))
    return pl.pallas_call(
        write_out,
        out_shape=tuple(jax.ShapeDtypeStruct(r.shape, r.dtype) for r in results),
        in_specs=[vmem] * 3,
        out_specs=(hbm,) * 3,
        scratch_shapes=[dma((3,))],
        compiler_params=pltpu.CompilerParams(vmem_limit_bytes=1024 * 1024),
    )(*results)


def solution(mesh):
    return jax.shard_map(
        per_device,
        mesh=mesh,
        in_specs=(
            P("seq", "head"),
            P("seq", "head"),
            P("seq", "head"),
            P("head", None, None),
            P("head", None),
            P("seq", "head"),
        ),
        out_specs=(P("seq", "head"), P("seq", "head"), P("head", None, None)),
        check_vma=False,
    )
```

```python
import functools

import jax
import jax.numpy as jnp
from jax import lax
from jax.experimental import pallas as pl
from jax.experimental.pallas import tpu as pltpu
from jax.sharding import PartitionSpec as P

BLOCK = 512
TILE = 256
CHUNK = 128
SUBS = 2
NEG = -1e30
LOG2E = 1.4426950408889634
F32 = jnp.float32
BF16 = jnp.bfloat16
MESH = pl.DeviceIdType.MESH


def nn(a, b):
    return lax.dot_general(a, b, (((1,), (0,)), ((), ())), preferred_element_type=F32)


def nt(a, b):
    return lax.dot_general(a, b, (((1,), (1,)), ((), ())), preferred_element_type=F32)


def kernel(
    n_seq, n_head,
    q_in, v_in, codes_in, cb_in, w_in, go_in,
    gq_ref, gv_ref, gc_ref,
    q_ref, v_ref, codes_ref, cb_ref, w_ref, gath, dout,
    hot_t, hot, keys, keys_t, book_t, own, cnt_block, cnt_pre, cnt_full, cval,
    local_low, cache_low, local_part, vpart, code_acc, later_ref,
    cn_own, cn_in,
    py_out, py_in, pz_out, pz_in, pa_out, pa_in,
    ly_out, ly_in, lz_out, lz_in, la_out, la_in,
    cy_out, cy_in, c_out, c_below, c_above, c_fin,
    load_s, go_s, ag_s, ag_r, cn_s, cn_r,
    py_s, py_r, pz_s, pz_r, pa_s, pa_r,
    ly_s, ly_r, lz_s, lz_r, la_s, la_r,
    cy_s, cy_r, c_s, cb_r, cu_r, cp_s, cp_r, fu_s, fd_s, cf_r,
):
    rows_all = q_ref.shape[0]
    heads, entries, width = cb_ref.shape
    nb = rows_all // BLOCK
    parts = BLOCK // TILE
    chunks = rows_all // CHUNK
    per_tile = TILE // CHUNK
    outer = n_seq // 2
    half = entries // 2
    piece = half // SUBS
    center = outer // 2
    scale = width ** (-0.5)
    me = lax.axis_index("seq")
    mine = lax.axis_index("head")
    at = me // 2
    side = me % 2
    partner = me + 1 - 2 * side
    is_hi = side.astype(F32)
    is_lo = 1.0 - is_hi
    own_half = pl.ds(pl.multiple_of(side * half, half), half)
    other_half = pl.ds(pl.multiple_of((1 - side) * half, half), half)
    has_down = at > 0
    has_up = at < outer - 1
    bits = []
    bit = n_head // 2
    while bit >= 1:
        bits.append(bit)
        bit //= 2

    def flip(index, mask):
        for b in bits:
            if mask & b:
                index = index + b - 2 * b * ((index // b) % 2)
        return index

    def go_load(chunk):
        span = pl.ds(chunk * CHUNK, CHUNK)
        return pltpu.make_async_copy(go_in.at[span], gath.at[mine, span], go_s.at[chunk])

    loads = [
        pltpu.make_async_copy(src, dst, load_s.at[k])
        for k, (src, dst) in enumerate(
            ((codes_in, codes_ref), (cb_in, cb_ref), (v_in, v_ref), (q_in, q_ref), (w_in, w_ref)))
    ]
    loads[0].start()
    for chunk in range(chunks):
        go_load(chunk).start()
    for copy in loads[1:]:
        copy.start()

    barrier = pltpu.get_barrier_semaphore()
    def greet(k, carry):
        pl.semaphore_signal(barrier, inc=1, device_id={"seq": (me + k) % n_seq}, device_id_type=MESH)
        return carry

    lax.fori_loop(1, n_seq, greet, 0)
    for b in bits:
        pl.semaphore_signal(barrier, inc=1, device_id={"head": flip(mine, b)}, device_id_type=MESH)

    loads[0].wait()
    row_at = lax.broadcasted_iota(jnp.int32, (entries, BLOCK), 0)
    lane_at = lax.broadcasted_iota(jnp.int32, (BLOCK, entries), 1)

    def count(h, carry):
        total = jnp.zeros((1, entries), F32)
        for b in range(nb):
            code_row = codes_ref[pl.ds(h, 1), pl.ds(b * BLOCK, BLOCK)]
            code_full = jnp.transpose(jnp.broadcast_to(code_row, (width, BLOCK)))
            code_cols = jnp.concatenate([code_full] * (entries // width), axis=1)
            one_f = (lane_at == code_cols).astype(F32)
            hot[h, b] = one_f.astype(BF16)
            counts = jnp.sum(one_f, axis=0, keepdims=True)
            cnt_block[h, b] = counts
            total += counts
        cn_own[h] = total
        return carry

    lax.fori_loop(0, heads, count, 0)
    pl.semaphore_wait(barrier, n_seq - 1 + len(bits))

    def gather_copy(src_mask, to, chunk):
        block = flip(mine, src_mask)
        span = pl.ds(chunk * CHUNK, CHUNK)
        slot = src_mask ^ to
        return pltpu.make_async_remote_copy(
            src_ref=gath.at[block, span], dst_ref=gath.at[block, span],
            send_sem=ag_s.at[slot, chunk], recv_sem=ag_r.at[slot, chunk],
            device_id={"head": flip(mine, to)}, device_id_type=MESH)

    plan = []
    known = [0]
    for b in bits:
        plan += [(m, b) for m in known]
        known += [m ^ b for m in known]
    by_slot = {m ^ b: (m, b) for m, b in plan}
    for chunk in range(chunks):
        go_load(chunk).wait()
        for m, b in plan:
            if m == 0 and b == bits[0]:
                gather_copy(m, b, chunk).start()
    for m, b in plan:
        if m == 0 and b != bits[0]:
            for chunk in range(chunks):
                gather_copy(m, b, chunk).start()
    taken = set()

    def arrive(slot, chunk):
        if (slot, chunk) not in taken:
            taken.add((slot, chunk))
            m, b = by_slot[slot]
            gather_copy(m, b, chunk).wait_recv()

    def relay(chunk):
        for m, b in plan:
            if m != 0:
                arrive(m, chunk)
                gather_copy(m, b, chunk).start()

    def seq_copy(src, dst, send, recv, to):
        return pltpu.make_async_remote_copy(
            src_ref=src, dst_ref=dst, send_sem=send, recv_sem=recv,
            device_id={"seq": to}, device_id_type=MESH)

    def count_copy(to, source):
        return seq_copy(cn_own, cn_in.at[source], cn_s.at[to], cn_r.at[source], to)

    def send_counts(to, carry):
        count_copy(to, me).start()
        return carry

    lax.fori_loop(me + 1, n_seq, send_counts, 0)

    def take_counts():
        def wait(source, carry):
            count_copy(source, source).wait_recv()
            return carry

        lax.fori_loop(0, me, wait, 0)
        before = lax.fori_loop(0, me, lambda j, total: total + cn_in[j], jnp.zeros(cn_own.shape, F32))
        row = before
        for b in range(nb):
            cnt_pre[:, b] = row
            row = row + cnt_block[:, b]

    def prefix_pair(h):
        return seq_copy(py_out.at[h], py_in.at[h], py_s.at[h], py_r.at[h], partner)

    def prefix_hop(h, to):
        return seq_copy(pz_out.at[h], pz_in.at[h], pz_s.at[h], pz_r.at[h], to)

    def prefix_back(h):
        return seq_copy(pa_out.at[h], pa_in.at[h], pa_s.at[h], pa_r.at[h], partner)

    loads[1].wait()
    loads[2].wait()

    def sums(h, carry):
        head_lanes = pl.ds(pl.multiple_of(h * width, width), width)
        for b in range(nb):
            rows = pl.ds(b * BLOCK, BLOCK)
            one_t = (row_at == codes_ref[pl.ds(h, 1), rows]).astype(F32).astype(BF16)
            hot_t[h, b] = one_t
            own[h, b] = nn(one_t, v_ref[rows, head_lanes])
        total = own[h, 0, other_half]
        for b in range(1, nb):
            total += own[h, b, other_half]
        py_out[h] = total.astype(BF16)
        prefix_pair(h).start()
        return carry

    lax.fori_loop(0, heads, sums, 0)

    def make_keys(h, carry):
        book = cb_ref[h]
        book_t[h] = jnp.transpose(book.astype(F32)).astype(BF16)
        for b in range(nb):
            key = nn(hot[h, b], book)
            keys[h, b] = key.astype(BF16)
            keys_t[h, b] = jnp.transpose(key).astype(BF16)
        return carry

    lax.fori_loop(0, heads, make_keys, 0)

    def prefix_chain(h):
        prefix_pair(h).wait_recv()

        @pl.when(jnp.logical_not(has_down))
        def _():
            pz_in[h] = jnp.zeros(pz_in.shape[1:], BF16)

        @pl.when(has_down)
        def _():
            prefix_hop(h, me - 2).wait_recv()

        below = pz_in[h].astype(F32)
        pair = py_in[h].astype(F32)
        total = own[h, 0, own_half]
        for b in range(1, nb):
            total += own[h, b, own_half]
        pz_out[h] = (below + total + pair).astype(BF16)

        @pl.when(has_up)
        def _():
            prefix_hop(h, me + 2).start()

        pa_out[h] = (below + total * is_lo).astype(BF16)
        prefix_back(h).start()
        prefix = below + pair * is_hi
        for b in range(nb):
            cval[h, b, own_half] = prefix.astype(BF16)
            prefix = prefix + own[h, b, own_half]

    def prefix_gather(h):
        prefix_back(h).wait_recv()
        prefix = pa_in[h].astype(F32)
        for b in range(nb):
            cval[h, b, other_half] = prefix.astype(BF16)
            prefix = prefix + own[h, b, other_half]

    def softmax(h, b):
        head_lanes = pl.ds(pl.multiple_of(h * width, width), width)
        book = cb_ref[h]
        count_full = jnp.transpose(jnp.broadcast_to(cnt_pre[h, b], (width, entries)))
        cnt_full[h, b] = count_full
        bias_full = jnp.where(count_full > 0.0, 0.0, NEG)
        counts = jnp.concatenate([count_full] * (TILE // width), axis=1)
        bias = jnp.concatenate([bias_full] * (TILE // width), axis=1)
        for p in range(parts):
            seen = (p + 1) * TILE
            query = q_ref[pl.ds(pl.multiple_of(b * BLOCK + p * TILE, TILE), TILE), head_lanes]
            at_u = lax.broadcasted_iota(jnp.int32, (seen, TILE), 0)
            at_t = lax.broadcasted_iota(jnp.int32, (seen, TILE), 1) + p * TILE
            scores = jnp.where(at_u <= at_t, nt(keys[h, b, 0:seen], query) * (scale * LOG2E), NEG)
            cache_scores = nt(book, query) * (scale * LOG2E) + bias
            highest = jnp.maximum(
                jnp.max(scores, axis=0, keepdims=True), jnp.max(cache_scores, axis=0, keepdims=True))
            local_exp = jnp.exp2(scores - highest)
            cache_exp = jnp.exp2(cache_scores - highest)
            total = jnp.sum(local_exp, axis=0, keepdims=True) + jnp.sum(cache_exp * counts, axis=0, keepdims=True)
            inverse = 1.0 / total
            lanes = slice(p * TILE, seen)
            local_low[h, b, 0:seen, lanes] = (local_exp * inverse).astype(BF16)
            if seen < BLOCK:
                local_low[h, b, seen:BLOCK, lanes] = jnp.zeros((BLOCK - seen, TILE), BF16)
            cache_low[h, b, :, lanes] = (cache_exp * inverse).astype(BF16)

    rounds = heads * nb // 2
    turn = 2 * at

    def chain_at(slot):
        h = slot - turn

        @pl.when((h >= 0) & (h < heads))
        def _():
            prefix_chain(h)

    relay_at = {}
    for chunk in range(chunks):
        where = (0, 1, rounds - 1, "mid", "late", rounds, rounds + 2, rounds + heads - 1)[8 * chunk // chunks]
        relay_at.setdefault(where, []).append(chunk)

    def relays(first, last, now):
        for slot, which in relay_at.items():
            if not isinstance(slot, str) and first <= slot < last:
                @pl.when(now == slot - first)
                def _(which=which):
                    for chunk in which:
                        relay(chunk)

    def relay_named(name):
        for chunk in relay_at.get(name, []):
            relay(chunk)

    chain_at(0)
    take_counts()
    chain_at(1)
    loads[3].wait()

    def unit(k, carry):
        softmax(2 * k // nb, 2 * k % nb)
        softmax((2 * k + 1) // nb, (2 * k + 1) % nb)
        chain_at(k + 2)
        relays(0, rounds, k)
        return carry

    lax.fori_loop(0, rounds, unit, 0)
    loads[4].wait()

    depth = go_in.shape[1]

    def project(start):
        rows = pl.ds(start, TILE)
        total = nt(gath[0, rows], w_ref[:, 0:depth])
        for k in range(1, n_head):
            total += nt(gath[k, rows], w_ref[:, k * depth:(k + 1) * depth])
        dout[rows] = total.astype(BF16)

    def value_pass(h, b):
        head_lanes = pl.ds(pl.multiple_of(h * width, width), width)
        vpart[h, b] = nn(cache_low[h, b], dout[pl.ds(b * BLOCK, BLOCK), head_lanes])

    def grad_pass(h, b):
        head_lanes = pl.ds(pl.multiple_of(h * width, width), width)
        rows = pl.ds(b * BLOCK, BLOCK)
        query = q_ref[rows, head_lanes]
        grad = dout[rows, head_lanes]
        counts = jnp.concatenate([cnt_full[h, b]] * (BLOCK // width), axis=1)
        local_grad = nt(v_ref[rows, head_lanes], grad)
        cache_grad = nt(cval[h, b], grad)
        local_prob = local_low[h, b].astype(F32)
        cache_prob = cache_low[h, b].astype(F32)
        delta = (jnp.sum(local_prob * local_grad, axis=0, keepdims=True)
                 + jnp.sum(cache_prob * cache_grad, axis=0, keepdims=True))
        local_score_grad = (local_prob * (local_grad - delta) * scale).astype(BF16)
        cache_score_grad = (cache_prob * (cache_grad - delta * counts) * scale).astype(BF16)
        gq_t = nn(keys_t[h, b], local_score_grad) + nn(book_t[h], cache_score_grad)
        gq_ref[rows, head_lanes] = jnp.transpose(gq_t).astype(BF16)
        key_grad = nn(local_score_grad, query).astype(BF16)
        code = nn(hot_t[h, b], key_grad) + nn(cache_score_grad, query)
        local_part[h, b] = nn(local_low[h, b], grad)
        if b == 0:
            code_acc[h] = code
        else:
            code_acc[h] += code

    def later_pair(h):
        return seq_copy(ly_out.at[h], ly_in.at[h], ly_s.at[h], ly_r.at[h], partner)

    def later_hop(h, to):
        return seq_copy(lz_out.at[h], lz_in.at[h], lz_s.at[h], lz_r.at[h], to)

    def later_back(h):
        return seq_copy(la_out.at[h], la_in.at[h], la_s.at[h], la_r.at[h], partner)

    def part_total(h, span):
        total = vpart[h, 0, span]
        for b in range(1, nb):
            total += vpart[h, b, span]
        return total

    def send_later(h):
        ly_out[h] = part_total(h, other_half).astype(BF16)
        later_pair(h).start()

    def later_chain(h):
        later_pair(h).wait_recv()

        @pl.when(jnp.logical_not(has_up))
        def _():
            lz_in[h] = jnp.zeros(lz_in.shape[1:], BF16)

        @pl.when(has_up)
        def _():
            later_hop(h, me + 2).wait_recv()

        above = lz_in[h].astype(F32)
        pair = ly_in[h].astype(F32)
        total = part_total(h, own_half)
        lz_out[h] = (above + total + pair).astype(BF16)

        @pl.when(has_down)
        def _():
            later_hop(h, me - 2).start()

        la_out[h] = (above + total * is_hi).astype(BF16)
        later_ref[h, own_half] = above + pair * is_lo

    def later_gather(h):
        later_back(h).wait_recv()
        later_ref[h, other_half] = la_in[h].astype(F32)
        head_lanes = pl.ds(pl.multiple_of(h * width, width), width)
        later = later_ref[h]
        for b in reversed(range(nb)):
            rows = pl.ds(b * BLOCK, BLOCK)
            lookup = nn(hot[h, b], later.astype(BF16))
            gv_ref[rows, head_lanes] = (local_part[h, b] + lookup).astype(BF16)
            later = later + vpart[h, b]

    def code_pair(h):
        return seq_copy(cy_out.at[h], cy_in.at[h], cy_s.at[h], cy_r.at[h], partner)

    def code_up(h, s):
        return seq_copy(c_out.at[h, s], c_below.at[h, s], c_s.at[h, s], cb_r.at[h, s], me + 2)

    def code_down(h, s):
        return seq_copy(c_out.at[h, s], c_above.at[h, s], c_s.at[h, s], cu_r.at[h, s], me - 2)

    def fin_up(h, s):
        return seq_copy(c_fin.at[h, side, s], c_fin.at[h, side, s], fu_s.at[h, s], cf_r.at[h, s], me + 2)

    def fin_down(h, s):
        return seq_copy(c_fin.at[h, side, s], c_fin.at[h, side, s], fd_s.at[h, s], cf_r.at[h, s], me - 2)

    def fin_pair(h, which, s):
        return seq_copy(c_fin.at[h, which, s], c_fin.at[h, which, s], cp_s.at[h, s], cp_r.at[h, s], partner)

    def send_code(h):
        cy_out[h] = code_acc[h, other_half].astype(BF16)
        code_pair(h).start()

    def piece_of(which, s):
        return pl.ds(pl.multiple_of(which * half + s * piece, piece), piece)

    def reduce_code(h):
        code_pair(h).wait_recv()
        code_acc[h, own_half] += cy_in[h].astype(F32)
        for s in range(SUBS):
            span = piece_of(side, s)

            @pl.when((at <= center) & has_down)
            def _(s=s, span=span):
                code_up(h, s).wait_recv()
                code_acc[h, span] += c_below[h, s].astype(F32)

            @pl.when((at >= center) & has_up)
            def _(s=s, span=span):
                code_down(h, s).wait_recv()
                code_acc[h, span] += c_above[h, s].astype(F32)

            c_out[h, s] = code_acc[h, span].astype(BF16)

            @pl.when(at < center)
            def _(s=s):
                code_up(h, s).start()

            @pl.when(at > center)
            def _(s=s):
                code_down(h, s).start()

    def spread_code(h):
        for s in range(SUBS):
            @pl.when(at == center)
            def _(s=s):
                c_fin[h, side, s] = c_out[h, s]

            @pl.when(at != center)
            def _(s=s):
                fin_up(h, s).wait_recv()

            @pl.when((at <= center) & has_down)
            def _(s=s):
                fin_down(h, s).start()

            @pl.when((at >= center) & has_up)
            def _(s=s):
                fin_up(h, s).start()

            fin_pair(h, side, s).start()
            gc_ref[h, piece_of(side, s)] = c_fin[h, side, s].astype(F32)

    def last_code(h):
        for s in range(SUBS):
            fin_pair(h, 1 - side, s).wait_recv()
            gc_ref[h, piece_of(1 - side, s)] = c_fin[h, 1 - side, s].astype(F32)

    for b in range(nb):
        final = b == nb - 1
        for part in range(parts):
            start = b * BLOCK + part * TILE
            for chunk in range(start // CHUNK, (start + TILE) // CHUNK):
                for slot in by_slot:
                    arrive(slot, chunk)
            project(start)
            if b == 0:
                if part == 0:
                    relay_named("mid")
                chain_at(rounds + 2 + part)
        def values(h, carry, b=b, final=final):
            value_pass(h, b)
            if final:
                send_later(h)
            return carry

        lax.fori_loop(0, heads, values, 0)
        if b == 0:
            relay_named("late")

            def rest(h, carry):
                @pl.when(turn + h >= rounds + 2 + parts)
                def _():
                    prefix_chain(h)

                return carry

            lax.fori_loop(0, heads, rest, 0)

        def grads(h, carry, b=b, final=final):
            if b == 0:
                prefix_gather(h)
            grad_pass(h, b)
            if b == 0:
                relays(rounds, rounds + heads, h)
            if final:
                send_code(h)

                @pl.when(jnp.logical_not(has_up) & (h >= 1))
                def _():
                    later_chain(h - 1)

            return carry

        lax.fori_loop(0, heads, grads, 0)

    behind = outer - 1 - at
    soon = behind * 2 < outer

    @pl.when(behind == 0)
    def _():
        later_chain(heads - 1)

    def chain_step(h, carry):
        @pl.when(soon & (behind > 0))
        def _():
            later_chain(h)

        return carry

    lax.fori_loop(0, heads, chain_step, 0)

    def reduce_step(h, carry):
        reduce_code(h)

        @pl.when(at == center)
        def _():
            spread_code(h)

        @pl.when(jnp.logical_not(soon) & has_down)
        def _():
            later_chain(h)
            later_back(h).start()

        return carry

    lax.fori_loop(0, heads, reduce_step, 0)

    def back_step(h, carry):
        @pl.when(jnp.logical_not(soon | has_down))
        def _():
            later_chain(h)

        @pl.when(soon | jnp.logical_not(has_down))
        def _():
            later_back(h).start()

        return carry

    lax.fori_loop(0, heads, back_step, 0)

    def drain_early(h, carry):
        prefix_pair(h).wait_send()
        prefix_back(h).wait_send()

        @pl.when(has_up)
        def _():
            prefix_hop(h, me + 2).wait_send()

        return carry

    lax.fori_loop(0, heads, drain_early, 0)

    def drain_counts(to, carry):
        count_copy(to, me).wait_send()
        return carry

    lax.fori_loop(me + 1, n_seq, drain_counts, 0)

    for m, b in plan:
        for chunk in range(chunks):
            gather_copy(m, b, chunk).wait_send()

    def spread_step(h, carry):
        @pl.when(at != center)
        def _():
            spread_code(h)

        return carry

    lax.fori_loop(0, heads, spread_step, 0)

    def last_step(h, carry):
        later_gather(h)
        last_code(h)
        return carry

    lax.fori_loop(0, heads, last_step, 0)

    def drain(h, carry):
        later_pair(h).wait_send()
        later_back(h).wait_send()

        @pl.when(has_down)
        def _():
            later_hop(h, me - 2).wait_send()

        code_pair(h).wait_send()
        for s in range(SUBS):
            @pl.when(at < center)
            def _(s=s):
                code_up(h, s).wait_send()

            @pl.when(at > center)
            def _(s=s):
                code_down(h, s).wait_send()

            @pl.when((at <= center) & has_down)
            def _(s=s):
                fin_down(h, s).wait_send()

            @pl.when((at >= center) & has_up)
            def _(s=s):
                fin_up(h, s).wait_send()

            fin_pair(h, side, s).wait_send()

        return carry

    lax.fori_loop(0, heads, drain, 0)


def write_out(*refs):
    sems = refs[-1]
    copies = [pltpu.make_async_copy(refs[k], refs[k + 3], sems.at[k]) for k in range(3)]
    for copy in copies:
        copy.start()
    for copy in copies:
        copy.wait()


def per_device(queries, values, codes, codebook, out_weight, grad_out):
    n_seq, n_head = lax.axis_size("seq"), lax.axis_size("head")
    row_count = queries.shape[0]
    heads, entries, width = codebook.shape
    nb = row_count // BLOCK
    parts = BLOCK // TILE
    chunks = row_count // CHUNK
    half = entries // 2
    hbm = pl.BlockSpec(memory_space=pltpu.HBM)
    vmem = pl.BlockSpec(memory_space=pltpu.VMEM)
    dma = pltpu.SemaphoreType.DMA
    halves = pltpu.VMEM((heads, half, width), BF16)
    pieces = pltpu.VMEM((heads, SUBS, half // SUBS, width), BF16)
    counts = pltpu.VMEM((heads, 1, entries), F32)
    results = pl.pallas_call(
        functools.partial(kernel, n_seq, n_head),
        out_shape=(
            jax.ShapeDtypeStruct(queries.shape, BF16),
            jax.ShapeDtypeStruct(queries.shape, BF16),
            jax.ShapeDtypeStruct(codebook.shape, F32),
        ),
        in_specs=[hbm] * 6,
        out_specs=(vmem,) * 3,
        scratch_shapes=[
            pltpu.VMEM(queries.shape, BF16),
            pltpu.VMEM(queries.shape, BF16),
            pltpu.VMEM((heads, row_count), jnp.int32),
            pltpu.VMEM(codebook.shape, BF16),
            pltpu.VMEM(out_weight.shape, BF16),
            pltpu.VMEM((n_head,) + grad_out.shape, BF16),
            pltpu.VMEM(queries.shape, BF16),
            pltpu.VMEM((heads, nb, entries, BLOCK), BF16),
            pltpu.VMEM((heads, nb, BLOCK, entries), BF16),
            pltpu.VMEM((heads, nb, BLOCK, width), BF16),
            pltpu.VMEM((heads, nb, width, BLOCK), BF16),
            pltpu.VMEM((heads, width, entries), BF16),
            pltpu.VMEM((heads, nb, entries, width), F32),
            pltpu.VMEM((heads, nb, 1, entries), F32),
            pltpu.VMEM((heads, nb, 1, entries), F32),
            pltpu.VMEM((heads, nb, entries, width), F32),
            pltpu.VMEM((heads, nb, entries, width), BF16),
            pltpu.VMEM((heads, nb, BLOCK, BLOCK), BF16),
            pltpu.VMEM((heads, nb, entries, BLOCK), BF16),
            pltpu.VMEM((heads, nb, BLOCK, width), F32),
            pltpu.VMEM((heads, nb, entries, width), F32),
            pltpu.VMEM((heads, entries, width), F32),
            pltpu.VMEM((heads, entries, width), F32),
            counts, pltpu.VMEM((n_seq, heads, 1, entries), F32),
            halves, halves, halves, halves, halves, halves,
            halves, halves, halves, halves, halves, halves,
            halves, halves, pieces, pieces, pieces,
            pltpu.VMEM((heads, 2, SUBS, half // SUBS, width), BF16),
            dma((5,)), dma((chunks,)),
            dma((n_head, chunks)), dma((n_head, chunks)),
            dma((n_seq,)), dma((n_seq,)),
        ] + [dma((heads,))] * 14 + [dma((heads, SUBS))] * 8,
        compiler_params=pltpu.CompilerParams(
            collective_id=0, has_side_effects=True, vmem_limit_bytes=50 * 1024 * 1024),
    )(*(pltpu.with_memory_space_constraint(x, pltpu.HBM) for x in (queries, values, codes.T, codebook, out_weight, grad_out)))
    return pl.pallas_call(
        write_out,
        out_shape=tuple(jax.ShapeDtypeStruct(r.shape, r.dtype) for r in results),
        in_specs=[vmem] * 3,
        out_specs=(hbm,) * 3,
        scratch_shapes=[dma((3,))],
        compiler_params=pltpu.CompilerParams(vmem_limit_bytes=1024 * 1024),
    )(*results)


def solution(mesh):
    return jax.shard_map(
        per_device,
        mesh=mesh,
        in_specs=(
            P("seq", "head"),
            P("seq", "head"),
            P("seq", "head"),
            P("head", None, None),
            P("head", None),
            P("seq", "head"),
        ),
        out_specs=(P("seq", "head"), P("seq", "head"), P("head", None, None)),
        check_vma=False,
    )
```

```python
import functools

import jax
import jax.numpy as jnp
from jax import lax
from jax.experimental import pallas as pl
from jax.experimental.pallas import tpu as pltpu
from jax.sharding import PartitionSpec as P

BLOCK = 512
TILE = 256
CHUNK = 128
SUBS = 2
NEG = -1e30
LOG2E = 1.4426950408889634
F32 = jnp.float32
BF16 = jnp.bfloat16
MESH = pl.DeviceIdType.MESH


def nn(a, b):
    return lax.dot_general(a, b, (((1,), (0,)), ((), ())), preferred_element_type=F32)


def nt(a, b):
    return lax.dot_general(a, b, (((1,), (1,)), ((), ())), preferred_element_type=F32)


def kernel(
    n_seq, n_head,
    q_in, v_in, codes_in, cb_in, w_in, go_in,
    gq_ref, gv_ref, gc_ref,
    q_ref, v_ref, codes_ref, cb_ref, w_ref, gath, dout,
    hot_t, hot, keys, keys_t, book_t, own, cnt_block, cnt_pre, cnt_full, cval,
    local_low, cache_low, local_part, vpart, code_acc, later_ref,
    cn_own, cny_in, cnz_out, cnz_in,
    py_out, py_in, pz_out, pz_in, pa_out, pa_in,
    ly_out, ly_in, lz_out, lz_in, la_out, la_in,
    cy_out, cy_in, c_out, c_below, c_above, c_fin,
    load_s, go_s, ag_s, ag_r, ax_r, cny_s, cny_r, cnz_s, cnz_r,
    py_s, py_r, pz_s, pz_r, pa_s, pa_r,
    ly_s, ly_r, lz_s, lz_r, la_s, la_r,
    cy_s, cy_r, c_s, cb_r, cu_r, cp_s, cp_r, fu_s, fd_s, cf_r,
):
    rows_all = q_ref.shape[0]
    heads, entries, width = cb_ref.shape
    nb = rows_all // BLOCK
    parts = BLOCK // TILE
    chunks = rows_all // CHUNK
    per_tile = TILE // CHUNK
    outer = n_seq // 2
    half = entries // 2
    piece = half // SUBS
    center = outer // 2
    scale = width ** (-0.5)
    me = lax.axis_index("seq")
    mine = lax.axis_index("head")
    at = me // 2
    side = me % 2
    partner = me + 1 - 2 * side
    is_hi = side.astype(F32)
    is_lo = 1.0 - is_hi
    own_half = pl.ds(pl.multiple_of(side * half, half), half)
    other_half = pl.ds(pl.multiple_of((1 - side) * half, half), half)
    has_down = at > 0
    has_up = at < outer - 1
    bits = []
    bit = n_head // 2
    while bit >= 1:
        bits.append(bit)
        bit //= 2

    def flip(index, mask):
        for b in bits:
            if mask & b:
                index = index + b - 2 * b * ((index // b) % 2)
        return index

    def go_load(first, last):
        span = pl.ds(first * CHUNK, (last - first) * CHUNK)
        return pltpu.make_async_copy(go_in.at[span], gath.at[mine, span], go_s.at[min(first, 1)])

    loads = [
        pltpu.make_async_copy(src, dst, load_s.at[k])
        for k, (src, dst) in enumerate(
            ((codes_in, codes_ref), (cb_in, cb_ref), (v_in, v_ref), (q_in, q_ref), (w_in, w_ref)))
    ]
    loads[0].start()
    go_load(0, 1).start()
    go_load(1, chunks).start()
    for copy in loads[1:]:
        copy.start()

    barrier = pltpu.get_barrier_semaphore()
    pl.semaphore_signal(barrier, inc=1, device_id={"seq": partner}, device_id_type=MESH)

    @pl.when(has_down)
    def _():
        pl.semaphore_signal(barrier, inc=1, device_id={"seq": me - 2}, device_id_type=MESH)

    @pl.when(has_up)
    def _():
        pl.semaphore_signal(barrier, inc=1, device_id={"seq": me + 2}, device_id_type=MESH)

    for b in bits:
        pl.semaphore_signal(barrier, inc=1, device_id={"head": flip(mine, b)}, device_id_type=MESH)

    loads[0].wait()
    row_at = lax.broadcasted_iota(jnp.int32, (entries, BLOCK), 0)
    lane_at = lax.broadcasted_iota(jnp.int32, (BLOCK, entries), 1)

    def count(h, carry):
        total = jnp.zeros((1, entries), F32)
        for b in range(nb):
            code_row = codes_ref[pl.ds(h, 1), pl.ds(b * BLOCK, BLOCK)]
            code_full = jnp.transpose(jnp.broadcast_to(code_row, (width, BLOCK)))
            code_cols = jnp.concatenate([code_full] * (entries // width), axis=1)
            one_f = (lane_at == code_cols).astype(F32)
            hot[h, b] = one_f.astype(BF16)
            counts = jnp.sum(one_f, axis=0, keepdims=True)
            cnt_block[h, b] = counts
            total += counts
        cn_own[h] = total
        return carry

    lax.fori_loop(0, heads, count, 0)
    pl.semaphore_wait(
        barrier, 1 + len(bits) + jnp.where(has_down, 1, 0) + jnp.where(has_up, 1, 0))

    def gather_copy(src_mask, to, chunk):
        block = flip(mine, src_mask)
        span = pl.ds(chunk * CHUNK, CHUNK)
        slot = src_mask ^ to
        return pltpu.make_async_remote_copy(
            src_ref=gath.at[block, span], dst_ref=gath.at[block, span],
            send_sem=ag_s.at[0], recv_sem=ax_r.at[rank[slot], chunk] if slot in feeds else ag_r.at[rank[slot], chunk // per_tile],
            device_id={"head": flip(mine, to)}, device_id_type=MESH)

    plan = []
    known = [0]
    for b in bits:
        plan += [(m, b) for m in known]
        known += [m ^ b for m in known]
    by_slot = {m ^ b: (m, b) for m, b in plan}
    feeds = {m for m, _ in plan if m != 0}
    rank = {slot: k for k, slot in enumerate(sorted(feeds))}
    rank.update({slot: k for k, slot in enumerate(sorted(set(by_slot) - feeds))})
    for chunk in range(chunks):
        if chunk == 0:
            go_load(0, 1).wait()
        elif chunk == 1:
            go_load(1, chunks).wait()
        for m, b in plan:
            if m == 0 and b == bits[0]:
                gather_copy(m, b, chunk).start()
    for m, b in plan:
        if m == 0 and b != bits[0]:
            for chunk in range(chunks):
                gather_copy(m, b, chunk).start()
    taken = set()

    def tile_copy(slot, start):
        m, b = by_slot[slot]
        block = flip(mine, m)
        span = pl.ds(start, TILE)
        return pltpu.make_async_remote_copy(
            src_ref=gath.at[block, span], dst_ref=gath.at[block, span],
            send_sem=ag_s.at[0], recv_sem=ag_r.at[rank[slot], start // TILE],
            device_id={"head": flip(mine, b)}, device_id_type=MESH)

    def all_sent():
        span = gath.at[pl.ds(0, len(plan))]
        return pltpu.make_async_remote_copy(
            src_ref=span, dst_ref=span, send_sem=ag_s.at[0], recv_sem=ag_r.at[0, 0],
            device_id={"head": flip(mine, bits[0])}, device_id_type=MESH)

    def arrive(slot, chunk):
        if (slot, chunk) not in taken:
            taken.add((slot, chunk))
            m, b = by_slot[slot]
            gather_copy(m, b, chunk).wait_recv()

    def relay(chunk):
        for m, b in plan:
            if m != 0:
                arrive(m, chunk)
                gather_copy(m, b, chunk).start()

    def seq_copy(src, dst, send, recv, to):
        return pltpu.make_async_remote_copy(
            src_ref=src, dst_ref=dst, send_sem=send, recv_sem=recv,
            device_id={"seq": to}, device_id_type=MESH)

    count_pair = seq_copy(cn_own, cny_in, cny_s.at[0], cny_r.at[0], partner)
    count_pair.start()

    def count_hop(to):
        return seq_copy(cnz_out, cnz_in, cnz_s.at[0], cnz_r.at[0], to)

    def take_counts():
        count_pair.wait_recv()

        @pl.when(jnp.logical_not(has_down))
        def _():
            cnz_in[...] = jnp.zeros(cnz_in.shape, F32)

        @pl.when(has_down)
        def _():
            count_hop(me - 2).wait_recv()

        cnz_out[...] = cnz_in[...] + cn_own[...] + cny_in[...]

        @pl.when(has_up)
        def _():
            count_hop(me + 2).start()

        row = cnz_in[...] + cny_in[...] * is_hi
        for b in range(nb):
            cnt_pre[:, b] = row
            row = row + cnt_block[:, b]

    def prefix_pair(h):
        return seq_copy(py_out.at[h], py_in.at[h], py_s.at[0], py_r.at[h], partner)

    def prefix_hop(h, to):
        return seq_copy(pz_out.at[h], pz_in.at[h], pz_s.at[0], pz_r.at[h], to)

    def prefix_back(h):
        return seq_copy(pa_out.at[h], pa_in.at[h], pa_s.at[0], pa_r.at[h], partner)

    loads[1].wait()
    loads[2].wait()

    def sums(h, carry):
        head_lanes = pl.ds(pl.multiple_of(h * width, width), width)
        for b in range(nb):
            rows = pl.ds(b * BLOCK, BLOCK)
            one_t = (row_at == codes_ref[pl.ds(h, 1), rows]).astype(F32).astype(BF16)
            hot_t[h, b] = one_t
            own[h, b] = nn(one_t, v_ref[rows, head_lanes])
        total = own[h, 0, other_half]
        for b in range(1, nb):
            total += own[h, b, other_half]
        py_out[h] = total.astype(BF16)
        prefix_pair(h).start()
        return carry

    lax.fori_loop(0, heads, sums, 0)

    @pl.when(jnp.logical_not(has_down))
    def _():
        take_counts()

    def make_keys(h, carry):
        book = cb_ref[h]
        book_t[h] = jnp.transpose(book.astype(F32)).astype(BF16)
        for b in range(nb):
            key = nn(hot[h, b], book)
            keys[h, b] = key.astype(BF16)
            keys_t[h, b] = jnp.transpose(key).astype(BF16)
        return carry

    lax.fori_loop(0, heads, make_keys, 0)

    def prefix_chain(h):
        prefix_pair(h).wait_recv()

        @pl.when(jnp.logical_not(has_down))
        def _():
            pz_in[h] = jnp.zeros(pz_in.shape[1:], BF16)

        @pl.when(has_down)
        def _():
            prefix_hop(h, me - 2).wait_recv()

        below = pz_in[h].astype(F32)
        pair = py_in[h].astype(F32)
        total = own[h, 0, own_half]
        for b in range(1, nb):
            total += own[h, b, own_half]
        pz_out[h] = (below + total + pair).astype(BF16)

        @pl.when(has_up)
        def _():
            prefix_hop(h, me + 2).start()

        pa_out[h] = (below + total * is_lo).astype(BF16)
        prefix_back(h).start()
        prefix = below + pair * is_hi
        for b in range(nb):
            cval[h, b, own_half] = prefix.astype(BF16)
            prefix = prefix + own[h, b, own_half]

    def prefix_gather(h):
        prefix_back(h).wait_recv()
        prefix = pa_in[h].astype(F32)
        for b in range(nb):
            cval[h, b, other_half] = prefix.astype(BF16)
            prefix = prefix + own[h, b, other_half]

    def softmax(h, b):
        head_lanes = pl.ds(pl.multiple_of(h * width, width), width)
        book = cb_ref[h]
        count_full = jnp.transpose(jnp.broadcast_to(cnt_pre[h, b], (width, entries)))
        cnt_full[h, b] = count_full
        bias_full = jnp.where(count_full > 0.0, 0.0, NEG)
        counts = jnp.concatenate([count_full] * (TILE // width), axis=1)
        bias = jnp.concatenate([bias_full] * (TILE // width), axis=1)
        for p in range(parts):
            seen = (p + 1) * TILE
            query = q_ref[pl.ds(pl.multiple_of(b * BLOCK + p * TILE, TILE), TILE), head_lanes]
            at_u = lax.broadcasted_iota(jnp.int32, (seen, TILE), 0)
            at_t = lax.broadcasted_iota(jnp.int32, (seen, TILE), 1) + p * TILE
            scores = jnp.where(at_u <= at_t, nt(keys[h, b, 0:seen], query) * (scale * LOG2E), NEG)
            cache_scores = nt(book, query) * (scale * LOG2E) + bias
            highest = jnp.maximum(
                jnp.max(scores, axis=0, keepdims=True), jnp.max(cache_scores, axis=0, keepdims=True))
            local_exp = jnp.exp2(scores - highest)
            cache_exp = jnp.exp2(cache_scores - highest)
            total = jnp.sum(local_exp, axis=0, keepdims=True) + jnp.sum(cache_exp * counts, axis=0, keepdims=True)
            inverse = 1.0 / total
            lanes = slice(p * TILE, seen)
            local_low[h, b, 0:seen, lanes] = (local_exp * inverse).astype(BF16)
            if seen < BLOCK:
                local_low[h, b, seen:BLOCK, lanes] = jnp.zeros((BLOCK - seen, TILE), BF16)
            cache_low[h, b, :, lanes] = (cache_exp * inverse).astype(BF16)

    rounds = heads * nb // 2
    turn = 2 * at

    def chain_at(slot):
        h = slot - turn

        @pl.when((h >= 0) & (h < heads))
        def _():
            prefix_chain(h)

    relay_at = {}
    for chunk in range(chunks):
        where = (0, 1, rounds - 1, "mid", "late", rounds, rounds + 2, rounds + heads - 1)[8 * chunk // chunks]
        relay_at.setdefault(where, []).append(chunk)

    def relays(first, last, now):
        for slot, which in relay_at.items():
            if not isinstance(slot, str) and first <= slot < last:
                @pl.when(now == slot - first)
                def _(which=which):
                    for chunk in which:
                        relay(chunk)

    def relay_named(name):
        for chunk in relay_at.get(name, []):
            relay(chunk)

    chain_at(0)

    @pl.when(has_down)
    def _():
        take_counts()

    chain_at(1)
    loads[3].wait()

    def unit(k, carry):
        softmax(2 * k // nb, 2 * k % nb)
        softmax((2 * k + 1) // nb, (2 * k + 1) % nb)
        chain_at(k + 2)
        relays(0, rounds, k)
        return carry

    lax.fori_loop(0, rounds, unit, 0)
    loads[4].wait()

    depth = go_in.shape[1]

    def project(start):
        rows = pl.ds(start, TILE)
        total = nt(gath[0, rows], w_ref[:, 0:depth])
        for k in range(1, n_head):
            total += nt(gath[k, rows], w_ref[:, k * depth:(k + 1) * depth])
        dout[rows] = total.astype(BF16)

    def value_pass(h, b):
        head_lanes = pl.ds(pl.multiple_of(h * width, width), width)
        vpart[h, b] = nn(cache_low[h, b], dout[pl.ds(b * BLOCK, BLOCK), head_lanes])

    def grad_pass(h, b):
        head_lanes = pl.ds(pl.multiple_of(h * width, width), width)
        rows = pl.ds(b * BLOCK, BLOCK)
        query = q_ref[rows, head_lanes]
        grad = dout[rows, head_lanes]
        counts = jnp.concatenate([cnt_full[h, b]] * (BLOCK // width), axis=1)
        local_grad = nt(v_ref[rows, head_lanes], grad)
        cache_grad = nt(cval[h, b], grad)
        local_prob = local_low[h, b].astype(F32)
        cache_prob = cache_low[h, b].astype(F32)
        delta = (jnp.sum(local_prob * local_grad, axis=0, keepdims=True)
                 + jnp.sum(cache_prob * cache_grad, axis=0, keepdims=True))
        local_score_grad = (local_prob * (local_grad - delta) * scale).astype(BF16)
        cache_score_grad = (cache_prob * (cache_grad - delta * counts) * scale).astype(BF16)
        gq_t = nn(keys_t[h, b], local_score_grad) + nn(book_t[h], cache_score_grad)
        gq_ref[rows, head_lanes] = jnp.transpose(gq_t).astype(BF16)
        key_grad = nn(local_score_grad, query).astype(BF16)
        code = nn(hot_t[h, b], key_grad) + nn(cache_score_grad, query)
        local_part[h, b] = nn(local_low[h, b], grad)
        if b == 0:
            code_acc[h] = code
        else:
            code_acc[h] += code

    def later_pair(h):
        return seq_copy(ly_out.at[h], ly_in.at[h], ly_s.at[0], ly_r.at[h], partner)

    def later_hop(h, to):
        return seq_copy(lz_out.at[h], lz_in.at[h], lz_s.at[0], lz_r.at[h], to)

    def later_back(h):
        return seq_copy(la_out.at[h], la_in.at[h], la_s.at[0], la_r.at[h], partner)

    def part_total(h, span):
        total = vpart[h, 0, span]
        for b in range(1, nb):
            total += vpart[h, b, span]
        return total

    def send_later(h):
        ly_out[h] = part_total(h, other_half).astype(BF16)
        later_pair(h).start()

    def later_chain(h):
        later_pair(h).wait_recv()

        @pl.when(jnp.logical_not(has_up))
        def _():
            lz_in[h] = jnp.zeros(lz_in.shape[1:], BF16)

        @pl.when(has_up)
        def _():
            later_hop(h, me + 2).wait_recv()

        above = lz_in[h].astype(F32)
        pair = ly_in[h].astype(F32)
        total = part_total(h, own_half)
        lz_out[h] = (above + total + pair).astype(BF16)

        @pl.when(has_down)
        def _():
            later_hop(h, me - 2).start()

        la_out[h] = (above + total * is_hi).astype(BF16)
        later_ref[h, own_half] = above + pair * is_lo

    def later_gather(h):
        later_back(h).wait_recv()
        later_ref[h, other_half] = la_in[h].astype(F32)
        head_lanes = pl.ds(pl.multiple_of(h * width, width), width)
        later = later_ref[h]
        for b in reversed(range(nb)):
            rows = pl.ds(b * BLOCK, BLOCK)
            lookup = nn(hot[h, b], later.astype(BF16))
            gv_ref[rows, head_lanes] = (local_part[h, b] + lookup).astype(BF16)
            later = later + vpart[h, b]

    def code_pair(h):
        return seq_copy(cy_out.at[h], cy_in.at[h], cy_s.at[0], cy_r.at[h], partner)

    def code_up(h, s):
        return seq_copy(c_out.at[h, s], c_below.at[h, s], c_s.at[0], cb_r.at[h, s], me + 2)

    def code_down(h, s):
        return seq_copy(c_out.at[h, s], c_above.at[h, s], c_s.at[0], cu_r.at[h, s], me - 2)

    def fin_up(h, s):
        return seq_copy(c_fin.at[side, h, s], c_fin.at[side, h, s], fu_s.at[0], cf_r.at[h, s], me + 2)

    def fin_down(h, s):
        return seq_copy(c_fin.at[side, h, s], c_fin.at[side, h, s], fd_s.at[0], cf_r.at[h, s], me - 2)

    def fin_pair(h, which, s):
        return seq_copy(c_fin.at[which, h, s], c_fin.at[which, h, s], cp_s.at[0], cp_r.at[h, s], partner)

    def send_code(h):
        cy_out[h] = code_acc[h, other_half].astype(BF16)
        code_pair(h).start()

    def piece_of(which, s):
        return pl.ds(pl.multiple_of(which * half + s * piece, piece), piece)

    def reduce_code(h):
        code_pair(h).wait_recv()
        code_acc[h, own_half] += cy_in[h].astype(F32)
        for s in range(SUBS):
            span = piece_of(side, s)

            @pl.when((at <= center) & has_down)
            def _(s=s, span=span):
                code_up(h, s).wait_recv()
                code_acc[h, span] += c_below[h, s].astype(F32)

            @pl.when((at >= center) & has_up)
            def _(s=s, span=span):
                code_down(h, s).wait_recv()
                code_acc[h, span] += c_above[h, s].astype(F32)

            c_out[h, s] = code_acc[h, span].astype(BF16)

            @pl.when(at < center)
            def _(s=s):
                code_up(h, s).start()

            @pl.when(at > center)
            def _(s=s):
                code_down(h, s).start()

    def spread_code(h):
        for s in range(SUBS):
            @pl.when(at == center)
            def _(s=s):
                c_fin[side, h, s] = c_out[h, s]

            @pl.when(at != center)
            def _(s=s):
                fin_up(h, s).wait_recv()

            @pl.when((at <= center) & has_down)
            def _(s=s):
                fin_down(h, s).start()

            @pl.when((at >= center) & has_up)
            def _(s=s):
                fin_up(h, s).start()

            fin_pair(h, side, s).start()
            gc_ref[h, piece_of(side, s)] = c_fin[side, h, s].astype(F32)

    def last_code(h):
        for s in range(SUBS):
            fin_pair(h, 1 - side, s).wait_recv()
            gc_ref[h, piece_of(1 - side, s)] = c_fin[1 - side, h, s].astype(F32)

    for b in range(nb):
        final = b == nb - 1
        for part in range(parts):
            start = b * BLOCK + part * TILE
            for slot in by_slot:
                if slot in feeds:
                    for chunk in range(start // CHUNK, (start + TILE) // CHUNK):
                        arrive(slot, chunk)
                else:
                    tile_copy(slot, start).wait_recv()
            project(start)
            if b == 0:
                if part == 0:
                    relay_named("mid")
                chain_at(rounds + 2 + part)
        def values(h, carry, b=b, final=final):
            value_pass(h, b)
            if final:
                send_later(h)
            return carry

        lax.fori_loop(0, heads, values, 0)
        if b == 0:
            relay_named("late")

            def rest(h, carry):
                @pl.when(turn + h >= rounds + 2 + parts)
                def _():
                    prefix_chain(h)

                return carry

            lax.fori_loop(0, heads, rest, 0)

        def grads(h, carry, b=b, final=final):
            if b == 0:
                prefix_gather(h)
            grad_pass(h, b)
            if b == 0:
                relays(rounds, rounds + heads, h)
            if final:
                send_code(h)

                @pl.when(jnp.logical_not(has_up) & (h >= 1))
                def _():
                    later_chain(h - 1)

            return carry

        lax.fori_loop(0, heads, grads, 0)

    behind = outer - 1 - at
    soon = behind * 2 < outer

    @pl.when(behind == 0)
    def _():
        later_chain(heads - 1)

    def chain_step(h, carry):
        @pl.when(soon & (behind > 0))
        def _():
            later_chain(h)

        return carry

    lax.fori_loop(0, heads, chain_step, 0)

    @pl.when(soon & (behind > 0))
    def _():
        for h in range(heads):
            later_back(h).start()

    def reduce_step(h, carry):
        reduce_code(h)

        @pl.when(at == center)
        def _():
            spread_code(h)

        @pl.when(jnp.logical_not(soon) & has_down & (h == 1))
        def _():
            later_chain(h - 1)
            later_back(h - 1).start()

        return carry

    lax.fori_loop(0, heads, reduce_step, 0)

    def back_step(h, carry):
        @pl.when(jnp.logical_not(soon | (has_down & (h == 0))))
        def _():
            later_chain(h)

        @pl.when((behind == 0) | jnp.logical_not(soon | (has_down & (h == 0))))
        def _():
            later_back(h).start()

        return carry

    lax.fori_loop(0, heads, back_step, 0)

    def sent(ref, sem):
        return seq_copy(ref, ref, sem.at[0], sem.at[0], partner)

    sent(py_out, py_s).wait_send()
    sent(pa_out, pa_s).wait_send()

    @pl.when(has_up)
    def _():
        sent(pz_out, pz_s).wait_send()

    count_pair.wait_send()

    @pl.when(has_up)
    def _():
        count_hop(me + 2).wait_send()

    all_sent().wait_send()

    quiet = (at == center) | jnp.logical_not(has_down & has_up)

    def spread_step(h, carry):
        @pl.when(at != center)
        def _():
            spread_code(h)

        @pl.when(quiet)
        def _():
            later_gather(h)

        return carry

    lax.fori_loop(0, heads, spread_step, 0)

    def last_step(h, carry):
        @pl.when(jnp.logical_not(quiet))
        def _():
            later_gather(h)

        last_code(h)
        return carry

    lax.fori_loop(0, heads, last_step, 0)
    sent(ly_out, ly_s).wait_send()
    sent(la_out, la_s).wait_send()
    sent(cy_out, cy_s).wait_send()
    sent(c_fin.at[side], cp_s).wait_send()

    @pl.when(has_down)
    def _():
        sent(lz_out, lz_s).wait_send()

    @pl.when(at != center)
    def _():
        sent(c_out, c_s).wait_send()

    @pl.when((at <= center) & has_down)
    def _():
        sent(c_fin.at[side], fd_s).wait_send()

    @pl.when((at >= center) & has_up)
    def _():
        sent(c_fin.at[side], fu_s).wait_send()


def write_out(*refs):
    sems = refs[-1]
    copies = [pltpu.make_async_copy(refs[k], refs[k + 3], sems.at[k]) for k in range(3)]
    for copy in copies:
        copy.start()
    for copy in copies:
        copy.wait()


def per_device(queries, values, codes, codebook, out_weight, grad_out):
    n_seq, n_head = lax.axis_size("seq"), lax.axis_size("head")
    row_count = queries.shape[0]
    heads, entries, width = codebook.shape
    nb = row_count // BLOCK
    parts = BLOCK // TILE
    chunks = row_count // CHUNK
    half = entries // 2
    hbm = pl.BlockSpec(memory_space=pltpu.HBM)
    vmem = pl.BlockSpec(memory_space=pltpu.VMEM)
    dma = pltpu.SemaphoreType.DMA
    halves = pltpu.VMEM((heads, half, width), BF16)
    pieces = pltpu.VMEM((heads, SUBS, half // SUBS, width), BF16)
    counts = pltpu.VMEM((heads, 1, entries), F32)
    results = pl.pallas_call(
        functools.partial(kernel, n_seq, n_head),
        out_shape=(
            jax.ShapeDtypeStruct(queries.shape, BF16),
            jax.ShapeDtypeStruct(queries.shape, BF16),
            jax.ShapeDtypeStruct(codebook.shape, F32),
        ),
        in_specs=[hbm] * 6,
        out_specs=(vmem,) * 3,
        scratch_shapes=[
            pltpu.VMEM(queries.shape, BF16),
            pltpu.VMEM(queries.shape, BF16),
            pltpu.VMEM((heads, row_count), jnp.int32),
            pltpu.VMEM(codebook.shape, BF16),
            pltpu.VMEM(out_weight.shape, BF16),
            pltpu.VMEM((n_head,) + grad_out.shape, BF16),
            pltpu.VMEM(queries.shape, BF16),
            pltpu.VMEM((heads, nb, entries, BLOCK), BF16),
            pltpu.VMEM((heads, nb, BLOCK, entries), BF16),
            pltpu.VMEM((heads, nb, BLOCK, width), BF16),
            pltpu.VMEM((heads, nb, width, BLOCK), BF16),
            pltpu.VMEM((heads, width, entries), BF16),
            pltpu.VMEM((heads, nb, entries, width), F32),
            pltpu.VMEM((heads, nb, 1, entries), F32),
            pltpu.VMEM((heads, nb, 1, entries), F32),
            pltpu.VMEM((heads, nb, entries, width), F32),
            pltpu.VMEM((heads, nb, entries, width), BF16),
            pltpu.VMEM((heads, nb, BLOCK, BLOCK), BF16),
            pltpu.VMEM((heads, nb, entries, BLOCK), BF16),
            pltpu.VMEM((heads, nb, BLOCK, width), F32),
            pltpu.VMEM((heads, nb, entries, width), F32),
            pltpu.VMEM((heads, entries, width), F32),
            pltpu.VMEM((heads, entries, width), F32),
            counts, counts, counts, counts,
            halves, halves, halves, halves, halves, halves,
            halves, halves, halves, halves, halves, halves,
            halves, halves, pieces, pieces, pieces,
            pltpu.VMEM((2, heads, SUBS, half // SUBS, width), BF16),
            dma((5,)), dma((2,)),
            dma((1,)), dma((n_head // 2, row_count // TILE)), dma((max(n_head // 2 - 1, 1), chunks)),
            dma((1,)), dma((1,)), dma((1,)), dma((1,)),
        ] + [dma((1,)), dma((heads,))] * 7 + [
            dma((1,)), dma((heads, SUBS)), dma((heads, SUBS)), dma((1,)), dma((heads, SUBS)),
            dma((1,)), dma((1,)), dma((heads, SUBS)),
        ],
        compiler_params=pltpu.CompilerParams(
            collective_id=0, has_side_effects=True, vmem_limit_bytes=50 * 1024 * 1024),
    )(*(pltpu.with_memory_space_constraint(x, pltpu.HBM) for x in (queries, values, codes.T, codebook, out_weight, grad_out)))
    return pl.pallas_call(
        write_out,
        out_shape=tuple(jax.ShapeDtypeStruct(r.shape, r.dtype) for r in results),
        in_specs=[vmem] * 3,
        out_specs=(hbm,) * 3,
        scratch_shapes=[dma((3,))],
        compiler_params=pltpu.CompilerParams(vmem_limit_bytes=1024 * 1024),
    )(*results)


def solution(mesh):
    return jax.shard_map(
        per_device,
        mesh=mesh,
        in_specs=(
            P("seq", "head"),
            P("seq", "head"),
            P("seq", "head"),
            P("head", None, None),
            P("head", None),
            P("seq", "head"),
        ),
        out_specs=(P("seq", "head"), P("seq", "head"), P("head", None, None)),
        check_vma=False,
    )
```

```python
import functools

import jax
import jax.numpy as jnp
from jax import lax
from jax.experimental import pallas as pl
from jax.experimental.pallas import tpu as pltpu
from jax.sharding import PartitionSpec as P

BLOCK = 512
TILE = 256
CHUNK = 128
SUBS = 2
NEG = -1e30
LOG2E = 1.4426950408889634
F32 = jnp.float32
BF16 = jnp.bfloat16
MESH = pl.DeviceIdType.MESH


def nn(a, b):
    return lax.dot_general(a, b, (((1,), (0,)), ((), ())), preferred_element_type=F32)


def nt(a, b):
    return lax.dot_general(a, b, (((1,), (1,)), ((), ())), preferred_element_type=F32)


def kernel(
    n_seq, n_head,
    q_in, v_in, codes_in, cb_in, w_in, go_in,
    gq_ref, gv_ref, gc_ref,
    q_ref, v_ref, codes_ref, cb_ref, w_ref, gath, dout,
    hot_t, hot, keys, keys_t, book_t, own, cnt_block, cnt_pre, cnt_full, cval,
    local_low, cache_low, local_part, vpart, code_acc, later_ref,
    cn_own, cny_in, cnz_out, cnz_in,
    py_out, py_in, pz_out, pz_in, pa_out, pa_in,
    ly_out, ly_in, lz_out, lz_in, la_out, la_in,
    cy_out, cy_in, c_out, c_below, c_above, c_fin,
    load_s, go_s, ag_s, ag_r, ax_r, cny_s, cny_r, cnz_s, cnz_r,
    py_s, py_r, pz_s, pz_r, pa_s, pa_r,
    ly_s, ly_r, lz_s, lz_r, la_s, la_r,
    cy_s, cy_r, c_s, cb_r, cu_r, cp_s, cp_r, fu_s, fd_s, cf_r,
):
    rows_all = q_ref.shape[0]
    heads, entries, width = cb_ref.shape
    nb = rows_all // BLOCK
    parts = BLOCK // TILE
    chunks = rows_all // CHUNK
    per_tile = TILE // CHUNK
    outer = n_seq // 2
    half = entries // 2
    piece = half // SUBS
    center = outer // 2
    scale = width ** (-0.5)
    me = lax.axis_index("seq")
    mine = lax.axis_index("head")
    at = me // 2
    side = me % 2
    partner = me + 1 - 2 * side
    is_hi = side.astype(F32)
    is_lo = 1.0 - is_hi
    own_half = pl.ds(pl.multiple_of(side * half, half), half)
    other_half = pl.ds(pl.multiple_of((1 - side) * half, half), half)
    has_down = at > 0
    has_up = at < outer - 1
    bits = []
    bit = n_head // 2
    while bit >= 1:
        bits.append(bit)
        bit //= 2

    def flip(index, mask):
        for b in bits:
            if mask & b:
                index = index + b - 2 * b * ((index // b) % 2)
        return index

    def go_load(first, last):
        span = pl.ds(first * CHUNK, (last - first) * CHUNK)
        return pltpu.make_async_copy(go_in.at[span], gath.at[mine, span], go_s.at[min(first, 1)])

    loads = [
        pltpu.make_async_copy(src, dst, load_s.at[k])
        for k, (src, dst) in enumerate(
            ((codes_in, codes_ref), (cb_in, cb_ref), (v_in, v_ref), (q_in, q_ref), (w_in, w_ref)))
    ]
    loads[0].start()
    go_load(0, 1).start()
    go_load(1, chunks).start()
    for copy in loads[1:]:
        copy.start()

    barrier = pltpu.get_barrier_semaphore()
    pl.semaphore_signal(barrier, inc=1, device_id={"seq": partner}, device_id_type=MESH)

    @pl.when(has_down)
    def _():
        pl.semaphore_signal(barrier, inc=1, device_id={"seq": me - 2}, device_id_type=MESH)

    @pl.when(has_up)
    def _():
        pl.semaphore_signal(barrier, inc=1, device_id={"seq": me + 2}, device_id_type=MESH)

    for b in bits:
        pl.semaphore_signal(barrier, inc=1, device_id={"head": flip(mine, b)}, device_id_type=MESH)

    loads[0].wait()
    row_at = lax.broadcasted_iota(jnp.int32, (entries, BLOCK), 0)
    lane_at = lax.broadcasted_iota(jnp.int32, (BLOCK, entries), 1)

    def count(h, carry):
        total = jnp.zeros((1, entries), F32)
        for b in range(nb):
            code_row = codes_ref[pl.ds(h, 1), pl.ds(b * BLOCK, BLOCK)]
            code_full = jnp.transpose(jnp.broadcast_to(code_row, (width, BLOCK)))
            code_cols = jnp.concatenate([code_full] * (entries // width), axis=1)
            one_f = (lane_at == code_cols).astype(F32)
            hot[h, b] = one_f.astype(BF16)
            counts = jnp.sum(one_f, axis=0, keepdims=True)
            cnt_block[h, b] = counts
            total += counts
        cn_own[h] = total
        return carry

    lax.fori_loop(0, heads, count, 0)
    pl.semaphore_wait(
        barrier, 1 + len(bits) + jnp.where(has_down, 1, 0) + jnp.where(has_up, 1, 0))

    def gather_copy(src_mask, to, chunk):
        block = flip(mine, src_mask)
        span = pl.ds(chunk * CHUNK, CHUNK)
        slot = src_mask ^ to
        return pltpu.make_async_remote_copy(
            src_ref=gath.at[block, span], dst_ref=gath.at[block, span],
            send_sem=ag_s.at[0], recv_sem=ax_r.at[rank[slot], chunk] if slot in feeds else ag_r.at[rank[slot], chunk // per_tile],
            device_id={"head": flip(mine, to)}, device_id_type=MESH)

    plan = []
    known = [0]
    for b in bits:
        plan += [(m, b) for m in known]
        known += [m ^ b for m in known]
    by_slot = {m ^ b: (m, b) for m, b in plan}
    feeds = {m for m, _ in plan if m != 0}
    rank = {slot: k for k, slot in enumerate(sorted(feeds))}
    rank.update({slot: k for k, slot in enumerate(sorted(set(by_slot) - feeds))})
    for chunk in range(chunks):
        if chunk == 0:
            go_load(0, 1).wait()
        elif chunk == 1:
            go_load(1, chunks).wait()
        for m, b in plan:
            if m == 0 and b == bits[0]:
                gather_copy(m, b, chunk).start()
    for m, b in plan:
        if m == 0 and b != bits[0]:
            for chunk in range(chunks):
                gather_copy(m, b, chunk).start()
    taken = set()

    def tile_copy(slot, start):
        m, b = by_slot[slot]
        block = flip(mine, m)
        span = pl.ds(start, TILE)
        return pltpu.make_async_remote_copy(
            src_ref=gath.at[block, span], dst_ref=gath.at[block, span],
            send_sem=ag_s.at[0], recv_sem=ag_r.at[rank[slot], start // TILE],
            device_id={"head": flip(mine, b)}, device_id_type=MESH)

    def all_sent():
        span = gath.at[pl.ds(0, len(plan))]
        return pltpu.make_async_remote_copy(
            src_ref=span, dst_ref=span, send_sem=ag_s.at[0], recv_sem=ag_r.at[0, 0],
            device_id={"head": flip(mine, bits[0])}, device_id_type=MESH)

    def arrive(slot, chunk):
        if (slot, chunk) not in taken:
            taken.add((slot, chunk))
            m, b = by_slot[slot]
            gather_copy(m, b, chunk).wait_recv()

    def relay(chunk):
        for m, b in plan:
            if m != 0:
                arrive(m, chunk)
                gather_copy(m, b, chunk).start()

    def seq_copy(src, dst, send, recv, to):
        return pltpu.make_async_remote_copy(
            src_ref=src, dst_ref=dst, send_sem=send, recv_sem=recv,
            device_id={"seq": to}, device_id_type=MESH)

    count_pair = seq_copy(cn_own, cny_in, cny_s.at[0], cny_r.at[0], partner)
    count_pair.start()

    def count_hop(to):
        return seq_copy(cnz_out, cnz_in, cnz_s.at[0], cnz_r.at[0], to)

    def take_counts():
        count_pair.wait_recv()

        @pl.when(jnp.logical_not(has_down))
        def _():
            cnz_in[...] = jnp.zeros(cnz_in.shape, F32)

        @pl.when(has_down)
        def _():
            count_hop(me - 2).wait_recv()

        cnz_out[...] = cnz_in[...] + cn_own[...] + cny_in[...]

        @pl.when(has_up)
        def _():
            count_hop(me + 2).start()

        row = cnz_in[...] + cny_in[...] * is_hi
        for b in range(nb):
            cnt_pre[:, b] = row
            row = row + cnt_block[:, b]

    def prefix_pair(h):
        return seq_copy(py_out.at[h], py_in.at[h], py_s.at[0], py_r.at[h], partner)

    def prefix_hop(h, to):
        return seq_copy(pz_out.at[h], pz_in.at[h], pz_s.at[0], pz_r.at[h], to)

    def prefix_back(h):
        return seq_copy(pa_out.at[h], pa_in.at[h], pa_s.at[0], pa_r.at[h], partner)

    loads[1].wait()
    loads[2].wait()

    def sums(h, carry):
        head_lanes = pl.ds(pl.multiple_of(h * width, width), width)
        for b in range(nb):
            rows = pl.ds(b * BLOCK, BLOCK)
            one_t = (row_at == codes_ref[pl.ds(h, 1), rows]).astype(F32).astype(BF16)
            hot_t[h, b] = one_t
            own[h, b] = nn(one_t, v_ref[rows, head_lanes])
        total = own[h, 0, other_half]
        for b in range(1, nb):
            total += own[h, b, other_half]
        py_out[h] = total.astype(BF16)
        prefix_pair(h).start()
        return carry

    lax.fori_loop(0, heads, sums, 0)

    @pl.when(jnp.logical_not(has_down))
    def _():
        take_counts()

    def make_keys(h, carry):
        book = cb_ref[h]
        book_t[h] = jnp.transpose(book.astype(F32)).astype(BF16)
        for b in range(nb):
            key = nn(hot[h, b], book)
            keys[h, b] = key.astype(BF16)
            keys_t[h, b] = jnp.transpose(key).astype(BF16)
        return carry

    lax.fori_loop(0, heads, make_keys, 0)

    def prefix_chain(h):
        prefix_pair(h).wait_recv()

        @pl.when(jnp.logical_not(has_down))
        def _():
            pz_in[h] = jnp.zeros(pz_in.shape[1:], BF16)

        @pl.when(has_down)
        def _():
            prefix_hop(h, me - 2).wait_recv()

        below = pz_in[h].astype(F32)
        pair = py_in[h].astype(F32)
        total = own[h, 0, own_half]
        for b in range(1, nb):
            total += own[h, b, own_half]
        pz_out[h] = (below + total + pair).astype(BF16)

        @pl.when(has_up)
        def _():
            prefix_hop(h, me + 2).start()

        pa_out[h] = (below + total * is_lo).astype(BF16)
        prefix_back(h).start()
        prefix = below + pair * is_hi
        for b in range(nb):
            cval[h, b, own_half] = prefix.astype(BF16)
            prefix = prefix + own[h, b, own_half]

    def prefix_gather(h):
        prefix_back(h).wait_recv()
        prefix = pa_in[h].astype(F32)
        for b in range(nb):
            cval[h, b, other_half] = prefix.astype(BF16)
            prefix = prefix + own[h, b, other_half]

    def softmax(h, b):
        head_lanes = pl.ds(pl.multiple_of(h * width, width), width)
        book = cb_ref[h]
        count_full = jnp.transpose(jnp.broadcast_to(cnt_pre[h, b], (width, entries)))
        cnt_full[h, b] = count_full
        bias_full = jnp.where(count_full > 0.0, 0.0, NEG)
        counts = jnp.concatenate([count_full] * (TILE // width), axis=1)
        bias = jnp.concatenate([bias_full] * (TILE // width), axis=1)
        for p in range(parts):
            seen = (p + 1) * TILE
            query = q_ref[pl.ds(pl.multiple_of(b * BLOCK + p * TILE, TILE), TILE), head_lanes]
            at_u = lax.broadcasted_iota(jnp.int32, (seen, TILE), 0)
            at_t = lax.broadcasted_iota(jnp.int32, (seen, TILE), 1) + p * TILE
            scores = jnp.where(at_u <= at_t, nt(keys[h, b, 0:seen], query) * (scale * LOG2E), NEG)
            cache_scores = nt(book, query) * (scale * LOG2E) + bias
            highest = jnp.maximum(
                jnp.max(scores, axis=0, keepdims=True), jnp.max(cache_scores, axis=0, keepdims=True))
            local_exp = jnp.exp2(scores - highest)
            cache_exp = jnp.exp2(cache_scores - highest)
            total = jnp.sum(local_exp, axis=0, keepdims=True) + jnp.sum(cache_exp * counts, axis=0, keepdims=True)
            inverse = 1.0 / total
            lanes = slice(p * TILE, seen)
            local_low[h, b, 0:seen, lanes] = (local_exp * inverse).astype(BF16)
            if seen < BLOCK:
                local_low[h, b, seen:BLOCK, lanes] = jnp.zeros((BLOCK - seen, TILE), BF16)
            cache_low[h, b, :, lanes] = (cache_exp * inverse).astype(BF16)

    rounds = heads * nb // 2
    turn = 2 * at

    def chain_at(slot):
        h = slot - turn

        @pl.when((h >= 0) & (h < heads))
        def _():
            prefix_chain(h)

    relay_at = {}
    for chunk in range(chunks):
        where = (0, 1, rounds - 1, "mid", "late", rounds, rounds + 2, rounds + heads - 1)[8 * chunk // chunks]
        relay_at.setdefault(where, []).append(chunk)

    def relays(first, last, now):
        for slot, which in relay_at.items():
            if not isinstance(slot, str) and first <= slot < last:
                @pl.when(now == slot - first)
                def _(which=which):
                    for chunk in which:
                        relay(chunk)

    def relay_named(name):
        for chunk in relay_at.get(name, []):
            relay(chunk)

    chain_at(0)

    @pl.when(has_down)
    def _():
        take_counts()

    chain_at(1)
    loads[3].wait()

    def unit(k, carry):
        softmax(2 * k // nb, 2 * k % nb)
        softmax((2 * k + 1) // nb, (2 * k + 1) % nb)
        chain_at(k + 2)
        relays(0, rounds, k)
        return carry

    lax.fori_loop(0, rounds, unit, 0)
    loads[4].wait()

    depth = go_in.shape[1]

    def project(start):
        rows = pl.ds(start, TILE)
        total = nt(gath[0, rows], w_ref[:, 0:depth])
        for k in range(1, n_head):
            total += nt(gath[k, rows], w_ref[:, k * depth:(k + 1) * depth])
        dout[rows] = total.astype(BF16)

    def value_pass(h, b):
        head_lanes = pl.ds(pl.multiple_of(h * width, width), width)
        vpart[h, b] = nn(cache_low[h, b], dout[pl.ds(b * BLOCK, BLOCK), head_lanes])

    def grad_pass(h, b):
        head_lanes = pl.ds(pl.multiple_of(h * width, width), width)
        rows = pl.ds(b * BLOCK, BLOCK)
        query = q_ref[rows, head_lanes]
        grad = dout[rows, head_lanes]
        counts = jnp.concatenate([cnt_full[h, b]] * (BLOCK // width), axis=1)
        local_grad = nt(v_ref[rows, head_lanes], grad)
        cache_grad = nt(cval[h, b], grad)
        local_prob = local_low[h, b].astype(F32)
        cache_prob = cache_low[h, b].astype(F32)
        delta = (jnp.sum(local_prob * local_grad, axis=0, keepdims=True)
                 + jnp.sum(cache_prob * cache_grad, axis=0, keepdims=True))
        local_score_grad = (local_prob * (local_grad - delta) * scale).astype(BF16)
        cache_score_grad = (cache_prob * (cache_grad - delta * counts) * scale).astype(BF16)
        gq_t = nn(keys_t[h, b], local_score_grad) + nn(book_t[h], cache_score_grad)
        gq_ref[rows, head_lanes] = jnp.transpose(gq_t).astype(BF16)
        key_grad = nn(local_score_grad, query).astype(BF16)
        code = nn(hot_t[h, b], key_grad) + nn(cache_score_grad, query)
        local_part[h, b] = nn(local_low[h, b], grad)
        if b == 0:
            code_acc[h] = code
        else:
            code_acc[h] += code

    def later_pair(h):
        return seq_copy(ly_out.at[h], ly_in.at[h], ly_s.at[0], ly_r.at[h], partner)

    def later_hop(h, to):
        return seq_copy(lz_out.at[h], lz_in.at[h], lz_s.at[0], lz_r.at[h], to)

    def later_back(h):
        return seq_copy(la_out.at[h], la_in.at[h], la_s.at[0], la_r.at[h], partner)

    def part_total(h, span):
        total = vpart[h, 0, span]
        for b in range(1, nb):
            total += vpart[h, b, span]
        return total

    def send_later(h):
        ly_out[h] = part_total(h, other_half).astype(BF16)
        later_pair(h).start()

    def later_chain(h):
        later_pair(h).wait_recv()

        @pl.when(jnp.logical_not(has_up))
        def _():
            lz_in[h] = jnp.zeros(lz_in.shape[1:], BF16)

        @pl.when(has_up)
        def _():
            later_hop(h, me + 2).wait_recv()

        above = lz_in[h].astype(F32)
        pair = ly_in[h].astype(F32)
        total = part_total(h, own_half)
        lz_out[h] = (above + total + pair).astype(BF16)

        @pl.when(has_down)
        def _():
            later_hop(h, me - 2).start()

        la_out[h] = (above + total * is_hi).astype(BF16)
        later_ref[h, own_half] = above + pair * is_lo

    def later_gather(h):
        later_back(h).wait_recv()
        later_ref[h, other_half] = la_in[h].astype(F32)
        head_lanes = pl.ds(pl.multiple_of(h * width, width), width)
        later = later_ref[h]
        for b in reversed(range(nb)):
            rows = pl.ds(b * BLOCK, BLOCK)
            lookup = nn(hot[h, b], later.astype(BF16))
            gv_ref[rows, head_lanes] = (local_part[h, b] + lookup).astype(BF16)
            later = later + vpart[h, b]

    def code_pair(h):
        return seq_copy(cy_out.at[h], cy_in.at[h], cy_s.at[0], cy_r.at[h], partner)

    def code_up(h, s):
        return seq_copy(c_out.at[h, s], c_below.at[h, s], c_s.at[0], cb_r.at[h, s], me + 2)

    def code_down(h, s):
        return seq_copy(c_out.at[h, s], c_above.at[h, s], c_s.at[0], cu_r.at[h, s], me - 2)

    def fin_up(h, s):
        return seq_copy(c_fin.at[side, h, s], c_fin.at[side, h, s], fu_s.at[0], cf_r.at[h, s], me + 2)

    def fin_down(h, s):
        return seq_copy(c_fin.at[side, h, s], c_fin.at[side, h, s], fd_s.at[0], cf_r.at[h, s], me - 2)

    def fin_pair(h, which, s):
        return seq_copy(c_fin.at[which, h, s], c_fin.at[which, h, s], cp_s.at[0], cp_r.at[h, s], partner)

    def send_code(h):
        cy_out[h] = code_acc[h, other_half].astype(BF16)
        code_pair(h).start()

    def piece_of(which, s):
        return pl.ds(pl.multiple_of(which * half + s * piece, piece), piece)

    def reduce_code(h):
        code_pair(h).wait_recv()
        code_acc[h, own_half] += cy_in[h].astype(F32)
        for s in range(SUBS):
            span = piece_of(side, s)

            @pl.when((at <= center) & has_down)
            def _(s=s, span=span):
                code_up(h, s).wait_recv()
                code_acc[h, span] += c_below[h, s].astype(F32)

            @pl.when((at >= center) & has_up)
            def _(s=s, span=span):
                code_down(h, s).wait_recv()
                code_acc[h, span] += c_above[h, s].astype(F32)

            c_out[h, s] = code_acc[h, span].astype(BF16)

            @pl.when(at < center)
            def _(s=s):
                code_up(h, s).start()

            @pl.when(at > center)
            def _(s=s):
                code_down(h, s).start()

    def spread_code(h):
        for s in range(SUBS):
            @pl.when(at == center)
            def _(s=s):
                c_fin[side, h, s] = c_out[h, s]

            @pl.when(at != center)
            def _(s=s):
                fin_up(h, s).wait_recv()

            @pl.when((at <= center) & has_down)
            def _(s=s):
                fin_down(h, s).start()

            @pl.when((at >= center) & has_up)
            def _(s=s):
                fin_up(h, s).start()

            fin_pair(h, side, s).start()
            gc_ref[h, piece_of(side, s)] = c_fin[side, h, s].astype(F32)

    def last_code(h):
        for s in range(SUBS):
            fin_pair(h, 1 - side, s).wait_recv()
            gc_ref[h, piece_of(1 - side, s)] = c_fin[1 - side, h, s].astype(F32)

    for b in range(nb):
        final = b == nb - 1
        for part in range(parts):
            start = b * BLOCK + part * TILE
            for slot in by_slot:
                if slot in feeds:
                    for chunk in range(start // CHUNK, (start + TILE) // CHUNK):
                        arrive(slot, chunk)
                else:
                    tile_copy(slot, start).wait_recv()
            project(start)
            if b == 0:
                if part == 0:
                    relay_named("mid")
                chain_at(rounds + 2 + part)
        def values(h, carry, b=b, final=final):
            value_pass(h, b)
            if final:
                @pl.when(has_down)
                def _():
                    send_later(h)

            return carry

        lax.fori_loop(0, heads, values, 0)
        if b == 0:
            relay_named("late")

            def rest(h, carry):
                @pl.when(turn + h >= rounds + 2 + parts)
                def _():
                    prefix_chain(h)

                return carry

            lax.fori_loop(0, heads, rest, 0)

        def grads(h, carry, b=b, final=final):
            if b == 0:
                prefix_gather(h)
            grad_pass(h, b)
            if b == 0:
                relays(rounds, rounds + heads, h)
            if final:
                send_code(h)

                @pl.when(jnp.logical_not(has_up))
                def _():
                    later_chain(h)

            return carry

        lax.fori_loop(0, heads, grads, 0)

    def send_rest(h, carry):
        @pl.when(jnp.logical_not(has_down))
        def _():
            send_later(h)

        return carry

    lax.fori_loop(0, heads, send_rest, 0)

    behind = outer - 1 - at
    soon = behind * 2 < outer

    def chain_step(h, carry):
        @pl.when(soon & (behind > 0))
        def _():
            later_chain(h)

        return carry

    lax.fori_loop(0, heads, chain_step, 0)

    @pl.when(soon & (behind > 0))
    def _():
        for h in range(heads):
            later_back(h).start()

    def reduce_step(h, carry):
        reduce_code(h)

        @pl.when(at == center)
        def _():
            spread_code(h)

        @pl.when(jnp.logical_not(soon) & has_down & (h == 1))
        def _():
            later_chain(h - 1)
            later_back(h - 1).start()

        return carry

    lax.fori_loop(0, heads, reduce_step, 0)

    def back_step(h, carry):
        @pl.when(jnp.logical_not(soon | (has_down & (h == 0))))
        def _():
            later_chain(h)

        @pl.when((behind == 0) | jnp.logical_not(soon | (has_down & (h == 0))))
        def _():
            later_back(h).start()

        return carry

    lax.fori_loop(0, heads, back_step, 0)

    def sent(ref, sem):
        return seq_copy(ref, ref, sem.at[0], sem.at[0], partner)

    sent(py_out, py_s).wait_send()
    sent(pa_out, pa_s).wait_send()

    @pl.when(has_up)
    def _():
        sent(pz_out, pz_s).wait_send()

    count_pair.wait_send()

    @pl.when(has_up)
    def _():
        count_hop(me + 2).wait_send()

    all_sent().wait_send()

    quiet = (at == center) | jnp.logical_not(has_down & has_up)

    def spread_step(h, carry):
        @pl.when(at != center)
        def _():
            spread_code(h)

        @pl.when(quiet)
        def _():
            later_gather(h)

        return carry

    lax.fori_loop(0, heads, spread_step, 0)

    def last_step(h, carry):
        @pl.when(jnp.logical_not(quiet))
        def _():
            later_gather(h)

        last_code(h)
        return carry

    lax.fori_loop(0, heads, last_step, 0)
    sent(ly_out, ly_s).wait_send()
    sent(la_out, la_s).wait_send()
    sent(cy_out, cy_s).wait_send()
    sent(c_fin.at[side], cp_s).wait_send()

    @pl.when(has_down)
    def _():
        sent(lz_out, lz_s).wait_send()

    @pl.when(at != center)
    def _():
        sent(c_out, c_s).wait_send()

    @pl.when((at <= center) & has_down)
    def _():
        sent(c_fin.at[side], fd_s).wait_send()

    @pl.when((at >= center) & has_up)
    def _():
        sent(c_fin.at[side], fu_s).wait_send()


def write_out(*refs):
    sems = refs[-1]
    copies = [pltpu.make_async_copy(refs[k], refs[k + 3], sems.at[k]) for k in range(3)]
    for copy in copies:
        copy.start()
    for copy in copies:
        copy.wait()


def per_device(queries, values, codes, codebook, out_weight, grad_out):
    n_seq, n_head = lax.axis_size("seq"), lax.axis_size("head")
    row_count = queries.shape[0]
    heads, entries, width = codebook.shape
    nb = row_count // BLOCK
    parts = BLOCK // TILE
    chunks = row_count // CHUNK
    half = entries // 2
    hbm = pl.BlockSpec(memory_space=pltpu.HBM)
    vmem = pl.BlockSpec(memory_space=pltpu.VMEM)
    dma = pltpu.SemaphoreType.DMA
    halves = pltpu.VMEM((heads, half, width), BF16)
    pieces = pltpu.VMEM((heads, SUBS, half // SUBS, width), BF16)
    counts = pltpu.VMEM((heads, 1, entries), F32)
    results = pl.pallas_call(
        functools.partial(kernel, n_seq, n_head),
        out_shape=(
            jax.ShapeDtypeStruct(queries.shape, BF16),
            jax.ShapeDtypeStruct(queries.shape, BF16),
            jax.ShapeDtypeStruct(codebook.shape, F32),
        ),
        in_specs=[hbm] * 6,
        out_specs=(vmem,) * 3,
        scratch_shapes=[
            pltpu.VMEM(queries.shape, BF16),
            pltpu.VMEM(queries.shape, BF16),
            pltpu.VMEM((heads, row_count), jnp.int32),
            pltpu.VMEM(codebook.shape, BF16),
            pltpu.VMEM(out_weight.shape, BF16),
            pltpu.VMEM((n_head,) + grad_out.shape, BF16),
            pltpu.VMEM(queries.shape, BF16),
            pltpu.VMEM((heads, nb, entries, BLOCK), BF16),
            pltpu.VMEM((heads, nb, BLOCK, entries), BF16),
            pltpu.VMEM((heads, nb, BLOCK, width), BF16),
            pltpu.VMEM((heads, nb, width, BLOCK), BF16),
            pltpu.VMEM((heads, width, entries), BF16),
            pltpu.VMEM((heads, nb, entries, width), F32),
            pltpu.VMEM((heads, nb, 1, entries), F32),
            pltpu.VMEM((heads, nb, 1, entries), F32),
            pltpu.VMEM((heads, nb, entries, width), F32),
            pltpu.VMEM((heads, nb, entries, width), BF16),
            pltpu.VMEM((heads, nb, BLOCK, BLOCK), BF16),
            pltpu.VMEM((heads, nb, entries, BLOCK), BF16),
            pltpu.VMEM((heads, nb, BLOCK, width), F32),
            pltpu.VMEM((heads, nb, entries, width), F32),
            pltpu.VMEM((heads, entries, width), F32),
            pltpu.VMEM((heads, entries, width), F32),
            counts, counts, counts, counts,
            halves, halves, halves, halves, halves, halves,
            halves, halves, halves, halves, halves, halves,
            halves, halves, pieces, pieces, pieces,
            pltpu.VMEM((2, heads, SUBS, half // SUBS, width), BF16),
            dma((5,)), dma((2,)),
            dma((1,)), dma((n_head // 2, row_count // TILE)), dma((max(n_head // 2 - 1, 1), chunks)),
            dma((1,)), dma((1,)), dma((1,)), dma((1,)),
        ] + [dma((1,)), dma((heads,))] * 7 + [
            dma((1,)), dma((heads, SUBS)), dma((heads, SUBS)), dma((1,)), dma((heads, SUBS)),
            dma((1,)), dma((1,)), dma((heads, SUBS)),
        ],
        compiler_params=pltpu.CompilerParams(
            collective_id=0, has_side_effects=True, vmem_limit_bytes=50 * 1024 * 1024),
    )(*(pltpu.with_memory_space_constraint(x, pltpu.HBM) for x in (queries, values, codes.T, codebook, out_weight, grad_out)))
    return pl.pallas_call(
        write_out,
        out_shape=tuple(jax.ShapeDtypeStruct(r.shape, r.dtype) for r in results),
        in_specs=[vmem] * 3,
        out_specs=(hbm,) * 3,
        scratch_shapes=[dma((3,))],
        compiler_params=pltpu.CompilerParams(vmem_limit_bytes=1024 * 1024),
    )(*results)


def solution(mesh):
    return jax.shard_map(
        per_device,
        mesh=mesh,
        in_specs=(
            P("seq", "head"),
            P("seq", "head"),
            P("seq", "head"),
            P("head", None, None),
            P("head", None),
            P("seq", "head"),
        ),
        out_specs=(P("seq", "head"), P("seq", "head"), P("head", None, None)),
        check_vma=False,
    )
```

```python
import functools

import jax
import jax.numpy as jnp
from jax import lax
from jax.experimental import pallas as pl
from jax.experimental.pallas import tpu as pltpu
from jax.sharding import PartitionSpec as P

BLOCK = 512
TILE = 256
CHUNK = 128
SUBS = 2
WRITES = 4
NEG = -1e30
LOG2E = 1.4426950408889634
F32 = jnp.float32
BF16 = jnp.bfloat16
MESH = pl.DeviceIdType.MESH


def nn(a, b):
    return lax.dot_general(a, b, (((1,), (0,)), ((), ())), preferred_element_type=F32)


def nt(a, b):
    return lax.dot_general(a, b, (((1,), (1,)), ((), ())), preferred_element_type=F32)


def kernel(
    n_seq, n_head,
    q_in, v_in, codes_in, cb_in, w_in, go_in,
    gq_ref, gv_ref, gc_ref,
    q_ref, v_ref, codes_ref, cb_ref, w_ref, gath, dout,
    hot_t, hot, keys, keys_t, book_t, own, cnt_block, cnt_pre, cnt_full, cval,
    local_low, cache_low, local_part, vpart, code_acc, later_ref,
    cn_own, cny_in, cnz_out, cnz_in,
    py_out, py_in, pz_out, pz_in, pa_out, pa_in,
    ly_out, ly_in, lz_out, lz_in, la_out, la_in,
    cy_out, cy_in, c_out, c_below, c_above, c_fin,
    load_s, go_s, ag_s, ag_r, ax_r, cny_s, cny_r, cnz_s, cnz_r,
    py_s, py_r, pz_s, pz_r, pa_s, pa_r,
    ly_s, ly_r, lz_s, lz_r, la_s, la_r,
    cy_s, cy_r, c_s, cb_r, cu_r, cp_s, cp_r, fu_s, fd_s, cf_r,
):
    rows_all = q_ref.shape[0]
    heads, entries, width = cb_ref.shape
    nb = rows_all // BLOCK
    parts = BLOCK // TILE
    chunks = rows_all // CHUNK
    per_tile = TILE // CHUNK
    outer = n_seq // 2
    half = entries // 2
    piece = half // SUBS
    center = outer // 2
    scale = width ** (-0.5)
    me = lax.axis_index("seq")
    mine = lax.axis_index("head")
    at = me // 2
    side = me % 2
    partner = me + 1 - 2 * side
    is_hi = side.astype(F32)
    is_lo = 1.0 - is_hi
    own_half = pl.ds(pl.multiple_of(side * half, half), half)
    other_half = pl.ds(pl.multiple_of((1 - side) * half, half), half)
    has_down = at > 0
    has_up = at < outer - 1
    bits = []
    bit = n_head // 2
    while bit >= 1:
        bits.append(bit)
        bit //= 2

    def flip(index, mask):
        for b in bits:
            if mask & b:
                index = index + b - 2 * b * ((index // b) % 2)
        return index

    def go_load(first, last):
        span = pl.ds(first * CHUNK, (last - first) * CHUNK)
        return pltpu.make_async_copy(go_in.at[span], gath.at[mine, span], go_s.at[min(first, 1)])

    loads = [
        pltpu.make_async_copy(src, dst, load_s.at[k])
        for k, (src, dst) in enumerate(
            ((codes_in, codes_ref), (cb_in, cb_ref), (v_in, v_ref), (q_in, q_ref), (w_in, w_ref)))
    ]
    loads[0].start()
    go_load(0, 1).start()
    go_load(1, chunks).start()
    for copy in loads[1:]:
        copy.start()

    barrier = pltpu.get_barrier_semaphore()
    pl.semaphore_signal(barrier, inc=1, device_id={"seq": partner}, device_id_type=MESH)

    @pl.when(has_down)
    def _():
        pl.semaphore_signal(barrier, inc=1, device_id={"seq": me - 2}, device_id_type=MESH)

    @pl.when(has_up)
    def _():
        pl.semaphore_signal(barrier, inc=1, device_id={"seq": me + 2}, device_id_type=MESH)

    for b in bits:
        pl.semaphore_signal(barrier, inc=1, device_id={"head": flip(mine, b)}, device_id_type=MESH)

    loads[0].wait()
    row_at = lax.broadcasted_iota(jnp.int32, (entries, BLOCK), 0)
    lane_at = lax.broadcasted_iota(jnp.int32, (BLOCK, entries), 1)

    def count(h, carry):
        total = jnp.zeros((1, entries), F32)
        for b in range(nb):
            code_row = codes_ref[pl.ds(h, 1), pl.ds(b * BLOCK, BLOCK)]
            code_full = jnp.transpose(jnp.broadcast_to(code_row, (width, BLOCK)))
            code_cols = jnp.concatenate([code_full] * (entries // width), axis=1)
            one_f = (lane_at == code_cols).astype(F32)
            hot[h, b] = one_f.astype(BF16)
            counts = jnp.sum(one_f, axis=0, keepdims=True)
            cnt_block[h, b] = counts
            total += counts
        cn_own[h] = total
        return carry

    lax.fori_loop(0, heads, count, 0)
    pl.semaphore_wait(
        barrier, 1 + len(bits) + jnp.where(has_down, 1, 0) + jnp.where(has_up, 1, 0))

    def gather_copy(src_mask, to, chunk):
        block = flip(mine, src_mask)
        span = pl.ds(chunk * CHUNK, CHUNK)
        slot = src_mask ^ to
        return pltpu.make_async_remote_copy(
            src_ref=gath.at[block, span], dst_ref=gath.at[block, span],
            send_sem=ag_s.at[0], recv_sem=ax_r.at[rank[slot], chunk] if slot in feeds else ag_r.at[rank[slot], chunk // per_tile],
            device_id={"head": flip(mine, to)}, device_id_type=MESH)

    plan = []
    known = [0]
    for b in bits:
        plan += [(m, b) for m in known]
        known += [m ^ b for m in known]
    by_slot = {m ^ b: (m, b) for m, b in plan}
    feeds = {m for m, _ in plan if m != 0}
    rank = {slot: k for k, slot in enumerate(sorted(feeds))}
    rank.update({slot: k for k, slot in enumerate(sorted(set(by_slot) - feeds))})
    for chunk in range(chunks):
        if chunk == 0:
            go_load(0, 1).wait()
        elif chunk == 1:
            go_load(1, chunks).wait()
        for m, b in plan:
            if m == 0 and b == bits[0]:
                gather_copy(m, b, chunk).start()
    for m, b in plan:
        if m == 0 and b != bits[0]:
            for chunk in range(chunks):
                gather_copy(m, b, chunk).start()
    taken = set()

    def tile_copy(slot, start):
        m, b = by_slot[slot]
        block = flip(mine, m)
        span = pl.ds(start, TILE)
        return pltpu.make_async_remote_copy(
            src_ref=gath.at[block, span], dst_ref=gath.at[block, span],
            send_sem=ag_s.at[0], recv_sem=ag_r.at[rank[slot], start // TILE],
            device_id={"head": flip(mine, b)}, device_id_type=MESH)

    def all_sent():
        span = gath.at[pl.ds(0, len(plan))]
        return pltpu.make_async_remote_copy(
            src_ref=span, dst_ref=span, send_sem=ag_s.at[0], recv_sem=ag_r.at[0, 0],
            device_id={"head": flip(mine, bits[0])}, device_id_type=MESH)

    def arrive(slot, chunk):
        if (slot, chunk) not in taken:
            taken.add((slot, chunk))
            m, b = by_slot[slot]
            gather_copy(m, b, chunk).wait_recv()

    def relay(chunk):
        for m, b in plan:
            if m != 0:
                arrive(m, chunk)
                gather_copy(m, b, chunk).start()

    def seq_copy(src, dst, send, recv, to):
        return pltpu.make_async_remote_copy(
            src_ref=src, dst_ref=dst, send_sem=send, recv_sem=recv,
            device_id={"seq": to}, device_id_type=MESH)

    count_pair = seq_copy(cn_own, cny_in, cny_s.at[0], cny_r.at[0], partner)
    count_pair.start()

    def count_hop(to):
        return seq_copy(cnz_out, cnz_in, cnz_s.at[0], cnz_r.at[0], to)

    def take_counts():
        count_pair.wait_recv()

        @pl.when(jnp.logical_not(has_down))
        def _():
            cnz_in[...] = jnp.zeros(cnz_in.shape, F32)

        @pl.when(has_down)
        def _():
            count_hop(me - 2).wait_recv()

        cnz_out[...] = cnz_in[...] + cn_own[...] + cny_in[...]

        @pl.when(has_up)
        def _():
            count_hop(me + 2).start()

        row = cnz_in[...] + cny_in[...] * is_hi
        for b in range(nb):
            cnt_pre[:, b] = row
            row = row + cnt_block[:, b]

    def prefix_pair(h):
        return seq_copy(py_out.at[h], py_in.at[h], py_s.at[0], py_r.at[h], partner)

    def prefix_hop(h, to):
        return seq_copy(pz_out.at[h], pz_in.at[h], pz_s.at[0], pz_r.at[h], to)

    def prefix_back(h):
        return seq_copy(pa_out.at[h], pa_in.at[h], pa_s.at[0], pa_r.at[h], partner)

    loads[1].wait()
    loads[2].wait()

    def sums(h, carry):
        head_lanes = pl.ds(pl.multiple_of(h * width, width), width)
        for b in range(nb):
            rows = pl.ds(b * BLOCK, BLOCK)
            one_t = (row_at == codes_ref[pl.ds(h, 1), rows]).astype(F32).astype(BF16)
            hot_t[h, b] = one_t
            own[h, b] = nn(one_t, v_ref[rows, head_lanes])
        total = own[h, 0, other_half]
        for b in range(1, nb):
            total += own[h, b, other_half]
        py_out[h] = total.astype(BF16)
        prefix_pair(h).start()
        return carry

    lax.fori_loop(0, heads, sums, 0)

    @pl.when(jnp.logical_not(has_down))
    def _():
        take_counts()

    def prefix_chain(h):
        prefix_pair(h).wait_recv()

        @pl.when(jnp.logical_not(has_down))
        def _():
            pz_in[h] = jnp.zeros(pz_in.shape[1:], BF16)

        @pl.when(has_down)
        def _():
            prefix_hop(h, me - 2).wait_recv()

        below = pz_in[h].astype(F32)
        pair = py_in[h].astype(F32)
        total = own[h, 0, own_half]
        for b in range(1, nb):
            total += own[h, b, own_half]
        pz_out[h] = (below + total + pair).astype(BF16)

        @pl.when(has_up)
        def _():
            prefix_hop(h, me + 2).start()

        pa_out[h] = (below + total * is_lo).astype(BF16)
        prefix_back(h).start()
        prefix = below + pair * is_hi
        for b in range(nb):
            cval[h, b, own_half] = prefix.astype(BF16)
            prefix = prefix + own[h, b, own_half]

    def prefix_gather(h):
        prefix_back(h).wait_recv()
        prefix = pa_in[h].astype(F32)
        for b in range(nb):
            cval[h, b, other_half] = prefix.astype(BF16)
            prefix = prefix + own[h, b, other_half]

    def make_keys(h, carry):
        book = cb_ref[h]
        book_t[h] = jnp.transpose(book.astype(F32)).astype(BF16)
        for b in range(nb):
            key = nn(hot[h, b], book)
            keys[h, b] = key.astype(BF16)
            keys_t[h, b] = jnp.transpose(key).astype(BF16)
        return carry

    pairs = heads // 2

    def chain_pair(j):
        prefix_chain(2 * j)
        prefix_chain(2 * j + 1)

    @pl.when(jnp.logical_not(has_down))
    def _():
        chain_pair(0)

    lax.fori_loop(0, heads, make_keys, 0)

    def softmax(h, b):
        head_lanes = pl.ds(pl.multiple_of(h * width, width), width)
        book = cb_ref[h]
        count_full = jnp.transpose(jnp.broadcast_to(cnt_pre[h, b], (width, entries)))
        cnt_full[h, b] = count_full
        bias_full = jnp.where(count_full > 0.0, 0.0, NEG)
        counts = jnp.concatenate([count_full] * (TILE // width), axis=1)
        bias = jnp.concatenate([bias_full] * (TILE // width), axis=1)
        for p in range(parts):
            seen = (p + 1) * TILE
            query = q_ref[pl.ds(pl.multiple_of(b * BLOCK + p * TILE, TILE), TILE), head_lanes]
            at_u = lax.broadcasted_iota(jnp.int32, (seen, TILE), 0)
            at_t = lax.broadcasted_iota(jnp.int32, (seen, TILE), 1) + p * TILE
            scores = jnp.where(at_u <= at_t, nt(keys[h, b, 0:seen], query) * (scale * LOG2E), NEG)
            cache_scores = nt(book, query) * (scale * LOG2E) + bias
            highest = jnp.maximum(
                jnp.max(scores, axis=0, keepdims=True), jnp.max(cache_scores, axis=0, keepdims=True))
            local_exp = jnp.exp2(scores - highest)
            cache_exp = jnp.exp2(cache_scores - highest)
            total = jnp.sum(local_exp, axis=0, keepdims=True) + jnp.sum(cache_exp * counts, axis=0, keepdims=True)
            inverse = 1.0 / total
            lanes = slice(p * TILE, seen)
            local_low[h, b, 0:seen, lanes] = (local_exp * inverse).astype(BF16)
            if seen < BLOCK:
                local_low[h, b, seen:BLOCK, lanes] = jnp.zeros((BLOCK - seen, TILE), BF16)
            cache_low[h, b, :, lanes] = (cache_exp * inverse).astype(BF16)

    rounds = heads * nb // 2
    relay_at = {}
    for chunk in range(chunks):
        where = (0, 1, rounds - 1, "mid", "late", rounds, rounds + 2, rounds + heads - 1)[8 * chunk // chunks]
        relay_at.setdefault(where, []).append(chunk)

    def relays(first, last, now):
        for slot, which in relay_at.items():
            if not isinstance(slot, str) and first <= slot < last:
                @pl.when(now == slot - first)
                def _(which=which):
                    for chunk in which:
                        relay(chunk)

    def relay_named(name):
        for chunk in relay_at.get(name, []):
            relay(chunk)

    @pl.when(jnp.logical_not(has_down))
    def _():
        for j in range(1, pairs):
            chain_pair(j)

    @pl.when(has_down)
    def _():
        take_counts()

    loads[3].wait()

    def unit(k, carry):
        softmax(2 * k // nb, 2 * k % nb)
        softmax((2 * k + 1) // nb, (2 * k + 1) % nb)
        j = k - at + 1

        @pl.when(has_down & (j >= 0) & (j < pairs))
        def _():
            chain_pair(j)

        relays(0, rounds, k)
        return carry

    lax.fori_loop(0, rounds, unit, 0)
    loads[4].wait()

    depth = go_in.shape[1]

    def project(start):
        rows = pl.ds(start, TILE)
        total = nt(gath[0, rows], w_ref[:, 0:depth])
        for k in range(1, n_head):
            total += nt(gath[k, rows], w_ref[:, k * depth:(k + 1) * depth])
        dout[rows] = total.astype(BF16)

    def value_pass(h, b):
        head_lanes = pl.ds(pl.multiple_of(h * width, width), width)
        vpart[h, b] = nn(cache_low[h, b], dout[pl.ds(b * BLOCK, BLOCK), head_lanes])

    def grad_pass(h, b):
        head_lanes = pl.ds(pl.multiple_of(h * width, width), width)
        rows = pl.ds(b * BLOCK, BLOCK)
        query = q_ref[rows, head_lanes]
        grad = dout[rows, head_lanes]
        counts = jnp.concatenate([cnt_full[h, b]] * (BLOCK // width), axis=1)
        local_grad = nt(v_ref[rows, head_lanes], grad)
        cache_grad = nt(cval[h, b], grad)
        local_prob = local_low[h, b].astype(F32)
        cache_prob = cache_low[h, b].astype(F32)
        delta = (jnp.sum(local_prob * local_grad, axis=0, keepdims=True)
                 + jnp.sum(cache_prob * cache_grad, axis=0, keepdims=True))
        local_score_grad = (local_prob * (local_grad - delta) * scale).astype(BF16)
        cache_score_grad = (cache_prob * (cache_grad - delta * counts) * scale).astype(BF16)
        gq_t = nn(keys_t[h, b], local_score_grad) + nn(book_t[h], cache_score_grad)
        gq_ref[rows, head_lanes] = jnp.transpose(gq_t).astype(BF16)
        key_grad = nn(local_score_grad, query).astype(BF16)
        code = nn(hot_t[h, b], key_grad) + nn(cache_score_grad, query)
        local_part[h, b] = nn(local_low[h, b], grad)
        if b == 0:
            code_acc[h] = code
        else:
            code_acc[h] += code

    def later_pair(h):
        return seq_copy(ly_out.at[h], ly_in.at[h], ly_s.at[0], ly_r.at[h], partner)

    def later_hop(h, to):
        return seq_copy(lz_out.at[h], lz_in.at[h], lz_s.at[0], lz_r.at[h], to)

    def later_back(h):
        return seq_copy(la_out.at[h], la_in.at[h], la_s.at[0], la_r.at[h], partner)

    def part_total(h, span):
        total = vpart[h, 0, span]
        for b in range(1, nb):
            total += vpart[h, b, span]
        return total

    def send_later(h):
        ly_out[h] = part_total(h, other_half).astype(BF16)
        later_pair(h).start()

    def later_chain(h):
        later_pair(h).wait_recv()

        @pl.when(jnp.logical_not(has_up))
        def _():
            lz_in[h] = jnp.zeros(lz_in.shape[1:], BF16)

        @pl.when(has_up)
        def _():
            later_hop(h, me + 2).wait_recv()

        above = lz_in[h].astype(F32)
        pair = ly_in[h].astype(F32)
        total = part_total(h, own_half)
        lz_out[h] = (above + total + pair).astype(BF16)

        @pl.when(has_down)
        def _():
            later_hop(h, me - 2).start()

        la_out[h] = (above + total * is_hi).astype(BF16)
        later_ref[h, own_half] = above + pair * is_lo

    def later_gather(h):
        later_back(h).wait_recv()
        later_ref[h, other_half] = la_in[h].astype(F32)
        head_lanes = pl.ds(pl.multiple_of(h * width, width), width)
        later = later_ref[h]
        for b in reversed(range(nb)):
            rows = pl.ds(b * BLOCK, BLOCK)
            lookup = nn(hot[h, b], later.astype(BF16))
            gv_ref[rows, head_lanes] = (local_part[h, b] + lookup).astype(BF16)
            later = later + vpart[h, b]

    def code_pair(h):
        return seq_copy(cy_out.at[h], cy_in.at[h], cy_s.at[0], cy_r.at[h], partner)

    def code_up(h, s):
        return seq_copy(c_out.at[h, s], c_below.at[h, s], c_s.at[0], cb_r.at[h, s], me + 2)

    def code_down(h, s):
        return seq_copy(c_out.at[h, s], c_above.at[h, s], c_s.at[0], cu_r.at[h, s], me - 2)

    def fin_up(h, s):
        return seq_copy(c_fin.at[side, h, s], c_fin.at[side, h, s], fu_s.at[0], cf_r.at[h, s], me + 2)

    def fin_down(h, s):
        return seq_copy(c_fin.at[side, h, s], c_fin.at[side, h, s], fd_s.at[0], cf_r.at[h, s], me - 2)

    def fin_pair(h, which, s):
        return seq_copy(c_fin.at[which, h, s], c_fin.at[which, h, s], cp_s.at[0], cp_r.at[h, s], partner)

    def send_code(h):
        cy_out[h] = code_acc[h, other_half].astype(BF16)
        code_pair(h).start()

    def piece_of(which, s):
        return pl.ds(pl.multiple_of(which * half + s * piece, piece), piece)

    def reduce_code(h):
        code_pair(h).wait_recv()
        code_acc[h, own_half] += cy_in[h].astype(F32)
        for s in range(SUBS):
            span = piece_of(side, s)

            @pl.when((at <= center) & has_down)
            def _(s=s, span=span):
                code_up(h, s).wait_recv()
                code_acc[h, span] += c_below[h, s].astype(F32)

            @pl.when((at >= center) & has_up)
            def _(s=s, span=span):
                code_down(h, s).wait_recv()
                code_acc[h, span] += c_above[h, s].astype(F32)

            c_out[h, s] = code_acc[h, span].astype(BF16)

            @pl.when(at < center)
            def _(s=s):
                code_up(h, s).start()

            @pl.when(at > center)
            def _(s=s):
                code_down(h, s).start()

    def spread_code(h):
        for s in range(SUBS):
            @pl.when(at == center)
            def _(s=s):
                c_fin[side, h, s] = c_out[h, s]

            @pl.when(at != center)
            def _(s=s):
                fin_up(h, s).wait_recv()

            @pl.when((at <= center) & has_down)
            def _(s=s):
                fin_down(h, s).start()

            @pl.when((at >= center) & has_up)
            def _(s=s):
                fin_up(h, s).start()

            fin_pair(h, side, s).start()
            gc_ref[h, piece_of(side, s)] = c_fin[side, h, s].astype(F32)

    def last_code(h):
        for s in range(SUBS):
            fin_pair(h, 1 - side, s).wait_recv()
            gc_ref[h, piece_of(1 - side, s)] = c_fin[1 - side, h, s].astype(F32)

    for b in range(nb):
        final = b == nb - 1
        for part in range(parts):
            start = b * BLOCK + part * TILE
            for slot in by_slot:
                if slot in feeds:
                    for chunk in range(start // CHUNK, (start + TILE) // CHUNK):
                        arrive(slot, chunk)
                else:
                    tile_copy(slot, start).wait_recv()
            project(start)
            if b == 0:
                if part == 0:
                    relay_named("mid")
        def values(h, carry, b=b, final=final):
            value_pass(h, b)
            if final:
                @pl.when(has_down)
                def _():
                    send_later(h)

            return carry

        lax.fori_loop(0, heads, values, 0)
        if b == 0:
            relay_named("late")

            def rest(h, carry):
                @pl.when(has_down & (at - 1 + h // 2 >= rounds))
                def _():
                    prefix_chain(h)

                return carry

            lax.fori_loop(0, heads, rest, 0)

        def grads(h, carry, b=b, final=final):
            if b == 0:
                prefix_gather(h)
            grad_pass(h, b)
            if b == 0:
                relays(rounds, rounds + heads, h)
            if final:
                send_code(h)

                @pl.when(jnp.logical_not(has_up))
                def _():
                    later_chain(h)

            return carry

        lax.fori_loop(0, heads, grads, 0)

    def send_rest(h, carry):
        @pl.when(jnp.logical_not(has_down))
        def _():
            send_later(h)

        return carry

    lax.fori_loop(0, heads, send_rest, 0)

    behind = outer - 1 - at
    soon = behind * 2 < outer

    def chain_step(h, carry):
        @pl.when(soon & (behind > 0))
        def _():
            later_chain(h)

        return carry

    lax.fori_loop(0, heads, chain_step, 0)

    @pl.when(soon & (behind > 0))
    def _():
        for h in range(heads):
            later_back(h).start()

    def reduce_step(h, carry):
        reduce_code(h)

        @pl.when(at == center)
        def _():
            spread_code(h)

        @pl.when(jnp.logical_not(soon) & has_down & (h == 1))
        def _():
            later_chain(h - 1)
            later_back(h - 1).start()

        return carry

    lax.fori_loop(0, heads, reduce_step, 0)

    def back_step(h, carry):
        @pl.when(jnp.logical_not(soon | (has_down & (h == 0))))
        def _():
            later_chain(h)

        @pl.when((behind == 0) | jnp.logical_not(soon | (has_down & (h == 0))))
        def _():
            later_back(h).start()

        return carry

    lax.fori_loop(0, heads, back_step, 0)

    def sent(ref, sem):
        return seq_copy(ref, ref, sem.at[0], sem.at[0], partner)

    sent(py_out, py_s).wait_send()
    sent(pa_out, pa_s).wait_send()

    @pl.when(has_up)
    def _():
        sent(pz_out, pz_s).wait_send()

    count_pair.wait_send()

    @pl.when(has_up)
    def _():
        count_hop(me + 2).wait_send()

    all_sent().wait_send()

    quiet = (at == center) | jnp.logical_not(has_down & has_up)

    def spread_step(h, carry):
        @pl.when(at != center)
        def _():
            spread_code(h)

        @pl.when(quiet)
        def _():
            later_gather(h)

        return carry

    lax.fori_loop(0, heads, spread_step, 0)

    def last_step(h, carry):
        @pl.when(jnp.logical_not(quiet))
        def _():
            later_gather(h)

        last_code(h)
        return carry

    lax.fori_loop(0, heads, last_step, 0)
    sent(ly_out, ly_s).wait_send()
    sent(la_out, la_s).wait_send()
    sent(cy_out, cy_s).wait_send()
    sent(c_fin.at[side], cp_s).wait_send()

    @pl.when(has_down)
    def _():
        sent(lz_out, lz_s).wait_send()

    @pl.when(at != center)
    def _():
        sent(c_out, c_s).wait_send()

    @pl.when((at <= center) & has_down)
    def _():
        sent(c_fin.at[side], fd_s).wait_send()

    @pl.when((at >= center) & has_up)
    def _():
        sent(c_fin.at[side], fu_s).wait_send()


def write_out(*refs):
    sems = refs[-1]
    copies = []
    for k in range(3):
        rows = refs[k].shape[0] // WRITES
        for n in range(WRITES):
            span = pl.ds(n * rows, rows)
            copies.append(pltpu.make_async_copy(refs[k].at[span], refs[k + 3].at[span], sems.at[k, n]))
    for copy in copies:
        copy.start()
    for copy in copies:
        copy.wait()


def per_device(queries, values, codes, codebook, out_weight, grad_out):
    n_seq, n_head = lax.axis_size("seq"), lax.axis_size("head")
    row_count = queries.shape[0]
    heads, entries, width = codebook.shape
    nb = row_count // BLOCK
    parts = BLOCK // TILE
    chunks = row_count // CHUNK
    half = entries // 2
    hbm = pl.BlockSpec(memory_space=pltpu.HBM)
    vmem = pl.BlockSpec(memory_space=pltpu.VMEM)
    dma = pltpu.SemaphoreType.DMA
    halves = pltpu.VMEM((heads, half, width), BF16)
    pieces = pltpu.VMEM((heads, SUBS, half // SUBS, width), BF16)
    counts = pltpu.VMEM((heads, 1, entries), F32)
    results = pl.pallas_call(
        functools.partial(kernel, n_seq, n_head),
        out_shape=(
            jax.ShapeDtypeStruct(queries.shape, BF16),
            jax.ShapeDtypeStruct(queries.shape, BF16),
            jax.ShapeDtypeStruct(codebook.shape, F32),
        ),
        in_specs=[hbm] * 6,
        out_specs=(vmem,) * 3,
        scratch_shapes=[
            pltpu.VMEM(queries.shape, BF16),
            pltpu.VMEM(queries.shape, BF16),
            pltpu.VMEM((heads, row_count), jnp.int32),
            pltpu.VMEM(codebook.shape, BF16),
            pltpu.VMEM(out_weight.shape, BF16),
            pltpu.VMEM((n_head,) + grad_out.shape, BF16),
            pltpu.VMEM(queries.shape, BF16),
            pltpu.VMEM((heads, nb, entries, BLOCK), BF16),
            pltpu.VMEM((heads, nb, BLOCK, entries), BF16),
            pltpu.VMEM((heads, nb, BLOCK, width), BF16),
            pltpu.VMEM((heads, nb, width, BLOCK), BF16),
            pltpu.VMEM((heads, width, entries), BF16),
            pltpu.VMEM((heads, nb, entries, width), F32),
            pltpu.VMEM((heads, nb, 1, entries), F32),
            pltpu.VMEM((heads, nb, 1, entries), F32),
            pltpu.VMEM((heads, nb, entries, width), F32),
            pltpu.VMEM((heads, nb, entries, width), BF16),
            pltpu.VMEM((heads, nb, BLOCK, BLOCK), BF16),
            pltpu.VMEM((heads, nb, entries, BLOCK), BF16),
            pltpu.VMEM((heads, nb, BLOCK, width), F32),
            pltpu.VMEM((heads, nb, entries, width), F32),
            pltpu.VMEM((heads, entries, width), F32),
            pltpu.VMEM((heads, entries, width), F32),
            counts, counts, counts, counts,
            halves, halves, halves, halves, halves, halves,
            halves, halves, halves, halves, halves, halves,
            halves, halves, pieces, pieces, pieces,
            pltpu.VMEM((2, heads, SUBS, half // SUBS, width), BF16),
            dma((5,)), dma((2,)),
            dma((1,)), dma((n_head // 2, row_count // TILE)), dma((max(n_head // 2 - 1, 1), chunks)),
            dma((1,)), dma((1,)), dma((1,)), dma((1,)),
        ] + [dma((1,)), dma((heads,))] * 7 + [
            dma((1,)), dma((heads, SUBS)), dma((heads, SUBS)), dma((1,)), dma((heads, SUBS)),
            dma((1,)), dma((1,)), dma((heads, SUBS)),
        ],
        compiler_params=pltpu.CompilerParams(
            collective_id=0, has_side_effects=True, vmem_limit_bytes=50 * 1024 * 1024),
    )(*(pltpu.with_memory_space_constraint(x, pltpu.HBM) for x in (queries, values, codes.T, codebook, out_weight, grad_out)))
    return pl.pallas_call(
        write_out,
        out_shape=tuple(jax.ShapeDtypeStruct(r.shape, r.dtype) for r in results),
        in_specs=[vmem] * 3,
        out_specs=(hbm,) * 3,
        scratch_shapes=[dma((3, WRITES))],
        compiler_params=pltpu.CompilerParams(vmem_limit_bytes=1024 * 1024),
    )(*results)


def solution(mesh):
    return jax.shard_map(
        per_device,
        mesh=mesh,
        in_specs=(
            P("seq", "head"),
            P("seq", "head"),
            P("seq", "head"),
            P("head", None, None),
            P("head", None),
            P("seq", "head"),
        ),
        out_specs=(P("seq", "head"), P("seq", "head"), P("head", None, None)),
        check_vma=False,
    )
```

```python
import functools

import jax
import jax.numpy as jnp
from jax import lax
from jax.experimental import pallas as pl
from jax.experimental.pallas import tpu as pltpu
from jax.sharding import PartitionSpec as P

BLOCK = 512
TILE = 256
CHUNK = 128
SUBS = 2
NEG = -1e30
LOG2E = 1.4426950408889634
F32 = jnp.float32
BF16 = jnp.bfloat16
MESH = pl.DeviceIdType.MESH


def nn(a, b):
    return lax.dot_general(a, b, (((1,), (0,)), ((), ())), preferred_element_type=F32)


def nt(a, b):
    return lax.dot_general(a, b, (((1,), (1,)), ((), ())), preferred_element_type=F32)


def kernel(
    n_seq, n_head,
    q_in, v_in, codes_in, cb_in, w_in, go_in,
    gq_ref, gv_ref, gc_ref,
    q_ref, v_ref, codes_ref, cb_ref, w_ref, gath, dout,
    hot_t, hot, keys, keys_t, book_t, own, cnt_block, cnt_pre, cnt_full, cval,
    local_low, cache_low, local_part, vpart, code_acc, later_ref,
    cn_own, cny_in, cnz_out, cnz_in,
    py_out, py_in, pz_out, pz_in, pa_out, pa_in,
    ly_out, ly_in, lz_out, lz_in, la_out, la_in,
    cy_out, cy_in, c_out, c_below, c_above, c_fin,
    load_s, go_s, ag_s, ag_r, ax_r, cny_s, cny_r, cnz_s, cnz_r,
    py_s, py_r, pz_s, pz_r, pa_s, pa_r,
    ly_s, ly_r, lz_s, lz_r, la_s, la_r,
    cy_s, cy_r, c_s, cb_r, cu_r, cp_s, cp_r, fu_s, fd_s, cf_r,
):
    rows_all = q_ref.shape[0]
    heads, entries, width = cb_ref.shape
    nb = rows_all // BLOCK
    parts = BLOCK // TILE
    chunks = rows_all // CHUNK
    per_tile = TILE // CHUNK
    outer = n_seq // 2
    half = entries // 2
    piece = half // SUBS
    center = outer // 2
    scale = width ** (-0.5)
    me = lax.axis_index("seq")
    mine = lax.axis_index("head")
    at = me // 2
    side = me % 2
    partner = me + 1 - 2 * side
    is_hi = side.astype(F32)
    is_lo = 1.0 - is_hi
    own_half = pl.ds(pl.multiple_of(side * half, half), half)
    other_half = pl.ds(pl.multiple_of((1 - side) * half, half), half)
    has_down = at > 0
    has_up = at < outer - 1
    bits = []
    bit = n_head // 2
    while bit >= 1:
        bits.append(bit)
        bit //= 2

    def flip(index, mask):
        for b in bits:
            if mask & b:
                index = index + b - 2 * b * ((index // b) % 2)
        return index

    def go_load(first, last):
        span = pl.ds(first * CHUNK, (last - first) * CHUNK)
        return pltpu.make_async_copy(go_in.at[span], gath.at[mine, span], go_s.at[min(first, 1)])

    loads = [
        pltpu.make_async_copy(src, dst, load_s.at[k])
        for k, (src, dst) in enumerate(
            ((codes_in, codes_ref), (cb_in, cb_ref), (v_in, v_ref), (q_in, q_ref), (w_in, w_ref)))
    ]
    loads[0].start()
    go_load(0, 1).start()
    go_load(1, chunks).start()
    for copy in loads[1:]:
        copy.start()

    barrier = pltpu.get_barrier_semaphore()
    pl.semaphore_signal(barrier, inc=1, device_id={"seq": partner}, device_id_type=MESH)

    @pl.when(has_down)
    def _():
        pl.semaphore_signal(barrier, inc=1, device_id={"seq": me - 2}, device_id_type=MESH)

    @pl.when(has_up)
    def _():
        pl.semaphore_signal(barrier, inc=1, device_id={"seq": me + 2}, device_id_type=MESH)

    for b in bits:
        pl.semaphore_signal(barrier, inc=1, device_id={"head": flip(mine, b)}, device_id_type=MESH)

    loads[0].wait()
    row_at = lax.broadcasted_iota(jnp.int32, (entries, BLOCK), 0)
    lane_at = lax.broadcasted_iota(jnp.int32, (BLOCK, entries), 1)

    def count(h, carry):
        total = jnp.zeros((1, entries), F32)
        for b in range(nb):
            code_row = codes_ref[pl.ds(h, 1), pl.ds(b * BLOCK, BLOCK)]
            code_full = jnp.transpose(jnp.broadcast_to(code_row, (width, BLOCK)))
            code_cols = jnp.concatenate([code_full] * (entries // width), axis=1)
            one_f = (lane_at == code_cols).astype(F32)
            hot[h, b] = one_f.astype(BF16)
            counts = jnp.sum(one_f, axis=0, keepdims=True)
            cnt_block[h, b] = counts
            total += counts
        cn_own[h] = total
        return carry

    lax.fori_loop(0, heads, count, 0)
    pl.semaphore_wait(
        barrier, 1 + len(bits) + jnp.where(has_down, 1, 0) + jnp.where(has_up, 1, 0))

    def gather_copy(src_mask, to, chunk):
        block = flip(mine, src_mask)
        span = pl.ds(chunk * CHUNK, CHUNK)
        slot = src_mask ^ to
        return pltpu.make_async_remote_copy(
            src_ref=gath.at[block, span], dst_ref=gath.at[block, span],
            send_sem=ag_s.at[0], recv_sem=ax_r.at[rank[slot], chunk] if slot in feeds else ag_r.at[rank[slot], chunk // per_tile],
            device_id={"head": flip(mine, to)}, device_id_type=MESH)

    plan = []
    known = [0]
    for b in bits:
        plan += [(m, b) for m in known]
        known += [m ^ b for m in known]
    by_slot = {m ^ b: (m, b) for m, b in plan}
    feeds = {m for m, _ in plan if m != 0}
    rank = {slot: k for k, slot in enumerate(sorted(feeds))}
    rank.update({slot: k for k, slot in enumerate(sorted(set(by_slot) - feeds))})
    for chunk in range(chunks):
        if chunk == 0:
            go_load(0, 1).wait()
        elif chunk == 1:
            go_load(1, chunks).wait()
        for m, b in plan:
            if m == 0 and b == bits[0]:
                gather_copy(m, b, chunk).start()
    for m, b in plan:
        if m == 0 and b != bits[0]:
            for chunk in range(chunks):
                gather_copy(m, b, chunk).start()
    taken = set()

    def tile_copy(slot, start):
        m, b = by_slot[slot]
        block = flip(mine, m)
        span = pl.ds(start, TILE)
        return pltpu.make_async_remote_copy(
            src_ref=gath.at[block, span], dst_ref=gath.at[block, span],
            send_sem=ag_s.at[0], recv_sem=ag_r.at[rank[slot], start // TILE],
            device_id={"head": flip(mine, b)}, device_id_type=MESH)

    def all_sent():
        span = gath.at[pl.ds(0, len(plan))]
        return pltpu.make_async_remote_copy(
            src_ref=span, dst_ref=span, send_sem=ag_s.at[0], recv_sem=ag_r.at[0, 0],
            device_id={"head": flip(mine, bits[0])}, device_id_type=MESH)

    def arrive(slot, chunk):
        if (slot, chunk) not in taken:
            taken.add((slot, chunk))
            m, b = by_slot[slot]
            gather_copy(m, b, chunk).wait_recv()

    def relay(chunk):
        for m, b in plan:
            if m != 0:
                arrive(m, chunk)
                gather_copy(m, b, chunk).start()

    def seq_copy(src, dst, send, recv, to):
        return pltpu.make_async_remote_copy(
            src_ref=src, dst_ref=dst, send_sem=send, recv_sem=recv,
            device_id={"seq": to}, device_id_type=MESH)

    count_pair = seq_copy(cn_own, cny_in, cny_s.at[0], cny_r.at[0], partner)
    count_pair.start()

    def count_hop(to):
        return seq_copy(cnz_out, cnz_in, cnz_s.at[0], cnz_r.at[0], to)

    def take_counts():
        count_pair.wait_recv()

        @pl.when(jnp.logical_not(has_down))
        def _():
            cnz_in[...] = jnp.zeros(cnz_in.shape, F32)

        @pl.when(has_down)
        def _():
            count_hop(me - 2).wait_recv()

        cnz_out[...] = cnz_in[...] + cn_own[...] + cny_in[...]

        @pl.when(has_up)
        def _():
            count_hop(me + 2).start()

        row = cnz_in[...] + cny_in[...] * is_hi
        for b in range(nb):
            cnt_pre[:, b] = row
            row = row + cnt_block[:, b]

    def prefix_pair(h):
        return seq_copy(py_out.at[h], py_in.at[h], py_s.at[0], py_r.at[h], partner)

    def prefix_hop(h, to):
        return seq_copy(pz_out.at[h], pz_in.at[h], pz_s.at[0], pz_r.at[h], to)

    def prefix_back(h):
        return seq_copy(pa_out.at[h], pa_in.at[h], pa_s.at[0], pa_r.at[h], partner)

    loads[1].wait()
    loads[2].wait()

    def sums(h, carry):
        head_lanes = pl.ds(pl.multiple_of(h * width, width), width)
        for b in range(nb):
            rows = pl.ds(b * BLOCK, BLOCK)
            one_t = (row_at == codes_ref[pl.ds(h, 1), rows]).astype(F32).astype(BF16)
            hot_t[h, b] = one_t
            own[h, b] = nn(one_t, v_ref[rows, head_lanes])
        total = own[h, 0, other_half]
        for b in range(1, nb):
            total += own[h, b, other_half]
        py_out[h] = total.astype(BF16)
        prefix_pair(h).start()
        return carry

    lax.fori_loop(0, heads, sums, 0)

    @pl.when(jnp.logical_not(has_down))
    def _():
        take_counts()

    def make_keys(h, carry):
        book = cb_ref[h]
        book_t[h] = jnp.transpose(book.astype(F32)).astype(BF16)
        for b in range(nb):
            key = nn(hot[h, b], book)
            keys[h, b] = key.astype(BF16)
            keys_t[h, b] = jnp.transpose(key).astype(BF16)
        return carry

    lax.fori_loop(0, heads, make_keys, 0)

    def prefix_chain(h):
        prefix_pair(h).wait_recv()

        @pl.when(jnp.logical_not(has_down))
        def _():
            pz_in[h] = jnp.zeros(pz_in.shape[1:], BF16)

        @pl.when(has_down)
        def _():
            prefix_hop(h, me - 2).wait_recv()

        below = pz_in[h].astype(F32)
        pair = py_in[h].astype(F32)
        total = own[h, 0, own_half]
        for b in range(1, nb):
            total += own[h, b, own_half]
        pz_out[h] = (below + total + pair).astype(BF16)

        @pl.when(has_up)
        def _():
            prefix_hop(h, me + 2).start()

        pa_out[h] = (below + total * is_lo).astype(BF16)
        prefix_back(h).start()
        prefix = below + pair * is_hi
        for b in range(nb):
            cval[h, b, own_half] = prefix.astype(BF16)
            prefix = prefix + own[h, b, own_half]

    def prefix_gather(h):
        prefix_back(h).wait_recv()
        prefix = pa_in[h].astype(F32)
        for b in range(nb):
            cval[h, b, other_half] = prefix.astype(BF16)
            prefix = prefix + own[h, b, other_half]

    def softmax(h, b):
        head_lanes = pl.ds(pl.multiple_of(h * width, width), width)
        book = cb_ref[h]
        count_full = jnp.transpose(jnp.broadcast_to(cnt_pre[h, b], (width, entries)))
        cnt_full[h, b] = count_full
        bias_full = jnp.where(count_full > 0.0, 0.0, NEG)
        counts = jnp.concatenate([count_full] * (TILE // width), axis=1)
        bias = jnp.concatenate([bias_full] * (TILE // width), axis=1)
        for p in range(parts):
            seen = (p + 1) * TILE
            query = q_ref[pl.ds(pl.multiple_of(b * BLOCK + p * TILE, TILE), TILE), head_lanes]
            at_u = lax.broadcasted_iota(jnp.int32, (seen, TILE), 0)
            at_t = lax.broadcasted_iota(jnp.int32, (seen, TILE), 1) + p * TILE
            scores = jnp.where(at_u <= at_t, nt(keys[h, b, 0:seen], query) * (scale * LOG2E), NEG)
            cache_scores = nt(book, query) * (scale * LOG2E) + bias
            highest = jnp.maximum(
                jnp.max(scores, axis=0, keepdims=True), jnp.max(cache_scores, axis=0, keepdims=True))
            local_exp = jnp.exp2(scores - highest)
            cache_exp = jnp.exp2(cache_scores - highest)
            total = jnp.sum(local_exp, axis=0, keepdims=True) + jnp.sum(cache_exp * counts, axis=0, keepdims=True)
            inverse = 1.0 / total
            lanes = slice(p * TILE, seen)
            local_low[h, b, 0:seen, lanes] = (local_exp * inverse).astype(BF16)
            if seen < BLOCK:
                local_low[h, b, seen:BLOCK, lanes] = jnp.zeros((BLOCK - seen, TILE), BF16)
            cache_low[h, b, :, lanes] = (cache_exp * inverse).astype(BF16)

    rounds = heads * nb // 2
    turn = 2 * at

    def chain_at(slot):
        h = slot - turn

        @pl.when((h >= 0) & (h < heads))
        def _():
            prefix_chain(h)

    relay_at = {}
    for chunk in range(chunks):
        where = (0, 1, rounds - 1, "mid", "late", rounds, rounds + 2, rounds + heads - 1)[8 * chunk // chunks]
        relay_at.setdefault(where, []).append(chunk)

    def relays(first, last, now):
        for slot, which in relay_at.items():
            if not isinstance(slot, str) and first <= slot < last:
                @pl.when(now == slot - first)
                def _(which=which):
                    for chunk in which:
                        relay(chunk)

    def relay_named(name):
        for chunk in relay_at.get(name, []):
            relay(chunk)

    chain_at(0)

    @pl.when(has_down)
    def _():
        take_counts()

    chain_at(1)
    loads[3].wait()

    def unit(k, carry):
        softmax(2 * k // nb, 2 * k % nb)
        softmax((2 * k + 1) // nb, (2 * k + 1) % nb)
        chain_at(k + 2)
        relays(0, rounds, k)
        return carry

    lax.fori_loop(0, rounds, unit, 0)
    loads[4].wait()

    depth = go_in.shape[1]

    def project(start):
        rows = pl.ds(start, TILE)
        total = nt(gath[0, rows], w_ref[:, 0:depth])
        for k in range(1, n_head):
            total += nt(gath[k, rows], w_ref[:, k * depth:(k + 1) * depth])
        dout[rows] = total.astype(BF16)

    def value_pass(h, b):
        head_lanes = pl.ds(pl.multiple_of(h * width, width), width)
        vpart[h, b] = nn(cache_low[h, b], dout[pl.ds(b * BLOCK, BLOCK), head_lanes])

    def grad_pass(h, b):
        head_lanes = pl.ds(pl.multiple_of(h * width, width), width)
        rows = pl.ds(b * BLOCK, BLOCK)
        query = q_ref[rows, head_lanes]
        grad = dout[rows, head_lanes]
        counts = jnp.concatenate([cnt_full[h, b]] * (BLOCK // width), axis=1)
        local_grad = nt(v_ref[rows, head_lanes], grad)
        cache_grad = nt(cval[h, b], grad)
        local_prob = local_low[h, b].astype(F32)
        cache_prob = cache_low[h, b].astype(F32)
        delta = (jnp.sum(local_prob * local_grad, axis=0, keepdims=True)
                 + jnp.sum(cache_prob * cache_grad, axis=0, keepdims=True))
        local_score_grad = (local_prob * (local_grad - delta) * scale).astype(BF16)
        cache_score_grad = (cache_prob * (cache_grad - delta * counts) * scale).astype(BF16)
        gq_t = nn(keys_t[h, b], local_score_grad) + nn(book_t[h], cache_score_grad)
        gq_ref[rows, head_lanes] = jnp.transpose(gq_t).astype(BF16)
        key_grad = nn(local_score_grad, query).astype(BF16)
        code = nn(hot_t[h, b], key_grad) + nn(cache_score_grad, query)
        local_part[h, b] = nn(local_low[h, b], grad)
        if b == 0:
            code_acc[h] = code
        else:
            code_acc[h] += code

    def later_pair(h):
        return seq_copy(ly_out.at[h], ly_in.at[h], ly_s.at[0], ly_r.at[h], partner)

    def later_hop(h, to):
        return seq_copy(lz_out.at[h], lz_in.at[h], lz_s.at[0], lz_r.at[h], to)

    def later_back(h):
        return seq_copy(la_out.at[h], la_in.at[h], la_s.at[0], la_r.at[h], partner)

    def part_total(h, span):
        total = vpart[h, 0, span]
        for b in range(1, nb):
            total += vpart[h, b, span]
        return total

    def send_later(h):
        ly_out[h] = part_total(h, other_half).astype(BF16)
        later_pair(h).start()

    def later_chain(h):
        later_pair(h).wait_recv()

        @pl.when(jnp.logical_not(has_up))
        def _():
            lz_in[h] = jnp.zeros(lz_in.shape[1:], BF16)

        @pl.when(has_up)
        def _():
            later_hop(h, me + 2).wait_recv()

        above = lz_in[h].astype(F32)
        pair = ly_in[h].astype(F32)
        total = part_total(h, own_half)
        lz_out[h] = (above + total + pair).astype(BF16)

        @pl.when(has_down)
        def _():
            later_hop(h, me - 2).start()

        la_out[h] = (above + total * is_hi).astype(BF16)
        later_ref[h, own_half] = above + pair * is_lo

    def later_gather(h):
        later_back(h).wait_recv()
        later_ref[h, other_half] = la_in[h].astype(F32)
        head_lanes = pl.ds(pl.multiple_of(h * width, width), width)
        later = later_ref[h]
        for b in reversed(range(nb)):
            rows = pl.ds(b * BLOCK, BLOCK)
            lookup = nn(hot[h, b], later.astype(BF16))
            gv_ref[rows, head_lanes] = (local_part[h, b] + lookup).astype(BF16)
            later = later + vpart[h, b]

    def code_pair(h):
        return seq_copy(cy_out.at[h], cy_in.at[h], cy_s.at[0], cy_r.at[h], partner)

    def code_up(h, s):
        return seq_copy(c_out.at[h, s], c_below.at[h, s], c_s.at[0], cb_r.at[h, s], me + 2)

    def code_down(h, s):
        return seq_copy(c_out.at[h, s], c_above.at[h, s], c_s.at[0], cu_r.at[h, s], me - 2)

    def fin_up(h, s):
        return seq_copy(c_fin.at[side, h, s], c_fin.at[side, h, s], fu_s.at[0], cf_r.at[h, s], me + 2)

    def fin_down(h, s):
        return seq_copy(c_fin.at[side, h, s], c_fin.at[side, h, s], fd_s.at[0], cf_r.at[h, s], me - 2)

    def fin_pair(h, which, s):
        return seq_copy(c_fin.at[which, h, s], c_fin.at[which, h, s], cp_s.at[0], cp_r.at[h, s], partner)

    def send_code(h):
        cy_out[h] = code_acc[h, other_half].astype(BF16)
        code_pair(h).start()

    def piece_of(which, s):
        return pl.ds(pl.multiple_of(which * half + s * piece, piece), piece)

    def reduce_code(h):
        code_pair(h).wait_recv()
        code_acc[h, own_half] += cy_in[h].astype(F32)
        for s in range(SUBS):
            span = piece_of(side, s)

            @pl.when((at <= center) & has_down)
            def _(s=s, span=span):
                code_up(h, s).wait_recv()
                code_acc[h, span] += c_below[h, s].astype(F32)

            @pl.when((at >= center) & has_up)
            def _(s=s, span=span):
                code_down(h, s).wait_recv()
                code_acc[h, span] += c_above[h, s].astype(F32)

            c_out[h, s] = code_acc[h, span].astype(BF16)

            @pl.when(at < center)
            def _(s=s):
                code_up(h, s).start()

            @pl.when(at > center)
            def _(s=s):
                code_down(h, s).start()

    def spread_code(h):
        for s in range(SUBS):
            @pl.when(at == center)
            def _(s=s):
                c_fin[side, h, s] = c_out[h, s]

            @pl.when(at != center)
            def _(s=s):
                fin_up(h, s).wait_recv()

            @pl.when((at <= center) & has_down)
            def _(s=s):
                fin_down(h, s).start()

            @pl.when((at >= center) & has_up)
            def _(s=s):
                fin_up(h, s).start()

            fin_pair(h, side, s).start()

        for s in range(SUBS):
            gc_ref[h, piece_of(side, s)] = c_fin[side, h, s].astype(F32)

    def last_code(h):
        for s in range(SUBS):
            fin_pair(h, 1 - side, s).wait_recv()
            gc_ref[h, piece_of(1 - side, s)] = c_fin[1 - side, h, s].astype(F32)

    for b in range(nb):
        final = b == nb - 1
        for part in range(parts):
            start = b * BLOCK + part * TILE
            for slot in by_slot:
                if slot in feeds:
                    for chunk in range(start // CHUNK, (start + TILE) // CHUNK):
                        arrive(slot, chunk)
                else:
                    tile_copy(slot, start).wait_recv()
            project(start)
            if b == 0:
                if part == 0:
                    relay_named("mid")
                chain_at(rounds + 2 + part)
        def values(h, carry, b=b, final=final):
            value_pass(h, b)
            if final:
                @pl.when(has_down)
                def _():
                    send_later(h)

            return carry

        lax.fori_loop(0, heads, values, 0)
        if b == 0:
            relay_named("late")

            def rest(h, carry):
                @pl.when(turn + h >= rounds + 2 + parts)
                def _():
                    prefix_chain(h)

                return carry

            lax.fori_loop(0, heads, rest, 0)

        def grads(h, carry, b=b, final=final):
            if b == 0:
                prefix_gather(h)
            grad_pass(h, b)
            if b == 0:
                relays(rounds, rounds + heads, h)
            if final:
                send_code(h)

                @pl.when(jnp.logical_not(has_up))
                def _():
                    later_chain(h)

            return carry

        lax.fori_loop(0, heads, grads, 0)

    def send_rest(h, carry):
        @pl.when(jnp.logical_not(has_down))
        def _():
            send_later(h)

        return carry

    lax.fori_loop(0, heads, send_rest, 0)

    behind = outer - 1 - at
    soon = behind * 2 < outer

    def chain_step(h, carry):
        @pl.when(soon & (behind > 0))
        def _():
            later_chain(h)

        return carry

    lax.fori_loop(0, heads, chain_step, 0)

    @pl.when(soon & (behind > 0))
    def _():
        for h in range(heads):
            later_back(h).start()

    def reduce_step(h, carry):
        reduce_code(h)

        @pl.when(at == center)
        def _():
            spread_code(h)

        @pl.when(jnp.logical_not(soon) & has_down & (h == 1))
        def _():
            later_chain(h - 1)
            later_back(h - 1).start()

        return carry

    lax.fori_loop(0, heads, reduce_step, 0)

    def back_step(h, carry):
        @pl.when(jnp.logical_not(soon | (has_down & (h == 0))))
        def _():
            later_chain(h)

        @pl.when((behind == 0) | jnp.logical_not(soon | (has_down & (h == 0))))
        def _():
            later_back(h).start()

        return carry

    lax.fori_loop(0, heads, back_step, 0)

    def sent(ref, sem):
        return seq_copy(ref, ref, sem.at[0], sem.at[0], partner)

    sent(py_out, py_s).wait_send()
    sent(pa_out, pa_s).wait_send()

    @pl.when(has_up)
    def _():
        sent(pz_out, pz_s).wait_send()

    count_pair.wait_send()

    @pl.when(has_up)
    def _():
        count_hop(me + 2).wait_send()

    all_sent().wait_send()

    quiet = (at == center) | jnp.logical_not(has_down & has_up)

    def spread_step(h, carry):
        @pl.when(at != center)
        def _():
            spread_code(h)

        @pl.when(quiet)
        def _():
            later_gather(h)

        return carry

    lax.fori_loop(0, heads, spread_step, 0)

    def last_step(h, carry):
        @pl.when(jnp.logical_not(quiet))
        def _():
            later_gather(h)

        last_code(h)
        return carry

    lax.fori_loop(0, heads, last_step, 0)
    sent(ly_out, ly_s).wait_send()
    sent(la_out, la_s).wait_send()
    sent(cy_out, cy_s).wait_send()
    sent(c_fin.at[side], cp_s).wait_send()

    @pl.when(has_down)
    def _():
        sent(lz_out, lz_s).wait_send()

    @pl.when(at != center)
    def _():
        sent(c_out, c_s).wait_send()

    @pl.when((at <= center) & has_down)
    def _():
        sent(c_fin.at[side], fd_s).wait_send()

    @pl.when((at >= center) & has_up)
    def _():
        sent(c_fin.at[side], fu_s).wait_send()


def write_out(*refs):
    sems = refs[-1]
    copies = [pltpu.make_async_copy(refs[k], refs[k + 3], sems.at[k]) for k in range(3)]
    for copy in copies:
        copy.start()
    for copy in copies:
        copy.wait()


def per_device(queries, values, codes, codebook, out_weight, grad_out):
    n_seq, n_head = lax.axis_size("seq"), lax.axis_size("head")
    row_count = queries.shape[0]
    heads, entries, width = codebook.shape
    nb = row_count // BLOCK
    parts = BLOCK // TILE
    chunks = row_count // CHUNK
    half = entries // 2
    hbm = pl.BlockSpec(memory_space=pltpu.HBM)
    vmem = pl.BlockSpec(memory_space=pltpu.VMEM)
    dma = pltpu.SemaphoreType.DMA
    halves = pltpu.VMEM((heads, half, width), BF16)
    pieces = pltpu.VMEM((heads, SUBS, half // SUBS, width), BF16)
    counts = pltpu.VMEM((heads, 1, entries), F32)
    results = pl.pallas_call(
        functools.partial(kernel, n_seq, n_head),
        out_shape=(
            jax.ShapeDtypeStruct(queries.shape, BF16),
            jax.ShapeDtypeStruct(queries.shape, BF16),
            jax.ShapeDtypeStruct(codebook.shape, F32),
        ),
        in_specs=[hbm] * 6,
        out_specs=(vmem,) * 3,
        scratch_shapes=[
            pltpu.VMEM(queries.shape, BF16),
            pltpu.VMEM(queries.shape, BF16),
            pltpu.VMEM((heads, row_count), jnp.int32),
            pltpu.VMEM(codebook.shape, BF16),
            pltpu.VMEM(out_weight.shape, BF16),
            pltpu.VMEM((n_head,) + grad_out.shape, BF16),
            pltpu.VMEM(queries.shape, BF16),
            pltpu.VMEM((heads, nb, entries, BLOCK), BF16),
            pltpu.VMEM((heads, nb, BLOCK, entries), BF16),
            pltpu.VMEM((heads, nb, BLOCK, width), BF16),
            pltpu.VMEM((heads, nb, width, BLOCK), BF16),
            pltpu.VMEM((heads, width, entries), BF16),
            pltpu.VMEM((heads, nb, entries, width), F32),
            pltpu.VMEM((heads, nb, 1, entries), F32),
            pltpu.VMEM((heads, nb, 1, entries), F32),
            pltpu.VMEM((heads, nb, entries, width), F32),
            pltpu.VMEM((heads, nb, entries, width), BF16),
            pltpu.VMEM((heads, nb, BLOCK, BLOCK), BF16),
            pltpu.VMEM((heads, nb, entries, BLOCK), BF16),
            pltpu.VMEM((heads, nb, BLOCK, width), F32),
            pltpu.VMEM((heads, nb, entries, width), F32),
            pltpu.VMEM((heads, entries, width), F32),
            pltpu.VMEM((heads, entries, width), F32),
            counts, counts, counts, counts,
            halves, halves, halves, halves, halves, halves,
            halves, halves, halves, halves, halves, halves,
            halves, halves, pieces, pieces, pieces,
            pltpu.VMEM((2, heads, SUBS, half // SUBS, width), BF16),
            dma((5,)), dma((2,)),
            dma((1,)), dma((n_head // 2, row_count // TILE)), dma((max(n_head // 2 - 1, 1), chunks)),
            dma((1,)), dma((1,)), dma((1,)), dma((1,)),
        ] + [dma((1,)), dma((heads,))] * 7 + [
            dma((1,)), dma((heads, SUBS)), dma((heads, SUBS)), dma((1,)), dma((heads, SUBS)),
            dma((1,)), dma((1,)), dma((heads, SUBS)),
        ],
        compiler_params=pltpu.CompilerParams(
            collective_id=0, has_side_effects=True, vmem_limit_bytes=50 * 1024 * 1024),
    )(*(pltpu.with_memory_space_constraint(x, pltpu.HBM) for x in (queries, values, codes.T, codebook, out_weight, grad_out)))
    return pl.pallas_call(
        write_out,
        out_shape=tuple(jax.ShapeDtypeStruct(r.shape, r.dtype) for r in results),
        in_specs=[vmem] * 3,
        out_specs=(hbm,) * 3,
        scratch_shapes=[dma((3,))],
        compiler_params=pltpu.CompilerParams(vmem_limit_bytes=1024 * 1024),
    )(*results)


def solution(mesh):
    return jax.shard_map(
        per_device,
        mesh=mesh,
        in_specs=(
            P("seq", "head"),
            P("seq", "head"),
            P("seq", "head"),
            P("head", None, None),
            P("head", None),
            P("seq", "head"),
        ),
        out_specs=(P("seq", "head"), P("seq", "head"), P("head", None, None)),
        check_vma=False,
    )
```
